32 devices in a mesh: scene: 2 (over x), space: 8 (over z, y), sub: 2 (over core).
Axes of the slice: x: 2, y: 2, z: 4, core: 2. Of those that a mesh axis runs over, the one named last changes fastest.
Arguments:
- features: bfloat16 [64, 1728, 128], P(('scene', 'space', 'sub')), parts along dimension 0, may hold values from -6 to 6
- out_grad: bfloat16 [64, 1728, 128], P(('scene', 'space', 'sub')), parts along dimension 0, may hold values from -6 to 6
- weight: bfloat16 [27, 128, 128], replicated, may hold values from -0.109375 to 0.109375
- neighbours: int32 [64, 6], P(('scene', 'space', 'sub')), parts along dimension 0, may hold values from -1 to 31, as said below
- active: int32 [64, 1728], P(('scene', 'space', 'sub')), parts along dimension 0, may hold values from 0 to 1
Outputs:
- input_grad: bfloat16 [64, 1728, 128], P(('scene', 'space', 'sub')), parts along dimension 0
- weight_grad: float32 [6912, 128], P(('scene', 'space', 'sub')), parts along dimension 0
The draws below stay inside these ranges and needn't reach their ends.
There are 2 independent parts, one for each index of `scene`. The reference program is written for one: setup_inputs(seed, part) draws one part's arguments, and reference() takes and returns one part's arrays. A program takes and returns all parts, laid end to end along the dimension named above; an argument that names none is the same for every part. Nothing has to cross between parts.
Inputs may be any that keep to these rules, and one draw needn't show every extreme that they name: The bricks form a full grid of 2 x 2 x 8; slots s * 2 * 2 to (s + 1) * 2 * 2 - 1 hold layer s of the third dimension in some order, so neighbours along the first two dimensions lie in the same layer and along the third in the layer below or above.
All inputs are finite; a program needn't handle non-finite values.
Results may differ from the reference program's by a relative error of at most 0.001.
Values may be sent and summed in bfloat16 or wider, within the bound.
No kernel may reach another device: no remote copies, remote signals or barrier semaphores. Data moves between devices by JAX's collectives and lax.ppermute only.
A program may use at most 192 MiB of HBM per device.

```python
import jax
import jax.numpy as jnp
from jax import lax

C = 128
BSIDE = 12
VOX = 1728
GX = 2
GY = 2
GZ = 8
BRICKS = 32


def draw_neighbours(key, part):
    cells = GX * GY
    layer_keys = jax.random.split(jax.random.fold_in(key, 11), GZ)
    placed = jax.vmap(lambda one_key: jax.random.permutation(one_key, cells))(layer_keys)
    layers = jnp.arange(GZ, dtype=jnp.int32)[:, None]
    grid = (layers * cells + placed.astype(jnp.int32)).reshape(GZ, GX, GY)
    padded = jnp.pad(grid, 1, constant_values=-1)
    table = jnp.stack([padded[1:-1, :-2, 1:-1], padded[1:-1, 2:, 1:-1], padded[1:-1, 1:-1, :-2], padded[1:-1, 1:-1, 2:], padded[:-2, 1:-1, 1:-1], padded[2:, 1:-1, 1:-1]], axis=-1).reshape(GZ * cells, 6)
    result = jnp.zeros((BRICKS, 6), jnp.int32)
    return result.at[grid.reshape(-1)].set(table.astype(jnp.int32))


def draw_active(key, part):
    level = jax.random.randint(jax.random.fold_in(key, 3), (BRICKS, 1), 0, 4)
    rolls = jax.random.randint(jax.random.fold_in(key, 5), (BRICKS, VOX), 0, 8)
    limit = jnp.minimum(level * level, 8)
    return (rolls < limit).astype(jnp.int32)


def raised(entries, stream_key, source, target, blocks, factor):
    def block_of(axis_at):
        return (jnp.arange(entries.shape[axis_at]) // (entries.shape[axis_at] // blocks)).reshape((-1,) + (1,) * (entries.ndim - 1 - axis_at))

    first = jax.random.permutation(stream_key, blocks)[block_of(target)]
    far = (block_of(target) + blocks // 2) % blocks
    return jnp.where((block_of(source) == first) | (block_of(source) == far), factor * entries, entries)


def block_levels(key, dims, cuts, low, largest):
    gain = 1.0
    for position, blocks in cuts:
        steps = jax.random.uniform(jax.random.fold_in(jax.random.fold_in(key, 6), position), (blocks,), jnp.float32, low / len(cuts), largest / len(cuts))
        gain = gain * jnp.repeat(jnp.exp(steps), dims[position] // blocks).reshape((-1,) + (1,) * (len(dims) - 1 - position))
    return gain


def normal_values(stream_key, shape, scale, bound, shards=(), held_as=jnp.bfloat16):
    values = jax.random.normal(stream_key, shape, jnp.float32) * scale
    if len(shards) > 0:
        values = block_levels(stream_key, shape, shards, -0.22, 0.18) * values
    return jnp.clip(values, min=-bound, max=bound).astype(held_as)


def gaussian_with(rng, shape, spread, bound, cuts, heavy, kind=jnp.bfloat16):
    array = spread * jax.random.normal(rng, shape, jnp.float32)
    if cuts:
        array = array * block_levels(rng, shape, cuts, -0.22, 0.18)
    return jnp.clip(raised(array, jax.random.fold_in(rng, 3), *heavy), -bound, bound).astype(kind)


def setup_inputs(seed: int = 0, part: int = 0) -> dict:
    seeds = jax.random.split(jax.random.key(seed), 6)
    own_keys = jax.random.split(jax.random.fold_in(seeds[5], part), 6)
    return {
        "features": gaussian_with(own_keys[0], (BRICKS, VOX, C), 1.0, 6.0, ((0, 16),), (0, 2, 16, 2.0)),
        "out_grad": normal_values(own_keys[1], (BRICKS, VOX, C), 1.0, 6.0, ((0, 16),)),
        "weight": normal_values(seeds[2], (27, C, C), (27 * C) ** -0.5, 0.109375),
        "neighbours": draw_neighbours(jax.random.fold_in(jax.random.fold_in(seeds[5], part), 71), part),
        "active": draw_active(jax.random.fold_in(jax.random.fold_in(seeds[5], part), 71), part),
    }


def fetch(table, slot_ids):
    present = slot_ids >= 0
    picked = jnp.take(table, jnp.maximum(slot_ids, 0).astype(jnp.int32), axis=1)
    shape = (1, slot_ids.shape[0]) + (1,) * (picked.ndim - 2)
    return jnp.where(present.reshape(shape), picked, jnp.zeros((), picked.dtype))


def extend(fields, near, along, first):
    extent = fields.shape[along]
    low_plane = lax.slice_in_dim(fields, 0, 1, axis=along)
    high_plane = lax.slice_in_dim(fields, extent - 1, extent, axis=along)
    below = fetch(high_plane, near[:, first])
    above = fetch(low_plane, near[:, first + 1])
    return jnp.concatenate([below, fields, above], axis=along)


def reference(features, out_grad, weight, neighbours, active):
    count = features.shape[0]
    width = features.shape[2]
    mask_cast = active.astype(features.dtype)[:, :, None]
    fields = jnp.stack([features * mask_cast, out_grad * mask_cast])
    fields = fields.reshape(2, count, BSIDE, BSIDE, BSIDE, width)
    for along, first in ((2, 0), (3, 2), (4, 4)):
        fields = extend(fields, neighbours, along, first)
    feat_ext = fields[0].astype(jnp.float32)
    grad_ext = fields[1].astype(jnp.float32)
    inner = grad_ext[:, 1:-1, 1:-1, 1:-1]
    extent = BSIDE
    input_grad = jnp.zeros(inner.shape, jnp.float32)
    pieces = []
    for offset in range(27):
        shift_a = offset // 9 - 1
        shift_b = (offset // 3) % 3 - 1
        shift_c = offset % 3 - 1
        grad_slice = grad_ext[:, 1 - shift_a:1 - shift_a + extent, 1 - shift_b:1 - shift_b + extent, 1 - shift_c:1 - shift_c + extent]
        input_grad = input_grad + jnp.einsum("bxyzo,io->bxyzi", grad_slice, weight[offset].astype(jnp.float32))
        feat_slice = feat_ext[:, 1 + shift_a:1 + shift_a + extent, 1 + shift_b:1 + shift_b + extent, 1 + shift_c:1 + shift_c + extent]
        pieces.append(jnp.einsum("bxyzi,bxyzo->io", feat_slice, inner))
    input_grad = input_grad.reshape(count, VOX, width) * active.astype(jnp.float32)[:, :, None]
    weight_grad = (jnp.stack(pieces) / VOX).reshape(27 * width, width)
    return input_grad.astype(jnp.bfloat16), weight_grad
```

```python
import jax
import jax.numpy as jnp
import numpy as np
from jax import lax
from jax.experimental import pallas as pl
from jax.experimental.pallas import tpu as pltpu
from jax.sharding import PartitionSpec as P

BSIDE = 12
PLANE = BSIDE * BSIDE
VOX = BSIDE * PLANE
EXT = BSIDE + 2
C = 128
KROWS = 256
LIMIT = 56 * 2**20
BF = jnp.bfloat16
F32 = jnp.float32


def strip_matrix():
    m = np.zeros((64, PLANE), np.float32)
    for i in range(BSIDE):
        m[i, i * BSIDE] = 1
        m[16 + i, i * BSIDE + 11] = 1
        m[32 + i, i] = 1
        m[48 + i, 11 * BSIDE + i] = 1
    m[12, 0] = m[28, 11] = 1
    m[13, 11 * BSIDE] = m[29, 11 * BSIDE + 11] = 1
    return m.astype(jnp.bfloat16)


def shift_matrix():
    m = np.zeros((9, BSIDE, BSIDE, KROWS), np.float32)
    for k in range(9):
        for b in range(BSIDE):
            for c in range(BSIDE):
                sb, sc = b - (k // 3 - 1), c - (k % 3 - 1)
                if sc in (-1, 12):
                    row = {-1: 13, 12: 12}.get(sb, sb) + (176 if sc < 0 else 192)
                elif sb in (-1, 12):
                    row = sc + (144 if sb < 0 else 160)
                else:
                    row = sb * BSIDE + sc
                m[k, b, c, row] = 1
    return m.reshape(9 * PLANE, KROWS).astype(jnp.bfloat16)


def mask_spread():
    m = np.zeros((2, BSIDE, BSIDE, 2, C), np.float32)
    for j in range(2):
        for p in range(BSIDE):
            m[j, p, p, j] = 1
    return m.reshape(2 * BSIDE, BSIDE * 2 * C).astype(jnp.bfloat16)


def dot(a, b):
    return lax.dot_general(a, b, (((1,), (0,)), ((), ())), preferred_element_type=F32)


def dot_t(a, b):
    return lax.dot_general(a, b, (((1,), (1,)), ((), ())), preferred_element_type=F32)


def halves(x):
    return jnp.concatenate([x[:, C:], x[:, :C]], axis=1)


def per_half(first, second, rows=16):
    lane = lax.broadcasted_iota(jnp.int32, (rows, 2 * C), 1)
    return jnp.where(lane < C, first, second)


def prep_kernel(nb, act, spread, strips, g, gm, subm, up, dn):
    mask = dot(act[...], spread[...]).astype(BF)
    a0 = per_half((nb[0, 0] >= 0).astype(F32), (nb[1, 0] >= 0).astype(F32))
    b0 = per_half((nb[0, 2] >= 0).astype(F32), (nb[1, 2] >= 0).astype(F32))
    code = (2 * a0 + b0).astype(BF)
    a0, b0 = a0.astype(BF), b0.astype(BF)
    for p in range(BSIDE):
        rows = pl.ds(p * PLANE, PLANE)
        plane = jnp.concatenate([g[0, rows, :], g[1, rows, :]], axis=1) * mask[:, p * 256 : p * 256 + 256]
        gm[p] = plane
        s = dot(strips[...], plane).astype(BF)
        dn[pl.ds(p * 16, 16), :] = s[0:16]
        up[pl.ds(p * 16, 16), :] = s[16:32]
        subm[pl.ds(PLANE + p * 16, 16), :] = s[32:48] * b0 + s[48:64] * (1 - b0)
    for r in range(0, PLANE, 16):
        subm[pl.ds(r, 16), :] = gm[0, pl.ds(r, 16), :] * a0 + gm[11, pl.ds(r, 16), :] * (1 - a0)
    subm[pl.ds(PLANE + 192, 16), :] = code
    up[pl.ds(192, 16), :] = code
    dn[pl.ds(192, 16), :] = code


def features_kernel(act, spread, eye, f, ft, pad):
    mask = dot(act[...], spread[...]).astype(BF)
    zero = jnp.zeros((2 * PLANE, C), BF)
    for j in range(2):
        pad[pl.ds(0, 2 * PLANE), :] = zero
        pad[pl.ds(EXT * PLANE, 2 * PLANE), :] = zero
        for p in range(BSIDE):
            pad[pl.ds((p + 2) * PLANE, PLANE), :] = (
                f[j, pl.ds(p * PLANE, PLANE), :] * mask[:, p * 256 + j * C : p * 256 + j * C + C]
            )
        for d in range(3):
            ft[j, pl.ds(d * C, C), :] = dot_t(eye[...], pad[pl.ds(d * PLANE, EXT * PLANE), :]).astype(BF)


def operands(gm, own, other, zs, kop):
    code = own[pl.ds(336, 16), :].astype(F32)
    a0 = jnp.where(code >= 2, 1.0, 0.0)
    b0 = code - 2 * a0
    to_a, to_b, to_d = code + 2 - 4 * a0, code + 1 - 2 * b0, 3 - code

    def weights(refs, at):
        tiles = []
        for ref, swaps in refs:
            t = ref[pl.ds(at, 16), :].astype(F32)
            tiles += [(ref, False, t)] if not swaps else [(ref, True, halves(t))]
        return tiles

    layer = weights([(own, True), (other, False), (other, True)], 336)

    def hits(cands, q):
        return [(ref, sw, jnp.where(t == q, 1.0, 0.0).astype(BF)) for ref, sw, t in cands]

    def gather(picks, row):
        total = None
        for ref, sw, w in picks:
            x = ref[pl.ds(row, 16), :]
            x = (halves(x) if sw else x) * w
            total = x if total is None else total + x
        return total

    row16 = lax.broadcasted_iota(jnp.int32, (16, 2 * C), 0)
    inner = jnp.where(row16 < 12, 1.0, 0.0).astype(BF)
    edge = jnp.where(row16 == 12, 1 - b0, jnp.where(row16 == 13, b0, 0.0)).astype(BF)
    a0h, b0h = a0.astype(BF), b0.astype(BF)
    a1h, b1h = 1 - a0h, 1 - b0h

    pick_a, pick_b, pick_d = hits(layer, to_a), hits(layer, to_b), hits(layer, to_d)
    vert = []
    for first, second in zs:
        cands = weights([(first, False), (first, True), (second, False), (second, True)], 192)
        vert.append(
            (
                [(r, s, w * inner) for r, s, w in hits(cands, code)],
                [(r, s, w * edge) for r, s, w in hits(cands, to_b)],
                [(r, s, w * inner) for r, s, w in hits(cands, to_a)],
                [(r, s, w * edge) for r, s, w in hits(cands, to_d)],
            )
        )
    pad = jnp.zeros((KROWS - 208, 2 * C), BF)
    for p in range(BSIDE):
        kop[p + 1, pl.ds(0, PLANE), :] = gm[p]
        side = gather(pick_b, PLANE + p * 16)
        kop[p + 1, pl.ds(144, 16), :] = side * b0h
        kop[p + 1, pl.ds(160, 16), :] = side * b1h
        for n, (self_, nb_, _, _) in enumerate(vert):
            kop[p + 1, pl.ds(176 + 16 * n, 16), :] = gather(self_, p * 16) + gather(nb_, p * 16)
        kop[p + 1, pl.ds(208, KROWS - 208), :] = pad

    def outer(at, plane, w):
        for r in range(0, PLANE, 16):
            kop[at, pl.ds(r, 16), :] = gather(pick_a, r) * w
        side = gather(pick_d, PLANE + plane * 16) * w
        kop[at, pl.ds(144, 16), :] = side * b0h
        kop[at, pl.ds(160, 16), :] = side * b1h
        for n, (_, _, self_, nb_) in enumerate(vert):
            kop[at, pl.ds(176 + 16 * n, 16), :] = (gather(self_, plane * 16) + gather(nb_, plane * 16)) * w
        kop[at, pl.ds(208, KROWS - 208), :] = pad

    outer(0, 11, a0h)
    outer(EXT - 1, 0, a1h)


def shifted(shift, kop, x):
    for p in range(EXT):
        for k in range(9):
            y = dot(shift[pl.ds(k * PLANE, PLANE), :], kop[p]).astype(BF)
            for j in range(2):
                x[j, pl.ds(p * PLANE, PLANE), pl.ds(k * C, C)] = y[:, j * C : j * C + C]


def wgrad_kernel(sub, shift, ft, gm, own, other, d0, d1, u0, u1, keep, send, kop, x, acc):
    operands(gm, own, other, ((d0, d1), (u0, u1)), kop)
    shifted(shift, kop, x)
    acc[...] = dot(ft[0], x[0])
    acc[...] += dot(ft[1], x[1])
    blocks = keep.shape[0]
    size = keep.shape[1]
    for parity in range(2):

        @pl.when(sub[0] == parity)
        def _(parity=parity):
            for t in range(27):
                da, k = divmod(t, 9)
                row = t * C
                while row < (t + 1) * C:
                    n = row // size
                    end = min((n + 1) * size, (t + 1) * C)
                    v = acc[pl.ds(da * C + row - t * C, end - row), pl.ds(k * C, C)] * (1.0 / VOX)
                    ref = keep if n % 2 == parity else send
                    ref[n // 2, pl.ds(row - n * size, end - row), :] = v
                    row = end


def dgrad_kernel(act, spread, shift, w, kop, out, x, y):
    shifted(shift, kop, x)
    mask = dot(act[...], spread[...])
    for j in range(2):
        for d in range(3):
            wd = jnp.concatenate([w[d * 9 + k] for k in range(9)], axis=1)
            y[:, pl.ds(d * C, C)] = dot_t(x[j], wd)
        for p in range(BSIDE):
            total = y[pl.ds((p + 2) * PLANE, PLANE), pl.ds(0, C)]
            total = total + y[pl.ds((p + 1) * PLANE, PLANE), pl.ds(C, C)]
            total = total + y[pl.ds(p * PLANE, PLANE), pl.ds(2 * C, C)]
            out[j, pl.ds(p * PLANE, PLANE), :] = (total * mask[:, p * 256 + j * C : p * 256 + j * C + C]).astype(BF)


VMEM = pl.BlockSpec(memory_space=pltpu.MemorySpace.VMEM)
SMEM = pl.BlockSpec(memory_space=pltpu.MemorySpace.SMEM)


def call(kernel, name, ins, outs, scratch=(), flops=0, size=0):
    return pl.pallas_call(
        kernel,
        name=name,
        out_shape=[jax.ShapeDtypeStruct(s, d) for s, d in outs],
        in_specs=ins,
        out_specs=[VMEM] * len(outs),
        scratch_shapes=list(scratch),
        compiler_params=pltpu.CompilerParams(vmem_limit_bytes=LIMIT),
        cost_estimate=pl.CostEstimate(flops=flops, transcendentals=0, bytes_accessed=size),
    )


def exchange(value, axis, bit):
    pairs = [(i, i ^ bit) for i in range(lax.axis_size(axis))]
    return lax.ppermute(value, axis, pairs)


def part(value, index, dim):
    return lax.dynamic_index_in_dim(value, index, dim, keepdims=False)


def halve(value, axis_bit, mine, dim):
    return part(value, mine, dim) + exchange(part(value, 1 - mine, dim), "space", axis_bit)


def reduce_blocks(blocks):
    s = lax.axis_index("space")
    rows = blocks.shape[1]
    cut = rows // 16 * 8
    b2, b1, b0 = (s >> 2) & 1, (s >> 1) & 1, s & 1
    v = blocks.reshape(2, 2, 2, rows, C)
    one = halve(v[:, :, :, :cut], 1, b0, 2)
    two = halve(v[:, :, :, cut:], 2, b1, 1)
    one = halve(one, 2, b1, 1)
    two = halve(two, 1, b0, 1)
    both = jnp.concatenate([one, two], axis=1)
    return halve(both, 4, b2, 0)


def on_device(features, out_grad, weight, neighbours, active):
    layers = lax.axis_size("space")
    sub = lax.axis_index("sub").astype(jnp.int32).reshape(1)
    act = active.reshape(2 * BSIDE, PLANE).T.astype(BF)
    spread, strips, shift = jnp.asarray(mask_spread()), jnp.asarray(strip_matrix()), jnp.asarray(shift_matrix())
    eye = jnp.asarray(np.eye(C, dtype=np.float32).astype(jnp.bfloat16))

    gm, own, up, dn = call(
        prep_kernel,
        "prep",
        [SMEM] + [VMEM] * 4,
        [((BSIDE, PLANE, 2 * C), BF), ((352, 2 * C), BF), ((208, 2 * C), BF), ((208, 2 * C), BF)],
    )(neighbours, act, spread, strips, out_grad)

    other = exchange(own, "sub", 1)
    both = ("space", "sub")
    vertical = []
    for step, message in ((1, up), (-1, dn)):
        for target in range(2):
            pairs = [
                (2 * i + j, 2 * (i + step) + (j ^ target))
                for i in range(layers)
                for j in range(2)
                if 0 <= i + step < layers
            ]
            vertical.append(lax.ppermute(message, both, pairs))

    (ft,) = call(
        features_kernel,
        "features",
        [VMEM] * 4,
        [((2, 3 * C, EXT * PLANE), BF)],
        [pltpu.VMEM(((EXT + 2) * PLANE, C), BF)],
        flops=2 * 2 * 3 * C * C * EXT * PLANE,
        size=4 * 2**20,
    )(act, spread, eye, features)

    size = 27 * C // (2 * layers)
    custom = layers == 8
    rows = (layers, size, C) if custom else (8, 216, C)
    keep, send, kop = call(
        wgrad_kernel,
        "wgrad",
        [SMEM] + [VMEM] * 9,
        [(rows, F32), (rows, F32), ((EXT, KROWS, 2 * C), BF)],
        [pltpu.VMEM((2, EXT * PLANE, 9 * C), BF), pltpu.VMEM((3 * C, 9 * C), F32)],
        flops=2 * 3 * C * 9 * C * 2 * EXT * PLANE,
        size=8 * 2**20,
    )(sub, shift, ft, gm, own, other, *vertical)

    if custom:
        weight_grad = reduce_blocks(keep + exchange(send, "sub", 1))
    else:
        even = jnp.where(sub[0] == 0, keep, send)
        odd = jnp.where(sub[0] == 0, send, keep)
        kernel_term = jnp.stack([even, odd], axis=1).reshape(27 * C, C)
        weight_grad = lax.psum_scatter(kernel_term, both, scatter_dimension=0, tiled=True)

    (input_grad,) = call(
        dgrad_kernel,
        "dgrad",
        [VMEM] * 5,
        [((2, VOX, C), BF)],
        [pltpu.VMEM((2, EXT * PLANE, 9 * C), BF), pltpu.VMEM((EXT * PLANE, 3 * C), F32)],
        flops=2 * 3 * C * 9 * C * 2 * EXT * PLANE,
        size=4 * 2**20,
    )(act, spread, shift, weight, kop)
    return input_grad, weight_grad


def solution(mesh):
    in_specs = (
        P(("scene", "space", "sub"), None, None),
        P(("scene", "space", "sub"), None, None),
        P(),
        P(("scene", "space", "sub"), None),
        P(("scene", "space", "sub"), None),
    )
    out_specs = (P(("scene", "space", "sub"), None, None), P(("scene", "space", "sub"), None))
    return jax.shard_map(
        on_device, mesh=mesh, in_specs=in_specs, out_specs=out_specs, check_vma=False
    )
```

```python
import jax
import jax.numpy as jnp
import numpy as np
from jax import lax
from jax.experimental import pallas as pl
from jax.experimental.pallas import tpu as pltpu
from jax.sharding import PartitionSpec as P

BSIDE = 12
PLANE = BSIDE * BSIDE
VOX = BSIDE * PLANE
EXT = BSIDE + 2
C = 128
KROWS = 256
MINE = PLANE + 208
LIMIT = 16 * 2**20
BF = jnp.bfloat16
F32 = jnp.float32


def strip_matrix():
    m = np.zeros((64, PLANE), np.float32)
    for i in range(BSIDE):
        m[i, i * BSIDE] = 1
        m[16 + i, i * BSIDE + 11] = 1
        m[32 + i, i] = 1
        m[48 + i, 11 * BSIDE + i] = 1
    m[12, 0] = m[28, 11] = 1
    m[13, 11 * BSIDE] = m[29, 11 * BSIDE + 11] = 1
    return m.astype(jnp.bfloat16)


def shift_matrix():
    m = np.zeros((9, BSIDE, BSIDE, KROWS), np.float32)
    for k in range(9):
        for b in range(BSIDE):
            for c in range(BSIDE):
                sb, sc = b - (k // 3 - 1), c - (k % 3 - 1)
                if sc in (-1, 12):
                    row = {-1: 13, 12: 12}.get(sb, sb) + (176 if sc < 0 else 192)
                elif sb in (-1, 12):
                    row = sc + (144 if sb < 0 else 160)
                else:
                    row = sb * BSIDE + sc
                m[k, b, c, row] = 1
    return m.reshape(9 * PLANE, KROWS).astype(jnp.bfloat16)


def band_matrix():
    m = np.zeros((3, EXT, 16, EXT, 16), np.float32)
    for q in range(3):
        for b in range(BSIDE):
            source = b - (q - 1)
            for p in range(EXT):
                m[q, p, b, p, 13 if source < 0 else source] = 1
    return m.reshape(3 * EXT * 16, EXT * 16).astype(jnp.bfloat16)


def dot(a, b):
    return lax.dot_general(a, b, (((1,), (0,)), ((), ())), preferred_element_type=F32)


def dot_t(a, b):
    return lax.dot_general(a, b, (((1,), (1,)), ((), ())), preferred_element_type=F32)


def halves(x):
    return jnp.concatenate([x[:, C:], x[:, :C]], axis=1)


def per_half(first, second, rows=16):
    lane = lax.broadcasted_iota(jnp.int32, (rows, 2 * C), 1)
    return jnp.where(lane < C, first, second)


def masks(act, out):
    r = lax.broadcasted_iota(jnp.int32, (C, C), 0)
    eye = jnp.where(r == lax.broadcasted_iota(jnp.int32, (C, C), 1), 1.0, 0.0)
    wide = lax.broadcasted_iota(jnp.int32, (2 * C, 2 * C), 0) < C
    ones = jnp.where(wide == (lax.broadcasted_iota(jnp.int32, (2 * C, 2 * C), 1) < C), 1.0, 0.0).astype(BF)
    for n in range(0, VOX, C):
        cols = []
        for j in range(2):
            a = act[pl.ds(j, 1), pl.ds(n, min(C, VOX - n))].astype(F32)
            if n + C > VOX:
                a = jnp.concatenate([a, jnp.zeros((1, n + C - VOX), F32)], axis=1)
            cols.append((eye * a).astype(BF))
        out[pl.ds(n, C), :] = dot(jnp.concatenate(cols, axis=1), ones).astype(BF)


def prep_kernel(sub, nb, act_hbm, strips_hbm, g_hbm, gm, message, mine, mask, act, strips, g, sem):
    loads = [
        pltpu.make_async_copy(act_hbm, act, sem.at[0]),
        pltpu.make_async_copy(strips_hbm, strips, sem.at[1]),
        pltpu.make_async_copy(g_hbm, g, sem.at[2]),
    ]
    for load in loads:
        load.start()
    loads[0].wait()
    masks(act, mask)
    a0 = per_half((nb[0, 0] >= 0).astype(F32), (nb[1, 0] >= 0).astype(F32))
    b0 = per_half((nb[0, 2] >= 0).astype(F32), (nb[1, 2] >= 0).astype(F32))
    code = (2 * a0 + b0).astype(BF)
    a0, b0 = a0.astype(BF), b0.astype(BF)
    second = jnp.full((16, 2 * C), sub[0].astype(F32), F32).astype(BF)
    loads[1].wait()
    loads[2].wait()
    for p in range(BSIDE):
        rows = pl.ds(p * PLANE, PLANE)
        plane = jnp.concatenate([g[0, rows, :], g[1, rows, :]], axis=1) * mask[rows, :]
        gm[p] = plane
        s = dot(strips[...], plane).astype(BF)
        mine[pl.ds(p * 16, 16), :] = s[0:16] * second + s[16:32] * (1 - second)
        message[pl.ds(MINE + p * 16, 16), :] = s[16:32] * second + s[0:16] * (1 - second)
        message[pl.ds(PLANE + p * 16, 16), :] = s[32:48] * b0 + s[48:64] * (1 - b0)
    for r in range(0, PLANE, 16):
        message[pl.ds(r, 16), :] = gm[0, pl.ds(r, 16), :] * a0 + gm[11, pl.ds(r, 16), :] * (1 - a0)
    message[pl.ds(PLANE + 192, 16), :] = code
    message[pl.ds(MINE + 192, 16), :] = code
    mine[pl.ds(192, 16), :] = code


def features_kernel(mask, strips, f, pad, fs):
    zero = jnp.zeros((2 * PLANE, C), BF)
    edge = jnp.zeros((32, 2 * C), BF)
    for j in range(2):
        pad[j, pl.ds(0, 2 * PLANE), :] = zero
        pad[j, pl.ds(EXT * PLANE, 2 * PLANE), :] = zero
        pad[j, pl.ds(2 * PLANE, VOX), :] = f[j] * mask[pl.ds(0, VOX), pl.ds(j * C, C)]
    for n in range(2):
        fs[n, pl.ds(0, 32), :] = edge
        fs[n, pl.ds(EXT * 16, 32), :] = edge
    for p in range(BSIDE):
        rows = pl.ds((p + 2) * PLANE, PLANE)
        s = dot(strips[pl.ds(0, 32), :], jnp.concatenate([pad[0, rows, :], pad[1, rows, :]], axis=1)).astype(BF)
        for n in range(2):
            fs[n, pl.ds((p + 2) * 16, 16), :] = s[16 * n : 16 * n + 16]


def position(own):
    code = own[pl.ds(336, 16), :].astype(F32)
    a0 = jnp.where(code >= 2, 1.0, 0.0)
    b0 = code - 2 * a0
    return code, a0, b0


def candidates(refs, at):
    tiles = []
    for ref, base, swapped in refs:
        t = ref[pl.ds(base + at, 16), :].astype(F32)
        tiles.append(((ref, base, swapped), halves(t) if swapped else t))
    return tiles


def hits(cands, q):
    return [(*source, jnp.where(t == q, 1.0, 0.0).astype(BF)) for source, t in cands]


def gather(picks, row):
    total = None
    for ref, base, swapped, w in picks:
        x = ref[pl.ds(base + row, 16), :]
        x = (halves(x) if swapped else x) * w
        total = x if total is None else total + x
    return total


def layer_operands(gm, own, other, kop):
    code, a0, b0 = position(own)
    layer = candidates([(own, 0, True), (other, 0, False), (other, 0, True)], 336)
    pick_a = hits(layer, code + 2 - 4 * a0)
    pick_b = hits(layer, code + 1 - 2 * b0)
    pick_d = hits(layer, 3 - code)
    a0h, b0h = a0.astype(BF), b0.astype(BF)
    a1h, b1h = 1 - a0h, 1 - b0h
    rest = jnp.zeros((KROWS - 176, 2 * C), BF)
    for p in range(BSIDE):
        kop[p + 1, pl.ds(0, PLANE), :] = gm[p]
        side = gather(pick_b, PLANE + p * 16)
        kop[p + 1, pl.ds(144, 16), :] = side * b0h
        kop[p + 1, pl.ds(160, 16), :] = side * b1h
        kop[p + 1, pl.ds(176, KROWS - 176), :] = rest
    for at, plane, w in ((0, 11, a0h), (EXT - 1, 0, a1h)):
        for r in range(0, PLANE, 16):
            kop[at, pl.ds(r, 16), :] = gather(pick_a, r) * w
        side = gather(pick_d, PLANE + plane * 16) * w
        kop[at, pl.ds(144, 16), :] = side * b0h
        kop[at, pl.ds(160, 16), :] = side * b1h
        kop[at, pl.ds(176, KROWS - 176), :] = rest


def vertical_operands(own, zs, z):
    code, a0, b0 = position(own)
    row16 = lax.broadcasted_iota(jnp.int32, (16, 2 * C), 0)
    inner = jnp.where(row16 < 12, 1.0, 0.0).astype(BF)
    edge = jnp.where(row16 == 12, 1 - b0, jnp.where(row16 == 13, b0, 0.0)).astype(BF)
    a0h = a0.astype(BF)
    for n, ref in enumerate(zs):
        cands = candidates([(ref, base, swapped) for base in (0, 208) for swapped in (False, True)], 192)
        near = [(*q, w * inner) for *q, w in hits(cands, code)]
        near += [(*q, w * edge) for *q, w in hits(cands, code + 1 - 2 * b0)]
        far = [(*q, w * inner) for *q, w in hits(cands, code + 2 - 4 * a0)]
        far += [(*q, w * edge) for *q, w in hits(cands, 3 - code)]
        for p in range(BSIDE):
            z[n, pl.ds((p + 1) * 16, 16), :] = gather(near, p * 16)
        z[n, pl.ds(0, 16), :] = gather(far, 11 * 16) * a0h
        z[n, pl.ds((EXT - 1) * 16, 16), :] = gather(far, 0) * (1 - a0h)


def shifted(shift, kop, x, ks, first, count):
    for p in range(count):
        for n, k in enumerate(ks):
            y = dot(shift[pl.ds(k * PLANE, PLANE), :], kop[first + p]).astype(BF)
            for j in range(2):
                x[j, pl.ds(p * PLANE, PLANE), pl.ds(n * C, C)] = y[:, j * C : j * C + C]


def stacked(ref, j, width, lanes):
    return jnp.concatenate([ref[j, pl.ds(d * width, EXT * width), lanes] for d in range(3)], axis=1)


def dot_rows(a, b):
    return lax.dot_general(a, b, (((0,), (0,)), ((), ())), preferred_element_type=F32)


def first_kernel(shift, gm, own, other, pad, x, acc, kop):
    layer_operands(gm, own, other, kop)
    shifted(shift, kop, x, range(9), 0, EXT)
    acc[...] = dot_rows(stacked(pad, 0, PLANE, slice(None)), x[0])


def second_kernel(pad, x, before, acc):
    acc[...] = before[...] + dot_rows(stacked(pad, 1, PLANE, slice(None)), x[1])


def tilt_kernel(sub, own, got, got2, fs, bands, acc, keep, send, zs, z, more):
    for parity in range(2):

        @pl.when(sub[0] == parity)
        def _(parity=parity):
            vertical_operands(own, (got2, got) if parity else (got, got2), z)

    for n in range(2):
        v = dot(bands[...], z[n]).astype(BF)
        rows = EXT * 16
        total = None
        for j in range(2):
            lanes = slice(j * C, j * C + C)
            zs[n, j] = jnp.concatenate([v[q * rows : q * rows + rows, lanes] for q in range(3)], axis=1)
            f3 = jnp.concatenate([fs[n, pl.ds(d * 16, rows), lanes] for d in range(3)], axis=1)
            part_ = dot_rows(f3, zs[n, j])
            total = part_ if total is None else total + part_
        more[n] = total
    size = keep.shape[1]
    for parity in range(2):

        @pl.when(sub[0] == parity)
        def _(parity=parity):
            for t in range(27):
                da, k = divmod(t, 9)
                row = t * C
                while row < (t + 1) * C:
                    block = row // size
                    end = min((block + 1) * size, (t + 1) * C)
                    at = pl.ds(da * C + row - t * C, end - row)
                    v = acc[at, pl.ds(k * C, C)]
                    if k % 3 != 1:
                        v = v + more[0 if k % 3 == 2 else 1, at, pl.ds(k // 3 * C, C)]
                    ref = keep if block % 2 == parity else send
                    ref[block // 2, pl.ds(row - block * size, end - row), :] = v * (1.0 / VOX)
                    row = end


def columns(w, ks):
    return jnp.concatenate([jnp.concatenate([w[d * 9 + k] for k in ks], axis=1) for d in range(3)], axis=0)


def joined(y, p, rows):
    total = y[pl.ds((p + 2) * rows, rows), pl.ds(0, C)]
    total = total + y[pl.ds((p + 1) * rows, rows), pl.ds(C, C)]
    return total + y[pl.ds(p * rows, rows), pl.ds(2 * C, C)]


def dgrad_kernel(j, mask, w, x, zs, before, out, y, yz, plane, res, sem):
    del before
    y[...] = dot_t(x[j], columns(w, range(9)))
    for n in range(2):
        yz[n] = dot_t(zs[n, j], columns(w, (2, 5, 8) if n == 0 else (0, 3, 6)))
    for p in range(BSIDE):
        plane[pl.ds(0, PLANE), :] = joined(y, p, PLANE)
        for n in range(2):
            at = pl.ds(11 * n, BSIDE, stride=BSIDE)
            plane[at, :] = plane[at, :] + joined(yz.at[n], p, 16)[:BSIDE]
        m = mask[pl.ds(p * PLANE, PLANE), pl.ds(j * C, C)].astype(F32)
        res[pl.ds(p * PLANE, PLANE), :] = (plane[pl.ds(0, PLANE), :] * m).astype(BF)
    store = pltpu.make_async_copy(res, out.at[j], sem)
    store.start()
    store.wait()


def blocks_kernel(bits, keep, got, send1, keep1, send2, keep2):
    b0, b1 = bits[0], bits[1]
    cut = send1.shape[2]
    for z1 in range(2):
        for n in range(2):
            for flip, ref1, ref2 in ((0, keep1, keep2), (1, send1, send2)):
                i = z1 * 4 + n * 2 + jnp.bitwise_xor(b0, flip)
                ref1[z1, n] = keep[i, pl.ds(0, cut), :] + got[i, pl.ds(0, cut), :]
                i = z1 * 4 + jnp.bitwise_xor(b1, flip) * 2 + n
                rest = pl.ds(cut, keep.shape[1] - cut)
                ref2[z1, n] = keep[i, rest, :] + got[i, rest, :]


def halves_kernel(bits, one, got1, two, got2, send1, keep1, send2, keep2):
    b0, b1 = bits[0], bits[1]
    for z1 in range(2):
        for flip, ref1, ref2 in ((0, keep1, keep2), (1, send1, send2)):
            i, k = jnp.bitwise_xor(b1, flip), jnp.bitwise_xor(b0, flip)
            ref1[z1] = one[z1, i] + got1[z1, i]
            ref2[z1] = two[z1, k] + got2[z1, k]


def last_kernel(bits, one, got1, two, got2, send, keep):
    cut = one.shape[1]
    for flip, ref in ((0, keep), (1, send)):
        i = jnp.bitwise_xor(bits[2], flip)
        ref[pl.ds(0, cut), :] = one[i] + got1[i]
        ref[pl.ds(cut, two.shape[1]), :] = two[i] + got2[i]


VMEM = pl.BlockSpec(memory_space=pltpu.MemorySpace.VMEM)
SMEM = pl.BlockSpec(memory_space=pltpu.MemorySpace.SMEM)
ANY = pl.BlockSpec(memory_space=pl.ANY)
HBM = pl.BlockSpec(memory_space=pltpu.MemorySpace.HBM)


def call(kernel, name, ins, outs, scratch=(), aliases=None, flops=0, size=0):
    return pl.pallas_call(
        kernel,
        name=name,
        out_shape=[jax.ShapeDtypeStruct(s, d) for s, d, _ in outs],
        in_specs=ins,
        out_specs=[o for _, _, o in outs],
        scratch_shapes=list(scratch),
        input_output_aliases=aliases or {},
        compiler_params=pltpu.CompilerParams(vmem_limit_bytes=LIMIT),
        cost_estimate=pl.CostEstimate(flops=flops, transcendentals=0, bytes_accessed=size),
    )


def exchange(value, axis, bit):
    pairs = [(i, i ^ bit) for i in range(lax.axis_size(axis))]
    return lax.ppermute(value, axis, pairs)


def tied(*values):
    return lax.optimization_barrier(values)


def reduce_blocks(keep, got, fillers):
    s = lax.axis_index("space").astype(jnp.int32)
    bits = jnp.stack([s & 1, (s >> 1) & 1, (s >> 2) & 1])
    rows = keep.shape[1]
    cut = rows // 16 * 8

    def sums(kernel, name, lead, *values):
        shapes = [((*lead, cut, C), F32, VMEM)] * 2 + [((*lead, rows - cut, C), F32, VMEM)] * 2
        return call(kernel, name, [SMEM] + [VMEM] * len(values), shapes)(bits, *values)

    send1, keep1, send2, keep2 = sums(blocks_kernel, "blocks", (2, 2), keep, got)
    got1, got2 = exchange(send1, "space", 1), exchange(send2, "space", 2)
    got1, got2, fill = tied(got1, got2, fillers[0](None))
    send1, keep1, send2, keep2 = sums(halves_kernel, "halves", (2,), keep1, got1, keep2, got2)
    got1, got2 = exchange(send1, "space", 2), exchange(send2, "space", 1)
    send, keep = call(last_kernel, "last", [SMEM] + [VMEM] * 4, [((rows, C), F32, VMEM)] * 2)(
        bits, keep1, got1, keep2, got2
    )
    got, fill = tied(exchange(send, "space", 4), fillers[1](fill))
    return keep + got, fill


def on_device(features, out_grad, weight, neighbours, active):
    layers = lax.axis_size("space")
    sub = lax.axis_index("sub").astype(jnp.int32).reshape(1)
    strips, shift, bands = jnp.asarray(strip_matrix()), jnp.asarray(shift_matrix()), jnp.asarray(band_matrix())

    gm, own, mine, mask = call(
        prep_kernel,
        "prep",
        [SMEM] * 2 + [HBM] * 3,
        [
            ((BSIDE, PLANE, 2 * C), BF, VMEM),
            ((MINE + 208, 2 * C), BF, VMEM),
            ((208, 2 * C), BF, VMEM),
            ((14 * C, 2 * C), BF, VMEM),
        ],
        [
            pltpu.VMEM((2, VOX), jnp.int32),
            pltpu.VMEM((64, PLANE), BF),
            pltpu.VMEM((2, VOX, C), BF),
            pltpu.SemaphoreType.DMA((3,)),
        ],
    )(sub, neighbours, active, strips, out_grad)

    other = exchange(own, "sub", 1)
    pad, fs = call(
        features_kernel,
        "features",
        [VMEM] * 3,
        [((2, (EXT + 2) * PLANE, C), BF, VMEM), ((2, (EXT + 2) * 16, 2 * C), BF, VMEM)],
        flops=10**7,
        size=10**6,
    )(mask, strips, features)

    ways = [(2 * i, 2 * i + 2) for i in range(layers - 1)] + [(2 * i + 3, 2 * i + 1) for i in range(layers - 1)]
    got = lax.ppermute(jnp.concatenate([mine, other[MINE:]], axis=0), ("space", "sub"), ways)

    kop_shape = (EXT, KROWS, 2 * C)
    work = 2 * 3 * C * 9 * C * EXT * PLANE
    x, acc = call(
        first_kernel,
        "first",
        [VMEM] * 5,
        [((2, EXT * PLANE, 9 * C), BF, VMEM), ((3 * C, 9 * C), F32, VMEM)],
        [pltpu.VMEM(kop_shape, BF)],
        flops=2 * work,
        size=8 * 2**20,
    )(shift, gm, own, other, pad)
    got, acc = tied(got, acc)
    got2 = exchange(got, "sub", 1)
    (acc,) = call(
        second_kernel,
        "second",
        [VMEM, VMEM, VMEM],
        [((3 * C, 9 * C), F32, VMEM)],
        flops=work,
        size=4 * 2**20,
    )(pad, x, acc)

    size = 27 * C // (2 * layers)
    custom = layers == 8
    rows = (layers, size, C) if custom else (8, 216, C)
    keep, send, zs = call(
        tilt_kernel,
        "tilt",
        [SMEM] + [VMEM] * 6,
        [(rows, F32, VMEM), (rows, F32, VMEM), ((2, 2, EXT * 16, 3 * C), BF, VMEM)],
        [pltpu.VMEM((2, EXT * 16, 2 * C), BF), pltpu.VMEM((2, 3 * C, 3 * C), F32)],
        flops=work // 4,
        size=4 * 2**20,
    )(sub, own, got, got2, fs, bands, acc)

    def dgrad(j):
        def run(before):
            fresh = before is None
            return call(
                (lambda m, w, x_, z, *refs: dgrad_kernel(j, m, w, x_, z, None, *refs))
                if fresh
                else (lambda *refs: dgrad_kernel(j, *refs)),
                "dgrad",
                [VMEM] * 4 + ([] if fresh else [ANY]),
                [((2, VOX, C), BF, ANY)],
                [
                    pltpu.VMEM((EXT * PLANE, 3 * C), F32),
                    pltpu.VMEM((2, EXT * 16, 3 * C), F32),
                    pltpu.VMEM((PLANE + 16, C), F32),
                    pltpu.VMEM((VOX, C), BF),
                    pltpu.SemaphoreType.DMA,
                ],
                aliases={} if fresh else {4: 0},
                flops=work,
                size=4 * 2**20,
            )(mask, weight, x, zs, *(() if fresh else (before,)))[0]

        return run

    if custom:
        got = exchange(send, "sub", 1)
        got, zs = tied(got, zs)
        weight_grad, input_grad = reduce_blocks(keep, got, [dgrad(0), dgrad(1)])
    else:
        even = jnp.where(sub[0] == 0, keep, send)
        odd = jnp.where(sub[0] == 0, send, keep)
        kernel_term = jnp.stack([even, odd], axis=1).reshape(27 * C, C)
        weight_grad = lax.psum_scatter(kernel_term, ("space", "sub"), scatter_dimension=0, tiled=True)
        input_grad = dgrad(1)(dgrad(0)(None))
    return input_grad, weight_grad


def solution(mesh):
    in_specs = (
        P(("scene", "space", "sub"), None, None),
        P(("scene", "space", "sub"), None, None),
        P(),
        P(("scene", "space", "sub"), None),
        P(("scene", "space", "sub"), None),
    )
    out_specs = (P(("scene", "space", "sub"), None, None), P(("scene", "space", "sub"), None))
    return jax.shard_map(
        on_device, mesh=mesh, in_specs=in_specs, out_specs=out_specs, check_vma=False
    )
```

```python
import jax
import jax.numpy as jnp
import numpy as np
from jax import lax
from jax.experimental import pallas as pl
from jax.experimental.pallas import tpu as pltpu
from jax.sharding import PartitionSpec as P

BSIDE = 12
PLANE = BSIDE * BSIDE
VOX = BSIDE * PLANE
EXT = BSIDE + 2
C = 128
KROWS = 256
CUT = 112
MINE = PLANE + 208
BF = jnp.bfloat16
F32 = jnp.float32


def strip_matrix():
    m = np.zeros((64, PLANE), np.float32)
    for i in range(BSIDE):
        m[i, i * BSIDE] = 1
        m[16 + i, i * BSIDE + 11] = 1
        m[32 + i, i] = 1
        m[48 + i, 11 * BSIDE + i] = 1
    m[12, 0] = m[28, 11] = 1
    m[13, 11 * BSIDE] = m[29, 11 * BSIDE + 11] = 1
    return m.astype(jnp.bfloat16)


def shift_matrix():
    m = np.zeros((9, BSIDE, BSIDE, KROWS), np.float32)
    for k in range(9):
        for b in range(BSIDE):
            for c in range(BSIDE):
                sb, sc = b - (k // 3 - 1), c - (k % 3 - 1)
                if sc in (-1, 12):
                    row = {-1: 13, 12: 12}.get(sb, sb) + (176 if sc < 0 else 192)
                elif sb in (-1, 12):
                    row = sc + (144 if sb < 0 else 160)
                else:
                    row = sb * BSIDE + sc
                m[k, b, c, row] = 1
    return m.reshape(9 * PLANE, KROWS).astype(jnp.bfloat16)


def band_matrix():
    m = np.zeros((3, EXT, 16, EXT, 16), np.float32)
    for q in range(3):
        for b in range(BSIDE):
            source = b - (q - 1)
            for p in range(EXT):
                m[q, p, b, p, 13 if source < 0 else source] = 1
    return m.reshape(3 * EXT * 16, EXT * 16).astype(jnp.bfloat16)


def dot(a, b):
    return lax.dot_general(a, b, (((1,), (0,)), ((), ())), preferred_element_type=F32)


def dot_t(a, b):
    return lax.dot_general(a, b, (((1,), (1,)), ((), ())), preferred_element_type=F32)


def halves(x):
    return jnp.concatenate([x[:, C:], x[:, :C]], axis=1)


def per_half(first, second, rows=16):
    lane = lax.broadcasted_iota(jnp.int32, (rows, 2 * C), 1)
    return jnp.where(lane < C, first, second)


def masks(act, out):
    r = lax.broadcasted_iota(jnp.int32, (C, C), 0)
    eye = jnp.where(r == lax.broadcasted_iota(jnp.int32, (C, C), 1), 1.0, 0.0)
    wide = lax.broadcasted_iota(jnp.int32, (2 * C, 2 * C), 0) < C
    ones = jnp.where(wide == (lax.broadcasted_iota(jnp.int32, (2 * C, 2 * C), 1) < C), 1.0, 0.0).astype(BF)
    for n in range(0, VOX, C):
        cols = []
        for j in range(2):
            a = act[pl.ds(j, 1), pl.ds(n, min(C, VOX - n))].astype(F32)
            if n + C > VOX:
                a = jnp.concatenate([a, jnp.zeros((1, n + C - VOX), F32)], axis=1)
            cols.append((eye * a).astype(BF))
        out[pl.ds(n, C), :] = dot(jnp.concatenate(cols, axis=1), ones).astype(BF)


def prep_kernel(sub, nb_hbm, act_hbm, strips_hbm, g_hbm, gm, message, mine, mask, strips, nb, act, g, sem):
    loads = [
        pltpu.make_async_copy(act_hbm, act, sem.at[0]),
        pltpu.make_async_copy(strips_hbm, strips, sem.at[1]),
        pltpu.make_async_copy(nb_hbm, nb, sem.at[2]),
    ]
    for n in range(4):
        rows = pl.ds(n * VOX // 4, VOX // 4)
        loads.append(pltpu.make_async_copy(g_hbm.at[:, rows], g.at[:, rows], sem.at[3 + n]))
    for load in loads:
        load.start()
    loads[0].wait()
    masks(act, mask)
    loads[2].wait()
    a0 = per_half((nb[0, 0] >= 0).astype(F32), (nb[1, 0] >= 0).astype(F32))
    b0 = per_half((nb[0, 2] >= 0).astype(F32), (nb[1, 2] >= 0).astype(F32))
    code = (2 * a0 + b0).astype(BF)
    a0, b0 = a0.astype(BF), b0.astype(BF)
    second = jnp.full((16, 2 * C), sub[0].astype(F32), F32).astype(BF)
    loads[1].wait()
    for p in range(BSIDE):
        if p % 3 == 0:
            loads[3 + p // 3].wait()
        rows = pl.ds(p * PLANE, PLANE)
        plane = jnp.concatenate([g[0, rows, :], g[1, rows, :]], axis=1) * mask[rows, :]
        gm[p] = plane
        s = dot(strips[...], plane).astype(BF)
        mine[pl.ds(p * 16, 16), :] = s[0:16] * second + s[16:32] * (1 - second)
        message[pl.ds(MINE + p * 16, 16), :] = s[16:32] * second + s[0:16] * (1 - second)
        message[pl.ds(PLANE + p * 16, 16), :] = s[32:48] * b0 + s[48:64] * (1 - b0)
    for r in range(0, PLANE, 16):
        message[pl.ds(r, 16), :] = gm[0, pl.ds(r, 16), :] * a0 + gm[11, pl.ds(r, 16), :] * (1 - a0)
    message[pl.ds(PLANE + 192, 16), :] = code
    message[pl.ds(MINE + 192, 16), :] = code
    mine[pl.ds(192, 16), :] = code


def features_kernel(mask, strips, f_hbm, pad, fs, f, sem):
    load = pltpu.make_async_copy(f_hbm, f, sem)
    load.start()
    zero = jnp.zeros((2 * PLANE, C), BF)
    edge = jnp.zeros((32, 2 * C), BF)
    for j in range(2):
        pad[j, pl.ds(0, 2 * PLANE), :] = zero
        pad[j, pl.ds(EXT * PLANE, 2 * PLANE), :] = zero
    load.wait()
    for j in range(2):
        pad[j, pl.ds(2 * PLANE, VOX), :] = f[j] * mask[pl.ds(0, VOX), pl.ds(j * C, C)]
    for n in range(2):
        fs[n, pl.ds(0, 32), :] = edge
        fs[n, pl.ds(EXT * 16, 32), :] = edge
    for p in range(BSIDE):
        rows = pl.ds((p + 2) * PLANE, PLANE)
        s = dot(strips[pl.ds(0, 32), :], jnp.concatenate([pad[0, rows, :], pad[1, rows, :]], axis=1)).astype(BF)
        for n in range(2):
            fs[n, pl.ds((p + 2) * 16, 16), :] = s[16 * n : 16 * n + 16]


def position(own):
    code = own[pl.ds(336, 16), :].astype(F32)
    a0 = jnp.where(code >= 2, 1.0, 0.0)
    b0 = code - 2 * a0
    return code, a0, b0


def candidates(refs, at):
    tiles = []
    for ref, base, swapped in refs:
        t = ref[pl.ds(base + at, 16), :].astype(F32)
        tiles.append(((ref, base, swapped), halves(t) if swapped else t))
    return tiles


def hits(cands, q):
    return [(*source, jnp.where(t == q, 1.0, 0.0).astype(BF)) for source, t in cands]


def gather(picks, row):
    total = None
    for ref, base, swapped, w in picks:
        x = ref[pl.ds(base + row, 16), :]
        x = (halves(x) if swapped else x) * w
        total = x if total is None else total + x
    return total


def layer_operands(gm, own, other, kop):
    code, a0, b0 = position(own)
    layer = candidates([(own, 0, True), (other, 0, False), (other, 0, True)], 336)
    pick_a = hits(layer, code + 2 - 4 * a0)
    pick_b = hits(layer, code + 1 - 2 * b0)
    pick_d = hits(layer, 3 - code)
    a0h, b0h = a0.astype(BF), b0.astype(BF)
    a1h, b1h = 1 - a0h, 1 - b0h
    rest = jnp.zeros((KROWS - 176, 2 * C), BF)
    for p in range(BSIDE):
        kop[p + 1, pl.ds(0, PLANE), :] = gm[p]
        side = gather(pick_b, PLANE + p * 16)
        kop[p + 1, pl.ds(144, 16), :] = side * b0h
        kop[p + 1, pl.ds(160, 16), :] = side * b1h
        kop[p + 1, pl.ds(176, KROWS - 176), :] = rest
    for at, plane, w in ((0, 11, a0h), (EXT - 1, 0, a1h)):
        for r in range(0, PLANE, 16):
            kop[at, pl.ds(r, 16), :] = gather(pick_a, r) * w
        side = gather(pick_d, PLANE + plane * 16) * w
        kop[at, pl.ds(144, 16), :] = side * b0h
        kop[at, pl.ds(160, 16), :] = side * b1h
        kop[at, pl.ds(176, KROWS - 176), :] = rest


def vertical_operands(own, zs, z):
    code, a0, b0 = position(own)
    row16 = lax.broadcasted_iota(jnp.int32, (16, 2 * C), 0)
    inner = jnp.where(row16 < 12, 1.0, 0.0).astype(BF)
    edge = jnp.where(row16 == 12, 1 - b0, jnp.where(row16 == 13, b0, 0.0)).astype(BF)
    a0h = a0.astype(BF)
    for n, ref in enumerate(zs):
        cands = candidates([(ref, base, swapped) for base in (0, 208) for swapped in (False, True)], 192)
        near = [(*q, w * inner) for *q, w in hits(cands, code)]
        near += [(*q, w * edge) for *q, w in hits(cands, code + 1 - 2 * b0)]
        far = [(*q, w * inner) for *q, w in hits(cands, code + 2 - 4 * a0)]
        far += [(*q, w * edge) for *q, w in hits(cands, 3 - code)]
        for p in range(BSIDE):
            z[n, pl.ds((p + 1) * 16, 16), :] = gather(near, p * 16)
        z[n, pl.ds(0, 16), :] = gather(far, 11 * 16) * a0h
        z[n, pl.ds((EXT - 1) * 16, 16), :] = gather(far, 0) * (1 - a0h)


def shifted(shift, kop, x, ks, first, count):
    for p in range(count):
        for n, k in enumerate(ks):
            y = dot(shift[pl.ds(k * PLANE, PLANE), :], kop[first + p]).astype(BF)
            for j in range(2):
                x[j, pl.ds(p * PLANE, PLANE), pl.ds(n * C, C)] = y[:, j * C : j * C + C]


def stacked(ref, j, width, lanes):
    return jnp.concatenate([ref[j, pl.ds(d * width, EXT * width), lanes] for d in range(3)], axis=1)


def dot_rows(a, b):
    return lax.dot_general(a, b, (((0,), (0,)), ((), ())), preferred_element_type=F32)


def first_kernel(shift, gm, own, other, pad, x, acc, kop):
    layer_operands(gm, own, other, kop)
    shifted(shift, kop, x, range(9), 0, EXT)
    acc[...] = dot_rows(stacked(pad, 0, PLANE, slice(None)), x[0])


def second_kernel(pad, x, before, acc):
    acc[...] = before[...] + dot_rows(stacked(pad, 1, PLANE, slice(None)), x[1])


def tilt_kernel(sub, own, got, got2, fs, bands, acc, keep, send, zs, z, more):
    for parity in range(2):

        @pl.when(sub[0] == parity)
        def _(parity=parity):
            vertical_operands(own, (got2, got) if parity else (got, got2), z)

    for n in range(2):
        v = dot(bands[...], z[n]).astype(BF)
        rows = EXT * 16
        total = None
        for j in range(2):
            lanes = slice(j * C, j * C + C)
            zs[n, j] = jnp.concatenate([v[q * rows : q * rows + rows, lanes] for q in range(3)], axis=1)
            f3 = jnp.concatenate([fs[n, pl.ds(d * 16, rows), lanes] for d in range(3)], axis=1)
            part_ = dot_rows(f3, zs[n, j])
            total = part_ if total is None else total + part_
        more[n] = total
    size = keep.shape[1]
    for parity in range(2):

        @pl.when(sub[0] == parity)
        def _(parity=parity):
            for t in range(27):
                da, k = divmod(t, 9)
                row = t * C
                while row < (t + 1) * C:
                    block = row // size
                    end = min((block + 1) * size, (t + 1) * C)
                    at = pl.ds(da * C + row - t * C, end - row)
                    v = acc[at, pl.ds(k * C, C)]
                    if k % 3 != 1:
                        v = v + more[0 if k % 3 == 2 else 1, at, pl.ds(k // 3 * C, C)]
                    ref = keep if block % 2 == parity else send
                    ref[block // 2, pl.ds(row - block * size, end - row), :] = v * (1.0 / VOX)
                    row = end


def columns(w, ks):
    return jnp.concatenate([jnp.concatenate([w[d * 9 + k] for k in ks], axis=1) for d in range(3)], axis=0)


def joined(y, p, rows):
    total = y[pl.ds((p + 2) * rows, rows), pl.ds(0, C)]
    total = total + y[pl.ds((p + 1) * rows, rows), pl.ds(C, C)]
    return total + y[pl.ds(p * rows, rows), pl.ds(2 * C, C)]


def dgrad_kernel(j, mask, w, x, zs, before, out, y, yz, plane, res, sem):
    del before
    y[...] = dot_t(x[j], columns(w, range(9)))
    for n in range(2):
        yz[n] = dot_t(zs[n, j], columns(w, (2, 5, 8) if n == 0 else (0, 3, 6)))
    for p in range(BSIDE):
        plane[pl.ds(0, PLANE), :] = joined(y, p, PLANE)
        for n in range(2):
            at = pl.ds(11 * n, BSIDE, stride=BSIDE)
            plane[at, :] = plane[at, :] + joined(yz.at[n], p, 16)[:BSIDE]
        m = mask[pl.ds(p * PLANE, PLANE), pl.ds(j * C, C)].astype(F32)
        res[pl.ds(p * PLANE, PLANE), :] = (plane[pl.ds(0, PLANE), :] * m).astype(BF)
    store = pltpu.make_async_copy(res, out.at[j], sem)
    store.start()
    store.wait()


def encode(ref, at, v):
    top = jnp.maximum(jnp.max(jnp.abs(v), axis=0, keepdims=True), 1e-33)
    e = jnp.floor(jnp.log2(top)) - 14
    q = jnp.clip(jnp.round(v * jnp.exp2(-e)), -32767, 32767)
    if v.shape[0] < CUT:
        q = jnp.concatenate([q, jnp.zeros((CUT - v.shape[0], C), F32)], axis=0)
    ref[(*at, pl.ds(0, CUT), slice(None))] = q.astype(jnp.int32).astype(jnp.int16)
    e = jnp.broadcast_to(e, (C - CUT, C))
    ref[(*at, pl.ds(CUT, C - CUT), slice(None))] = e.astype(jnp.int32).astype(jnp.int16)


def decoded(ref, at, rows):
    e = ref[(*at, pl.ds(CUT, C - CUT), slice(None))].astype(jnp.int32).astype(F32)[:1]
    q = ref[(*at, pl.ds(0, CUT), slice(None))].astype(jnp.int32).astype(F32)
    return (q * jnp.exp2(e))[:rows]


def blocks_kernel(bits, keep, got, send1, keep1, send2, keep2):
    b0, b1 = bits[1], bits[2]
    rest = pl.ds(CUT, keep.shape[1] - CUT)
    for z1 in range(2):
        for n in range(2):
            i, k = z1 * 4 + n * 2 + 1 - b0, z1 * 4 + (1 - b1) * 2 + n
            encode(send1, (z1, n), keep[i, pl.ds(0, CUT), :] + got[i, pl.ds(0, CUT), :])
            encode(send2, (z1, n), keep[k, rest, :] + got[k, rest, :])
            i, k = z1 * 4 + n * 2 + b0, z1 * 4 + b1 * 2 + n
            keep1[z1, n] = keep[i, pl.ds(0, CUT), :] + got[i, pl.ds(0, CUT), :]
            keep2[z1, n] = keep[k, rest, :] + got[k, rest, :]


def halves_kernel(bits, one, got1, two, got2, send1, keep1, send2, keep2):
    b0, b1 = bits[1], bits[2]
    rest = two.shape[2]
    for z1 in range(2):
        encode(send1, (z1,), one[z1, 1 - b1] + decoded(got1, (z1, 1 - b1), CUT))
        encode(send2, (z1,), two[z1, 1 - b0] + decoded(got2, (z1, 1 - b0), rest))
        keep1[z1] = one[z1, b1] + decoded(got1, (z1, b1), CUT)
        keep2[z1] = two[z1, b0] + decoded(got2, (z1, b0), rest)


def last_kernel(bits, one, got1, two, got2, send, keep):
    b2 = bits[3]
    rest = two.shape[1]
    encode(send, (0,), one[1 - b2] + decoded(got1, (1 - b2,), CUT))
    encode(send, (1,), two[1 - b2] + decoded(got2, (1 - b2,), rest))
    keep[pl.ds(0, CUT), :] = one[b2] + decoded(got1, (b2,), CUT)
    keep[pl.ds(CUT, rest), :] = two[b2] + decoded(got2, (b2,), rest)


def sum_kernel(keep, got, out):
    rest = keep.shape[0] - CUT
    out[pl.ds(0, CUT), :] = keep[pl.ds(0, CUT), :] + decoded(got, (0,), CUT)
    out[pl.ds(CUT, rest), :] = keep[pl.ds(CUT, rest), :] + decoded(got, (1,), rest)


VMEM = pl.BlockSpec(memory_space=pltpu.MemorySpace.VMEM)
SMEM = pl.BlockSpec(memory_space=pltpu.MemorySpace.SMEM)
ANY = pl.BlockSpec(memory_space=pl.ANY)
HBM = pl.BlockSpec(memory_space=pltpu.MemorySpace.HBM)
FIXED = None


def call(kernel, name, ins, outs, scratch=(), aliases=None, flops=0, size=0, limit=4):
    return pl.pallas_call(
        kernel,
        name=name,
        out_shape=[pltpu.VMEM(s, d) if o is FIXED else jax.ShapeDtypeStruct(s, d) for s, d, o in outs],
        in_specs=ins,
        out_specs=[VMEM if o is FIXED else o for _, _, o in outs],
        scratch_shapes=list(scratch),
        input_output_aliases=aliases or {},
        compiler_params=pltpu.CompilerParams(vmem_limit_bytes=limit * 2**20),
        cost_estimate=pl.CostEstimate(flops=flops, transcendentals=0, bytes_accessed=size),
    )


def exchange(value, axis, bit):
    pairs = [(i, i ^ bit) for i in range(lax.axis_size(axis))]
    return lax.ppermute(value, axis, pairs)


def in_hbm(value):
    return pltpu.with_memory_space_constraint(value, pltpu.MemorySpace.HBM)


def in_vmem(value):
    return pltpu.with_memory_space_constraint(value, pltpu.MemorySpace.VMEM)


def tied(*values):
    return lax.optimization_barrier(values)


def reduce_blocks(bits, keep, got, fillers):
    rest = keep.shape[1] - CUT

    def sums(kernel, name, lead, *values):
        code = ((*lead, C, C), jnp.int16, VMEM)
        shapes = [code, ((*lead, CUT, C), F32, VMEM), code, ((*lead, rest, C), F32, VMEM)]
        return call(kernel, name, [SMEM] + [VMEM] * len(values), shapes)(bits, *(in_vmem(v) for v in values))

    send1, keep1, send2, keep2 = sums(blocks_kernel, "blocks", (2, 2), keep, got)
    got1, got2 = exchange(send1, "space", 1), exchange(send2, "space", 2)
    got1, got2, fill = tied(got1, got2, fillers[0](None))
    send1, keep1, send2, keep2 = sums(halves_kernel, "halves", (2,), keep1, got1, keep2, got2)
    got1, got2 = exchange(send1, "space", 2), exchange(send2, "space", 1)
    send, keep = call(
        last_kernel, "last", [SMEM] + [VMEM] * 4, [((2, C, C), jnp.int16, VMEM), ((CUT + rest, C), F32, VMEM)]
    )(bits, keep1, got1, keep2, got2)
    got, fill = tied(exchange(send, "space", 4), fillers[1](fill))
    return call(sum_kernel, "sum", [VMEM] * 2, [((CUT + rest, C), F32, VMEM)])(keep, got)[0], fill


def on_device(features, out_grad, weight, neighbours, active):
    layers = lax.axis_size("space")
    core, layer = lax.axis_index("sub").astype(jnp.int32), lax.axis_index("space").astype(jnp.int32)
    sub = jnp.stack([core, layer & 1, (layer >> 1) & 1, (layer >> 2) & 1])
    strips, shift, bands = jnp.asarray(strip_matrix()), jnp.asarray(shift_matrix()), jnp.asarray(band_matrix())

    gm, own, mine, mask, strips = call(
        prep_kernel,
        "prep",
        [SMEM] + [HBM] * 4,
        [
            ((BSIDE, PLANE, 2 * C), BF, VMEM),
            ((MINE + 208, 2 * C), BF, VMEM),
            ((208, 2 * C), BF, VMEM),
            ((14 * C, 2 * C), BF, VMEM),
            ((64, PLANE), BF, VMEM),
        ],
        [
            pltpu.SMEM((2, 6), jnp.int32),
            pltpu.VMEM((2, VOX), jnp.int32),
            pltpu.VMEM((2, VOX, C), BF),
            pltpu.SemaphoreType.DMA((7,)),
        ],
    )(sub, in_hbm(neighbours), in_hbm(active), in_hbm(strips), in_hbm(out_grad))

    other, mask = tied(exchange(own, "sub", 1), mask)
    pad, fs = call(
        features_kernel,
        "features",
        [VMEM] * 2 + [HBM],
        [((2, (EXT + 2) * PLANE, C), BF, VMEM), ((2, (EXT + 2) * 16, 2 * C), BF, VMEM)],
        [pltpu.VMEM((2, VOX, C), BF), pltpu.SemaphoreType.DMA],
        flops=10**7,
        size=10**6,
    )(mask, strips, in_hbm(features))

    ways = [(2 * i, 2 * i + 2) for i in range(layers - 1)] + [(2 * i + 3, 2 * i + 1) for i in range(layers - 1)]
    got = lax.ppermute(jnp.concatenate([mine, other[MINE:]], axis=0), ("space", "sub"), ways)

    kop_shape = (EXT, KROWS, 2 * C)
    work = 2 * 3 * C * 9 * C * EXT * PLANE
    x, acc = call(
        first_kernel,
        "first",
        [VMEM] * 5,
        [((2, EXT * PLANE, 9 * C), BF, FIXED), ((3 * C, 9 * C), F32, VMEM)],
        [pltpu.VMEM(kop_shape, BF)],
        flops=2 * work,
        size=8 * 2**20,
        limit=6,
    )(shift, gm, own, other, pad)
    got, acc = tied(got, acc)
    got2 = exchange(got, "sub", 1)
    (acc,) = call(
        second_kernel,
        "second",
        [VMEM, VMEM, VMEM],
        [((3 * C, 9 * C), F32, VMEM)],
        flops=work,
        size=4 * 2**20,
    )(pad, in_vmem(x), acc)

    size = 27 * C // (2 * layers)
    custom = layers == 8
    rows = (layers, size, C) if custom else (8, 216, C)
    keep, send, zs = call(
        tilt_kernel,
        "tilt",
        [SMEM] + [VMEM] * 6,
        [(rows, F32, FIXED), (rows, F32, FIXED), ((2, 2, EXT * 16, 3 * C), BF, VMEM)],
        [pltpu.VMEM((2, EXT * 16, 2 * C), BF), pltpu.VMEM((2, 3 * C, 3 * C), F32)],
        flops=work // 4,
        size=4 * 2**20,
    )(sub, own, got, got2, fs, bands, acc)

    def dgrad(j):
        def run(before):
            fresh = before is None
            return call(
                (lambda m, w, x_, z, *refs: dgrad_kernel(j, m, w, x_, z, None, *refs))
                if fresh
                else (lambda *refs: dgrad_kernel(j, *refs)),
                "dgrad",
                [VMEM] * 4 + ([] if fresh else [ANY]),
                [((2, VOX, C), BF, ANY)],
                [
                    pltpu.VMEM((EXT * PLANE, 3 * C), F32),
                    pltpu.VMEM((2, EXT * 16, 3 * C), F32),
                    pltpu.VMEM((PLANE + 16, C), F32),
                    pltpu.VMEM((VOX, C), BF),
                    pltpu.SemaphoreType.DMA,
                ],
                aliases={} if fresh else {4: 0},
                flops=work,
                size=4 * 2**20,
                limit=10,
            )(mask, weight, in_vmem(x), zs, *(() if fresh else (before,)))[0]

        return run

    if custom:
        got = exchange(send, "sub", 1)
        got, zs = tied(got, zs)
        weight_grad, input_grad = reduce_blocks(sub, keep, got, [dgrad(0), dgrad(1)])
    else:
        even = jnp.where(sub[0] == 0, keep, send)
        odd = jnp.where(sub[0] == 0, send, keep)
        kernel_term = jnp.stack([even, odd], axis=1).reshape(27 * C, C)
        weight_grad = lax.psum_scatter(kernel_term, ("space", "sub"), scatter_dimension=0, tiled=True)
        input_grad = dgrad(1)(dgrad(0)(None))
    return input_grad, weight_grad


def solution(mesh):
    in_specs = (
        P(("scene", "space", "sub"), None, None),
        P(("scene", "space", "sub"), None, None),
        P(),
        P(("scene", "space", "sub"), None),
        P(("scene", "space", "sub"), None),
    )
    out_specs = (P(("scene", "space", "sub"), None, None), P(("scene", "space", "sub"), None))
    return jax.shard_map(
        on_device, mesh=mesh, in_specs=in_specs, out_specs=out_specs, check_vma=False
    )
```

```python
import jax
import jax.numpy as jnp
import numpy as np
from jax import lax
from jax.experimental import pallas as pl
from jax.experimental.pallas import tpu as pltpu
from jax.sharding import PartitionSpec as P

BSIDE = 12
PLANE = BSIDE * BSIDE
VOX = BSIDE * PLANE
EXT = BSIDE + 2
C = 128
KROWS = 256
EARLY = 9
CUT = 112
MINE = PLANE + 208
BF = jnp.bfloat16
F32 = jnp.float32


def strip_matrix():
    m = np.zeros((64, PLANE), np.float32)
    for i in range(BSIDE):
        m[i, i * BSIDE] = 1
        m[16 + i, i * BSIDE + 11] = 1
        m[32 + i, i] = 1
        m[48 + i, 11 * BSIDE + i] = 1
    m[12, 0] = m[28, 11] = 1
    m[13, 11 * BSIDE] = m[29, 11 * BSIDE + 11] = 1
    return m.astype(jnp.bfloat16)


def shift_matrix():
    m = np.zeros((9, BSIDE, BSIDE, KROWS), np.float32)
    for k in range(9):
        for b in range(BSIDE):
            for c in range(BSIDE):
                sb, sc = b - (k // 3 - 1), c - (k % 3 - 1)
                if sc in (-1, 12):
                    row = {-1: 13, 12: 12}.get(sb, sb) + (176 if sc < 0 else 192)
                elif sb in (-1, 12):
                    row = sc + (144 if sb < 0 else 160)
                else:
                    row = sb * BSIDE + sc
                m[k, b, c, row] = 1
    return m.reshape(9 * PLANE, KROWS).astype(jnp.bfloat16)


def band_matrix():
    m = np.zeros((3, EXT, 16, EXT, 16), np.float32)
    for q in range(3):
        for b in range(BSIDE):
            source = b - (q - 1)
            for p in range(EXT):
                m[q, p, b, p, 13 if source < 0 else source] = 1
    return m.reshape(3 * EXT * 16, EXT * 16).astype(jnp.bfloat16)


def dot(a, b):
    return lax.dot_general(a, b, (((1,), (0,)), ((), ())), preferred_element_type=F32)


def dot_t(a, b):
    return lax.dot_general(a, b, (((1,), (1,)), ((), ())), preferred_element_type=F32)


def halves(x):
    return jnp.concatenate([x[:, C:], x[:, :C]], axis=1)


def per_half(first, second, rows=16):
    lane = lax.broadcasted_iota(jnp.int32, (rows, 2 * C), 1)
    return jnp.where(lane < C, first, second)


def masks(act, out):
    r = lax.broadcasted_iota(jnp.int32, (C, C), 0)
    eye = jnp.where(r == lax.broadcasted_iota(jnp.int32, (C, C), 1), 1.0, 0.0)
    wide = lax.broadcasted_iota(jnp.int32, (2 * C, 2 * C), 0) < C
    ones = jnp.where(wide == (lax.broadcasted_iota(jnp.int32, (2 * C, 2 * C), 1) < C), 1.0, 0.0).astype(BF)
    for n in range(0, VOX, C):
        cols = []
        for j in range(2):
            a = act[pl.ds(j, 1), pl.ds(n, min(C, VOX - n))].astype(F32)
            if n + C > VOX:
                a = jnp.concatenate([a, jnp.zeros((1, n + C - VOX), F32)], axis=1)
            cols.append((eye * a).astype(BF))
        out[pl.ds(n, C), :] = dot(jnp.concatenate(cols, axis=1), ones).astype(BF)


def prep_kernel(nb_hbm, act_hbm, strips_hbm, g_hbm, gm, message, mine, mask, strips, nb, act, g, sem):
    loads = [
        pltpu.make_async_copy(act_hbm, act, sem.at[0]),
        pltpu.make_async_copy(strips_hbm, strips, sem.at[1]),
        pltpu.make_async_copy(nb_hbm, nb, sem.at[2]),
    ]
    for n in range(4):
        rows = pl.ds(n * VOX // 4, VOX // 4)
        loads.append(pltpu.make_async_copy(g_hbm.at[:, rows], g.at[:, rows], sem.at[3 + n]))
    for load in loads:
        load.start()
    loads[0].wait()
    masks(act, mask)
    loads[2].wait()
    a0 = per_half((nb[0, 0] >= 0).astype(F32), (nb[1, 0] >= 0).astype(F32))
    b0 = per_half((nb[0, 2] >= 0).astype(F32), (nb[1, 2] >= 0).astype(F32))
    code = (2 * a0 + b0).astype(BF)
    a0, b0 = a0.astype(BF), b0.astype(BF)
    second = jnp.full((16, 2 * C), lax.axis_index("sub").astype(F32), F32).astype(BF)
    loads[1].wait()
    for p in range(BSIDE):
        if p % 3 == 0:
            loads[3 + p // 3].wait()
        rows = pl.ds(p * PLANE, PLANE)
        plane = jnp.concatenate([g[0, rows, :], g[1, rows, :]], axis=1) * mask[rows, :]
        gm[p] = plane
        s = dot(strips[...], plane).astype(BF)
        mine[pl.ds(p * 16, 16), :] = s[0:16] * second + s[16:32] * (1 - second)
        message[pl.ds(MINE + p * 16, 16), :] = s[16:32] * second + s[0:16] * (1 - second)
        message[pl.ds(PLANE + p * 16, 16), :] = s[32:48] * b0 + s[48:64] * (1 - b0)
    for r in range(0, PLANE, 16):
        message[pl.ds(r, 16), :] = gm[0, pl.ds(r, 16), :] * a0 + gm[11, pl.ds(r, 16), :] * (1 - a0)
    message[pl.ds(PLANE + 192, 16), :] = code
    message[pl.ds(MINE + 192, 16), :] = code
    mine[pl.ds(192, 16), :] = code


def features_kernel(mask, strips, f_hbm, pad, fs, f, sem):
    load = pltpu.make_async_copy(f_hbm, f, sem)
    load.start()
    zero = jnp.zeros((2 * PLANE, C), BF)
    edge = jnp.zeros((32, 2 * C), BF)
    for j in range(2):
        pad[j, pl.ds(0, 2 * PLANE), :] = zero
        pad[j, pl.ds(EXT * PLANE, 2 * PLANE), :] = zero
    load.wait()
    for j in range(2):
        pad[j, pl.ds(2 * PLANE, VOX), :] = f[j] * mask[pl.ds(0, VOX), pl.ds(j * C, C)]
    for n in range(2):
        fs[n, pl.ds(0, 32), :] = edge
        fs[n, pl.ds(EXT * 16, 32), :] = edge
    for p in range(BSIDE):
        rows = pl.ds((p + 2) * PLANE, PLANE)
        s = dot(strips[pl.ds(0, 32), :], jnp.concatenate([pad[0, rows, :], pad[1, rows, :]], axis=1)).astype(BF)
        for n in range(2):
            fs[n, pl.ds((p + 2) * 16, 16), :] = s[16 * n : 16 * n + 16]


def position(own):
    code = own[pl.ds(336, 16), :].astype(F32)
    a0 = jnp.where(code >= 2, 1.0, 0.0)
    b0 = code - 2 * a0
    return code, a0, b0


def candidates(refs, at):
    tiles = []
    for ref, base, swapped in refs:
        t = ref[pl.ds(base + at, 16), :].astype(F32)
        tiles.append(((ref, base, swapped), halves(t) if swapped else t))
    return tiles


def hits(cands, q):
    return [(*source, jnp.where(t == q, 1.0, 0.0).astype(BF)) for source, t in cands]


def gather(picks, row):
    total = None
    for ref, base, swapped, w in picks:
        x = ref[pl.ds(base + row, 16), :]
        x = (halves(x) if swapped else x) * w
        total = x if total is None else total + x
    return total


def layer_operands(gm, own, other, kop):
    code, a0, b0 = position(own)
    layer = candidates([(own, 0, True), (other, 0, False), (other, 0, True)], 336)
    pick_a = hits(layer, code + 2 - 4 * a0)
    pick_b = hits(layer, code + 1 - 2 * b0)
    pick_d = hits(layer, 3 - code)
    a0h, b0h = a0.astype(BF), b0.astype(BF)
    a1h, b1h = 1 - a0h, 1 - b0h
    rest = jnp.zeros((KROWS - 176, 2 * C), BF)
    for p in range(BSIDE):
        kop[p + 1, pl.ds(0, PLANE), :] = gm[p]
        side = gather(pick_b, PLANE + p * 16)
        kop[p + 1, pl.ds(144, 16), :] = side * b0h
        kop[p + 1, pl.ds(160, 16), :] = side * b1h
        kop[p + 1, pl.ds(176, KROWS - 176), :] = rest
    for at, plane, w in ((0, 11, a0h), (EXT - 1, 0, a1h)):
        for r in range(0, PLANE, 16):
            kop[at, pl.ds(r, 16), :] = gather(pick_a, r) * w
        side = gather(pick_d, PLANE + plane * 16) * w
        kop[at, pl.ds(144, 16), :] = side * b0h
        kop[at, pl.ds(160, 16), :] = side * b1h
        kop[at, pl.ds(176, KROWS - 176), :] = rest


def vertical_operands(own, zs, z):
    code, a0, b0 = position(own)
    row16 = lax.broadcasted_iota(jnp.int32, (16, 2 * C), 0)
    inner = jnp.where(row16 < 12, 1.0, 0.0).astype(BF)
    edge = jnp.where(row16 == 12, 1 - b0, jnp.where(row16 == 13, b0, 0.0)).astype(BF)
    a0h = a0.astype(BF)
    for n, ref in enumerate(zs):
        cands = candidates([(ref, base, swapped) for base in (0, 208) for swapped in (False, True)], 192)
        near = [(*q, w * inner) for *q, w in hits(cands, code)]
        near += [(*q, w * edge) for *q, w in hits(cands, code + 1 - 2 * b0)]
        far = [(*q, w * inner) for *q, w in hits(cands, code + 2 - 4 * a0)]
        far += [(*q, w * edge) for *q, w in hits(cands, 3 - code)]
        for p in range(BSIDE):
            z[n, pl.ds((p + 1) * 16, 16), :] = gather(near, p * 16)
        z[n, pl.ds(0, 16), :] = gather(far, 11 * 16) * a0h
        z[n, pl.ds((EXT - 1) * 16, 16), :] = gather(far, 0) * (1 - a0h)


def shifted(shift, kop, x, ks, first, count):
    for p in range(count):
        for n, k in enumerate(ks):
            if k == 4:
                y = kop[first + p, pl.ds(0, PLANE), :]
            else:
                y = dot(shift[pl.ds(k * PLANE, PLANE), :], kop[first + p]).astype(BF)
            for j in range(2):
                x[j, pl.ds(p * PLANE, PLANE), pl.ds(n * C, C)] = y[:, j * C : j * C + C]


def stacked(ref, j, first, count):
    return jnp.concatenate([ref[j, pl.ds((d + first) * PLANE, count * PLANE), :] for d in range(3)], axis=1)


def dot_rows(a, b):
    return lax.dot_general(a, b, (((0,), (0,)), ((), ())), preferred_element_type=F32)


def first_kernel(shift, gm, own, other, pad, x, acc, kop):
    layer_operands(gm, own, other, kop)
    shifted(shift, kop, x, range(9), 0, EXT)
    acc[...] = dot_rows(stacked(pad, 0, 0, EXT), x[0])
    acc[...] += dot_rows(stacked(pad, 1, 0, EARLY), x[1, pl.ds(0, EARLY * PLANE), :])


def second_kernel(pad, x, before, acc):
    late = EXT - EARLY
    acc[...] = before[...] + dot_rows(stacked(pad, 1, EARLY, late), x[1, pl.ds(EARLY * PLANE, late * PLANE), :])


def encode(ref, at, v):
    top = jnp.maximum(jnp.max(jnp.abs(v), axis=0, keepdims=True), 1e-33)
    e = jnp.floor(jnp.log2(top)) - 14
    q = jnp.clip(jnp.round(v * jnp.exp2(-e)), -32767, 32767)
    if v.shape[0] < CUT:
        q = jnp.concatenate([q, jnp.zeros((CUT - v.shape[0], C), F32)], axis=0)
    ref[(*at, pl.ds(0, CUT), slice(None))] = q.astype(jnp.int32).astype(jnp.int16)
    e = jnp.broadcast_to(e, (C - CUT, C))
    ref[(*at, pl.ds(CUT, C - CUT), slice(None))] = e.astype(jnp.int32).astype(jnp.int16)


def decoded(ref, at, rows):
    e = ref[(*at, pl.ds(CUT, C - CUT), slice(None))].astype(jnp.int32).astype(F32)[:1]
    q = ref[(*at, pl.ds(0, CUT), slice(None))].astype(jnp.int32).astype(F32)
    return (q * jnp.exp2(e))[:rows]


def tilt_kernel(own, got, got2, fs, bands, acc, keep, code, zs, z, more, send):
    sub = lax.axis_index("sub")
    for parity in range(2):

        @pl.when(sub == parity)
        def _(parity=parity):
            vertical_operands(own, (got2, got) if parity else (got, got2), z)

    for n in range(2):
        v = dot(bands[...], z[n]).astype(BF)
        rows = EXT * 16
        total = None
        for j in range(2):
            lanes = slice(j * C, j * C + C)
            zs[n, j] = jnp.concatenate([v[q * rows : q * rows + rows, lanes] for q in range(3)], axis=1)
            f3 = jnp.concatenate([fs[n, pl.ds(d * 16, rows), lanes] for d in range(3)], axis=1)
            part_ = dot_rows(f3, zs[n, j])
            total = part_ if total is None else total + part_
        more[n] = total
    size = keep.shape[1]
    for parity in range(2):

        @pl.when(sub == parity)
        def _(parity=parity):
            for t in range(27):
                da, k = divmod(t, 9)
                row = t * C
                while row < (t + 1) * C:
                    block = row // size
                    end = min((block + 1) * size, (t + 1) * C)
                    at = pl.ds(da * C + row - t * C, end - row)
                    v = acc[at, pl.ds(k * C, C)]
                    if k % 3 != 1:
                        v = v + more[0 if k % 3 == 2 else 1, at, pl.ds(k // 3 * C, C)]
                    ref = keep if block % 2 == parity else send
                    ref[block // 2, pl.ds(row - block * size, end - row), :] = v * (1.0 / VOX)
                    row = end

    if code is send:
        return
    for n in range(keep.shape[0]):
        encode(code, (n, 0), send[n, pl.ds(0, CUT), :])
        encode(code, (n, 1), send[n, pl.ds(CUT, size - CUT), :])


def columns(w, ks):
    return jnp.concatenate([jnp.concatenate([w[d * 9 + k] for k in ks], axis=1) for d in range(3)], axis=0)


def joined(y, p, rows):
    total = y[pl.ds((p + 2) * rows, rows), pl.ds(0, C)]
    total = total + y[pl.ds((p + 1) * rows, rows), pl.ds(C, C)]
    return total + y[pl.ds(p * rows, rows), pl.ds(2 * C, C)]


def dgrad_kernel(j, first, count, mask, w, x, zs, before, out, y, yz, plane, res, sem):
    del before
    y[...] = dot_t(x[j, pl.ds(first * PLANE, (count + 2) * PLANE), :], columns(w, range(9)))
    for n in range(2):
        yz[n] = dot_t(zs[n, j, pl.ds(first * 16, (count + 2) * 16), :], columns(w, (2, 5, 8) if n == 0 else (0, 3, 6)))
    for p in range(count):
        plane[pl.ds(0, PLANE), :] = joined(y, p, PLANE)
        for n in range(2):
            at = pl.ds(11 * n, BSIDE, stride=BSIDE)
            plane[at, :] = plane[at, :] + joined(yz.at[n], p, 16)[:BSIDE]
        m = mask[pl.ds((first + p) * PLANE, PLANE), pl.ds(j * C, C)].astype(F32)
        res[pl.ds(p * PLANE, PLANE), :] = (plane[pl.ds(0, PLANE), :] * m).astype(BF)
    store = pltpu.make_async_copy(res, out.at[j, pl.ds(first * PLANE, count * PLANE)], sem)
    store.start()
    store.wait()


def place():
    s = lax.axis_index("space")
    return s % 2, s // 2 % 2, s // 4


def blocks_kernel(keep, got, send1, keep1, send2, keep2):
    b0, b1, _ = place()
    rows = keep.shape[1]

    def first(i):
        return keep[i, pl.ds(0, CUT), :] + decoded(got, (i, 0), CUT)

    def second(i):
        return keep[i, pl.ds(CUT, rows - CUT), :] + decoded(got, (i, 1), rows - CUT)

    for z1 in range(2):
        for n in range(2):
            i, k = z1 * 4 + n * 2, z1 * 4 + n
            encode(send1, (z1, n), first(i + 1 - b0))
            encode(send2, (z1, n), second(k + 2 - 2 * b1))
            keep1[z1, n] = first(i + b0)
            keep2[z1, n] = second(k + 2 * b1)


def halves_kernel(one, got1, two, got2, send1, keep1, send2, keep2):
    b0, b1, _ = place()
    rest = two.shape[2]
    for z1 in range(2):
        encode(send1, (z1,), one[z1, 1 - b1] + decoded(got1, (z1, 1 - b1), CUT))
        encode(send2, (z1,), two[z1, 1 - b0] + decoded(got2, (z1, 1 - b0), rest))
        keep1[z1] = one[z1, b1] + decoded(got1, (z1, b1), CUT)
        keep2[z1] = two[z1, b0] + decoded(got2, (z1, b0), rest)


def last_kernel(one, got1, two, got2, send, keep):
    b2 = place()[2]
    rest = two.shape[1]
    encode(send, (0,), one[1 - b2] + decoded(got1, (1 - b2,), CUT))
    encode(send, (1,), two[1 - b2] + decoded(got2, (1 - b2,), rest))
    keep[pl.ds(0, CUT), :] = one[b2] + decoded(got1, (b2,), CUT)
    keep[pl.ds(CUT, rest), :] = two[b2] + decoded(got2, (b2,), rest)


def sum_kernel(keep, got, out):
    rest = keep.shape[0] - CUT
    out[pl.ds(0, CUT), :] = keep[pl.ds(0, CUT), :] + decoded(got, (0,), CUT)
    out[pl.ds(CUT, rest), :] = keep[pl.ds(CUT, rest), :] + decoded(got, (1,), rest)


VMEM = pl.BlockSpec(memory_space=pltpu.MemorySpace.VMEM)
SMEM = pl.BlockSpec(memory_space=pltpu.MemorySpace.SMEM)
ANY = pl.BlockSpec(memory_space=pl.ANY)
HBM = pl.BlockSpec(memory_space=pltpu.MemorySpace.HBM)
FIXED = None


def call(kernel, name, ins, outs, scratch=(), aliases=None, flops=0, size=0, limit=4):
    return pl.pallas_call(
        kernel,
        name=name,
        out_shape=[pltpu.VMEM(s, d) if o is FIXED else jax.ShapeDtypeStruct(s, d) for s, d, o in outs],
        in_specs=ins,
        out_specs=[VMEM if o is FIXED else o for _, _, o in outs],
        scratch_shapes=list(scratch),
        input_output_aliases=aliases or {},
        compiler_params=pltpu.CompilerParams(vmem_limit_bytes=limit * 2**20),
        cost_estimate=pl.CostEstimate(flops=flops, transcendentals=0, bytes_accessed=size),
    )


def exchange(value, axis, bit):
    pairs = [(i, i ^ bit) for i in range(lax.axis_size(axis))]
    return lax.ppermute(value, axis, pairs)


def in_hbm(value):
    return pltpu.with_memory_space_constraint(value, pltpu.MemorySpace.HBM)


def tied(*values):
    return lax.optimization_barrier(values)


def reduce_blocks(keep, got, fillers):
    rest = keep.shape[1] - CUT

    def sums(kernel, name, lead, *values):
        code = ((*lead, C, C), jnp.int16, VMEM)
        shapes = [code, ((*lead, CUT, C), F32, VMEM), code, ((*lead, rest, C), F32, VMEM)]
        return call(kernel, name, [VMEM] * len(values), shapes)(*values)

    send1, keep1, send2, keep2 = sums(blocks_kernel, "blocks", (2, 2), keep, got)
    got1, got2 = exchange(send1, "space", 1), exchange(send2, "space", 2)
    got1, got2, fill = tied(got1, got2, fillers[0](None))
    send1, keep1, send2, keep2 = sums(halves_kernel, "halves", (2,), keep1, got1, keep2, got2)
    got1, got2 = exchange(send1, "space", 2), exchange(send2, "space", 1)
    got1, got2, fill = tied(got1, got2, fillers[1](fill))
    send, keep = call(
        last_kernel, "last", [VMEM] * 4, [((2, C, C), jnp.int16, VMEM), ((CUT + rest, C), F32, VMEM)]
    )(keep1, got1, keep2, got2)
    got, fill = tied(exchange(send, "space", 4), fillers[2](fill))
    return call(sum_kernel, "sum", [VMEM] * 2, [((CUT + rest, C), F32, VMEM)])(keep, got)[0], fill


def on_device(features, out_grad, weight, neighbours, active):
    layers = lax.axis_size("space")
    strips, shift, bands = jnp.asarray(strip_matrix()), jnp.asarray(shift_matrix()), jnp.asarray(band_matrix())

    gm, own, mine, mask, strips = call(
        prep_kernel,
        "prep",
        [HBM] * 4,
        [
            ((BSIDE, PLANE, 2 * C), BF, VMEM),
            ((MINE + 208, 2 * C), BF, VMEM),
            ((208, 2 * C), BF, VMEM),
            ((14 * C, 2 * C), BF, VMEM),
            ((64, PLANE), BF, VMEM),
        ],
        [
            pltpu.SMEM((2, 6), jnp.int32),
            pltpu.VMEM((2, VOX), jnp.int32),
            pltpu.VMEM((2, VOX, C), BF),
            pltpu.SemaphoreType.DMA((7,)),
        ],
    )(in_hbm(neighbours), in_hbm(active), in_hbm(strips), in_hbm(out_grad))

    other = exchange(own, "sub", 1)
    pad, fs = call(
        features_kernel,
        "features",
        [VMEM] * 2 + [HBM],
        [((2, (EXT + 2) * PLANE, C), BF, VMEM), ((2, (EXT + 2) * 16, 2 * C), BF, VMEM)],
        [pltpu.VMEM((2, VOX, C), BF), pltpu.SemaphoreType.DMA],
        flops=10**7,
        size=10**6,
    )(mask, strips, in_hbm(features))

    ways = [(2 * i, 2 * i + 2) for i in range(layers - 1)] + [(2 * i + 3, 2 * i + 1) for i in range(layers - 1)]
    got = lax.ppermute(jnp.concatenate([mine, other[MINE:]], axis=0), ("space", "sub"), ways)

    kop_shape = (EXT, KROWS, 2 * C)
    work = 2 * 3 * C * 9 * C * EXT * PLANE
    x, acc = call(
        first_kernel,
        "first",
        [VMEM] * 5,
        [((2, EXT * PLANE, 9 * C), BF, FIXED), ((3 * C, 9 * C), F32, VMEM)],
        [pltpu.VMEM(kop_shape, BF)],
        flops=2 * work,
        size=8 * 2**20,
        limit=6,
    )(shift, gm, own, other, pad)
    got, acc = tied(got, acc)
    got2 = exchange(got, "sub", 1)
    (acc,) = call(
        second_kernel,
        "second",
        [VMEM, VMEM, VMEM],
        [((3 * C, 9 * C), F32, VMEM)],
        flops=work,
        size=4 * 2**20,
    )(pad, x, acc)

    size = 27 * C // (2 * layers)
    custom = layers == 8
    rows = (layers, size, C) if custom else (8, 216, C)
    exact = (rows, F32, VMEM)
    tilt_ins = (own, got, got2, fs, bands, acc)
    tilt_scratch = [pltpu.VMEM((2, EXT * 16, 2 * C), BF), pltpu.VMEM((2, 3 * C, 3 * C), F32)]
    keep, send, zs = call(
        tilt_kernel if custom else (lambda *refs: tilt_kernel(*refs, refs[7])),
        "tilt",
        [VMEM] * 6,
        [
            exact,
            ((layers, 2, C, C), jnp.int16, VMEM) if custom else exact,
            ((2, 2, EXT * 16, 3 * C), BF, VMEM),
        ],
        tilt_scratch + ([pltpu.VMEM(rows, F32)] if custom else []),
        flops=work // 4,
        size=4 * 2**20,
    )(*tilt_ins)

    def dgrad(j, first, count):
        def run(before):
            fresh = before is None
            return call(
                (lambda m, w, x_, z, *refs: dgrad_kernel(j, first, count, m, w, x_, z, None, *refs))
                if fresh
                else (lambda *refs: dgrad_kernel(j, first, count, *refs)),
                "dgrad",
                [VMEM] * 4 + ([] if fresh else [ANY]),
                [((2, VOX, C), BF, ANY)],
                [
                    pltpu.VMEM(((count + 2) * PLANE, 3 * C), F32),
                    pltpu.VMEM((2, (count + 2) * 16, 3 * C), F32),
                    pltpu.VMEM((PLANE + 16, C), F32),
                    pltpu.VMEM((count * PLANE, C), BF),
                    pltpu.SemaphoreType.DMA,
                ],
                aliases={} if fresh else {4: 0},
                flops=work * count // 12,
                size=4 * 2**20,
                limit=10,
            )(mask, weight, x, zs, *(() if fresh else (before,)))[0]

        return run

    if custom:
        got = exchange(send, "sub", 1)
        got, zs = tied(got, zs)
        weight_grad, input_grad = reduce_blocks(keep, got, [dgrad(0, 0, 12), dgrad(1, 0, 6), dgrad(1, 6, 6)])
    else:
        first = lax.axis_index("sub") == 0
        even = jnp.where(first, keep, send)
        odd = jnp.where(first, send, keep)
        kernel_term = jnp.stack([even, odd], axis=1).reshape(27 * C, C)
        weight_grad = lax.psum_scatter(kernel_term, ("space", "sub"), scatter_dimension=0, tiled=True)
        input_grad = dgrad(1, 0, 12)(dgrad(0, 0, 12)(None))
    return input_grad, weight_grad


def solution(mesh):
    in_specs = (
        P(("scene", "space", "sub"), None, None),
        P(("scene", "space", "sub"), None, None),
        P(),
        P(("scene", "space", "sub"), None),
        P(("scene", "space", "sub"), None),
    )
    out_specs = (P(("scene", "space", "sub"), None, None), P(("scene", "space", "sub"), None))
    return jax.shard_map(
        on_device, mesh=mesh, in_specs=in_specs, out_specs=out_specs, check_vma=False
    )
```

```python
import jax
import jax.numpy as jnp
import numpy as np
from jax import lax
from jax.experimental import pallas as pl
from jax.experimental.pallas import tpu as pltpu
from jax.sharding import PartitionSpec as P

BSIDE = 12
PLANE = BSIDE * BSIDE
VOX = BSIDE * PLANE
EXT = BSIDE + 2
C = 128
KROWS = 256
EARLY = 9
MINE = PLANE + 208
BF = jnp.bfloat16
F32 = jnp.float32


def strip_matrix():
    m = np.zeros((64, PLANE), np.float32)
    for i in range(BSIDE):
        m[i, i * BSIDE] = 1
        m[16 + i, i * BSIDE + 11] = 1
        m[32 + i, i] = 1
        m[48 + i, 11 * BSIDE + i] = 1
    m[12, 0] = m[28, 11] = 1
    m[13, 11 * BSIDE] = m[29, 11 * BSIDE + 11] = 1
    return m.astype(jnp.bfloat16)


def shift_matrix():
    m = np.zeros((9, BSIDE, BSIDE, KROWS), np.float32)
    for k in range(9):
        for b in range(BSIDE):
            for c in range(BSIDE):
                sb, sc = b - (k // 3 - 1), c - (k % 3 - 1)
                if sc in (-1, 12):
                    row = {-1: 13, 12: 12}.get(sb, sb) + (176 if sc < 0 else 192)
                elif sb in (-1, 12):
                    row = sc + (144 if sb < 0 else 160)
                else:
                    row = sb * BSIDE + sc
                m[k, b, c, row] = 1
    return m.reshape(9 * PLANE, KROWS).astype(jnp.bfloat16)


def band_matrix():
    m = np.zeros((3, EXT, 16, EXT, 16), np.float32)
    for q in range(3):
        for b in range(BSIDE):
            source = b - (q - 1)
            for p in range(EXT):
                m[q, p, b, p, 13 if source < 0 else source] = 1
    return m.reshape(3 * EXT * 16, EXT * 16).astype(jnp.bfloat16)


def dot(a, b):
    return lax.dot_general(a, b, (((1,), (0,)), ((), ())), preferred_element_type=F32)


def dot_t(a, b):
    return lax.dot_general(a, b, (((1,), (1,)), ((), ())), preferred_element_type=F32)


def halves(x):
    return jnp.concatenate([x[:, C:], x[:, :C]], axis=1)


def per_half(first, second, rows=16):
    lane = lax.broadcasted_iota(jnp.int32, (rows, 2 * C), 1)
    return jnp.where(lane < C, first, second)


def masks(act, out):
    r = lax.broadcasted_iota(jnp.int32, (C, C), 0)
    eye = jnp.where(r == lax.broadcasted_iota(jnp.int32, (C, C), 1), 1.0, 0.0)
    wide = lax.broadcasted_iota(jnp.int32, (2 * C, 2 * C), 0) < C
    ones = jnp.where(wide == (lax.broadcasted_iota(jnp.int32, (2 * C, 2 * C), 1) < C), 1.0, 0.0).astype(BF)
    for n in range(0, VOX, C):
        cols = []
        for j in range(2):
            a = act[pl.ds(j, 1), pl.ds(n, min(C, VOX - n))].astype(F32)
            if n + C > VOX:
                a = jnp.concatenate([a, jnp.zeros((1, n + C - VOX), F32)], axis=1)
            cols.append((eye * a).astype(BF))
        out[pl.ds(n, C), :] = dot(jnp.concatenate(cols, axis=1), ones).astype(BF)


def prep_kernel(nb_hbm, act_hbm, strips_hbm, g_hbm, gm, message, mine, mask, strips, nb, act, g, sem):
    loads = [
        pltpu.make_async_copy(act_hbm, act, sem.at[0]),
        pltpu.make_async_copy(strips_hbm, strips, sem.at[1]),
        pltpu.make_async_copy(nb_hbm, nb, sem.at[2]),
    ]
    for n in range(4):
        rows = pl.ds(n * VOX // 4, VOX // 4)
        loads.append(pltpu.make_async_copy(g_hbm.at[:, rows], g.at[:, rows], sem.at[3 + n]))
    for load in loads:
        load.start()
    loads[0].wait()
    masks(act, mask)
    loads[2].wait()
    a0 = per_half((nb[0, 0] >= 0).astype(F32), (nb[1, 0] >= 0).astype(F32))
    b0 = per_half((nb[0, 2] >= 0).astype(F32), (nb[1, 2] >= 0).astype(F32))
    code = (2 * a0 + b0).astype(BF)
    a0, b0 = a0.astype(BF), b0.astype(BF)
    second = jnp.full((16, 2 * C), lax.axis_index("sub").astype(F32), F32).astype(BF)
    loads[1].wait()
    for p in range(BSIDE):
        if p % 3 == 0:
            loads[3 + p // 3].wait()
        rows = pl.ds(p * PLANE, PLANE)
        plane = jnp.concatenate([g[0, rows, :], g[1, rows, :]], axis=1) * mask[rows, :]
        gm[p] = plane
        s = dot(strips[...], plane).astype(BF)
        mine[pl.ds(p * 16, 16), :] = s[0:16] * second + s[16:32] * (1 - second)
        message[pl.ds(MINE + p * 16, 16), :] = s[16:32] * second + s[0:16] * (1 - second)
        message[pl.ds(PLANE + p * 16, 16), :] = s[32:48] * b0 + s[48:64] * (1 - b0)
    for r in range(0, PLANE, 16):
        message[pl.ds(r, 16), :] = gm[0, pl.ds(r, 16), :] * a0 + gm[11, pl.ds(r, 16), :] * (1 - a0)
    message[pl.ds(PLANE + 192, 16), :] = code
    message[pl.ds(MINE + 192, 16), :] = code
    mine[pl.ds(192, 16), :] = code


def features_kernel(mask, strips, f_hbm, pad, fs, f, sem):
    load = pltpu.make_async_copy(f_hbm, f, sem)
    load.start()
    zero = jnp.zeros((2 * PLANE, C), BF)
    edge = jnp.zeros((32, 2 * C), BF)
    for j in range(2):
        pad[j, pl.ds(0, 2 * PLANE), :] = zero
        pad[j, pl.ds(EXT * PLANE, 2 * PLANE), :] = zero
    load.wait()
    for j in range(2):
        pad[j, pl.ds(2 * PLANE, VOX), :] = f[j] * mask[pl.ds(0, VOX), pl.ds(j * C, C)]
    for n in range(2):
        fs[n, pl.ds(0, 32), :] = edge
        fs[n, pl.ds(EXT * 16, 32), :] = edge
    for p in range(BSIDE):
        rows = pl.ds((p + 2) * PLANE, PLANE)
        s = dot(strips[pl.ds(0, 32), :], jnp.concatenate([pad[0, rows, :], pad[1, rows, :]], axis=1)).astype(BF)
        for n in range(2):
            fs[n, pl.ds((p + 2) * 16, 16), :] = s[16 * n : 16 * n + 16]


def position(own):
    code = own[pl.ds(336, 16), :].astype(F32)
    a0 = jnp.where(code >= 2, 1.0, 0.0)
    b0 = code - 2 * a0
    return code, a0, b0


def candidates(refs, at):
    tiles = []
    for ref, base, swapped in refs:
        t = ref[pl.ds(base + at, 16), :].astype(F32)
        tiles.append(((ref, base, swapped), halves(t) if swapped else t))
    return tiles


def hits(cands, q):
    return [(*source, jnp.where(t == q, 1.0, 0.0).astype(BF)) for source, t in cands]


def gather(picks, row):
    total = None
    for ref, base, swapped, w in picks:
        x = ref[pl.ds(base + row, 16), :]
        x = (halves(x) if swapped else x) * w
        total = x if total is None else total + x
    return total


def layer_operands(gm, own, other, kop):
    code, a0, b0 = position(own)
    layer = candidates([(own, 0, True), (other, 0, False), (other, 0, True)], 336)
    pick_a = hits(layer, code + 2 - 4 * a0)
    pick_b = hits(layer, code + 1 - 2 * b0)
    pick_d = hits(layer, 3 - code)
    a0h, b0h = a0.astype(BF), b0.astype(BF)
    a1h, b1h = 1 - a0h, 1 - b0h
    rest = jnp.zeros((KROWS - 176, 2 * C), BF)
    for p in range(BSIDE):
        kop[p + 1, pl.ds(0, PLANE), :] = gm[p]
        side = gather(pick_b, PLANE + p * 16)
        kop[p + 1, pl.ds(144, 16), :] = side * b0h
        kop[p + 1, pl.ds(160, 16), :] = side * b1h
        kop[p + 1, pl.ds(176, KROWS - 176), :] = rest
    for at, plane, w in ((0, 11, a0h), (EXT - 1, 0, a1h)):
        for r in range(0, PLANE, 16):
            kop[at, pl.ds(r, 16), :] = gather(pick_a, r) * w
        side = gather(pick_d, PLANE + plane * 16) * w
        kop[at, pl.ds(144, 16), :] = side * b0h
        kop[at, pl.ds(160, 16), :] = side * b1h
        kop[at, pl.ds(176, KROWS - 176), :] = rest


def vertical_operands(own, zs, z):
    code, a0, b0 = position(own)
    row16 = lax.broadcasted_iota(jnp.int32, (16, 2 * C), 0)
    inner = jnp.where(row16 < 12, 1.0, 0.0).astype(BF)
    edge = jnp.where(row16 == 12, 1 - b0, jnp.where(row16 == 13, b0, 0.0)).astype(BF)
    a0h = a0.astype(BF)
    for n, ref in enumerate(zs):
        cands = candidates([(ref, base, swapped) for base in (0, 208) for swapped in (False, True)], 192)
        near = [(*q, w * inner) for *q, w in hits(cands, code)]
        near += [(*q, w * edge) for *q, w in hits(cands, code + 1 - 2 * b0)]
        far = [(*q, w * inner) for *q, w in hits(cands, code + 2 - 4 * a0)]
        far += [(*q, w * edge) for *q, w in hits(cands, 3 - code)]
        for p in range(BSIDE):
            z[n, pl.ds((p + 1) * 16, 16), :] = gather(near, p * 16)
        z[n, pl.ds(0, 16), :] = gather(far, 11 * 16) * a0h
        z[n, pl.ds((EXT - 1) * 16, 16), :] = gather(far, 0) * (1 - a0h)


def shifted(shift, kop, x, ks, first, count):
    for p in range(count):
        for n, k in enumerate(ks):
            if k == 4:
                y = kop[first + p, pl.ds(0, PLANE), :]
            else:
                y = dot(shift[pl.ds(k * PLANE, PLANE), :], kop[first + p]).astype(BF)
            for j in range(2):
                x[j, pl.ds(p * PLANE, PLANE), pl.ds(n * C, C)] = y[:, j * C : j * C + C]


def stacked(ref, j, first, count):
    return jnp.concatenate([ref[j, pl.ds((d + first) * PLANE, count * PLANE), :] for d in range(3)], axis=1)


def dot_rows(a, b):
    return lax.dot_general(a, b, (((0,), (0,)), ((), ())), preferred_element_type=F32)


def first_kernel(shift, gm, own, other, pad, x, acc, kop):
    layer_operands(gm, own, other, kop)
    shifted(shift, kop, x, range(9), 0, EXT)
    acc[...] = dot_rows(stacked(pad, 0, 0, EXT), x[0])
    acc[...] += dot_rows(stacked(pad, 1, 0, EARLY), x[1, pl.ds(0, EARLY * PLANE), :])


def second_kernel(pad, x, before, acc):
    late = EXT - EARLY
    acc[...] = before[...] + dot_rows(stacked(pad, 1, EARLY, late), x[1, pl.ds(EARLY * PLANE, late * PLANE), :])


def encode(ref, at, v):
    top = jnp.maximum(jnp.max(jnp.abs(v), axis=0, keepdims=True), 1e-33)
    e = jnp.floor(jnp.log2(top)) - 14
    q = jnp.clip(jnp.round(v * jnp.exp2(-e)), -32767, 32767)
    ref[at] = jnp.concatenate([q, jnp.broadcast_to(e, (8, C))], axis=0).astype(jnp.int32).astype(jnp.int16)


def decoded(ref, at):
    v = ref[at].astype(jnp.int32).astype(F32)
    rows = v.shape[0] - 8
    return v[:rows] * jnp.exp2(v[rows : rows + 1])


def tilt_kernel(own, got, got2, fs, bands, acc, keep, code, zs, z, more, send):
    sub = lax.axis_index("sub")
    for parity in range(2):

        @pl.when(sub == parity)
        def _(parity=parity):
            vertical_operands(own, (got2, got) if parity else (got, got2), z)

    for n in range(2):
        v = dot(bands[...], z[n]).astype(BF)
        rows = EXT * 16
        total = None
        for j in range(2):
            lanes = slice(j * C, j * C + C)
            zs[n, j] = jnp.concatenate([v[q * rows : q * rows + rows, lanes] for q in range(3)], axis=1)
            f3 = jnp.concatenate([fs[n, pl.ds(d * 16, rows), lanes] for d in range(3)], axis=1)
            part_ = dot_rows(f3, zs[n, j])
            total = part_ if total is None else total + part_
        more[n] = total
    size = keep.shape[1]
    for parity in range(2):

        @pl.when(sub == parity)
        def _(parity=parity):
            for t in range(27):
                da, k = divmod(t, 9)
                row = t * C
                while row < (t + 1) * C:
                    block = row // size
                    end = min((block + 1) * size, (t + 1) * C)
                    at = pl.ds(da * C + row - t * C, end - row)
                    v = acc[at, pl.ds(k * C, C)]
                    if k % 3 != 1:
                        v = v + more[0 if k % 3 == 2 else 1, at, pl.ds(k // 3 * C, C)]
                    ref = keep if block % 2 == parity else send
                    ref[block // 2, pl.ds(row - block * size, end - row), :] = v * (1.0 / VOX)
                    row = end

    if code is send:
        return
    for n in range(keep.shape[0]):
        encode(code, n, send[n])


def columns(w, ks):
    return jnp.concatenate([jnp.concatenate([w[d * 9 + k] for k in ks], axis=1) for d in range(3)], axis=0)


def joined(y, p, rows):
    total = y[pl.ds((p + 2) * rows, rows), pl.ds(0, C)]
    total = total + y[pl.ds((p + 1) * rows, rows), pl.ds(C, C)]
    return total + y[pl.ds(p * rows, rows), pl.ds(2 * C, C)]


def dgrad_kernel(pieces, mask, w, x, zs, before, out, y, yz, plane, res, sem):
    del before
    stores = []
    for j, first, count in pieces:
        rows = pl.ds(0, (count + 2) * PLANE)
        y[rows, :] = dot_t(x[j, pl.ds(first * PLANE, (count + 2) * PLANE), :], columns(w, range(9)))
        for n in range(2):
            faces = dot_t(zs[n, j, pl.ds(first * 16, (count + 2) * 16), :], columns(w, (2, 5, 8) if n == 0 else (0, 3, 6)))
            yz[n, pl.ds(0, (count + 2) * 16), :] = faces
        for p in range(count):
            plane[pl.ds(0, PLANE), :] = joined(y, p, PLANE)
            for n in range(2):
                at = pl.ds(11 * n, BSIDE, stride=BSIDE)
                plane[at, :] = plane[at, :] + joined(yz.at[n], p, 16)[:BSIDE]
            m = mask[pl.ds((first + p) * PLANE, PLANE), pl.ds(j * C, C)].astype(F32)
            at = pl.ds((first + p) * PLANE, PLANE)
            res[j, at, :] = (plane[pl.ds(0, PLANE), :] * m).astype(BF)
            if p % 2 == 1:
                at = pl.ds((first + p - 1) * PLANE, 2 * PLANE)
                stores.append(pltpu.make_async_copy(res.at[j, at], out.at[j, at], sem.at[len(stores)]))
                stores[-1].start()
    for store in stores:
        store.wait()


def place():
    s = lax.axis_index("space")
    return s % 2, s // 2 % 2, s // 4


def blocks_kernel(keep, got, send_y, send_z, send_yz, own):
    y, z, _ = place()
    for high in range(2):
        for ref, to_y, to_z in ((send_y, 1 - y, z), (send_z, y, 1 - z), (send_yz, 1 - y, 1 - z)):
            n = high * 4 + to_z * 2 + to_y
            encode(ref, high, keep[n] + decoded(got, n))
        n = high * 4 + z * 2 + y
        own[high] = keep[n] + decoded(got, n)


def last_kernel(own, got_y, got_z, got_yz, send, keep):
    high = place()[2]

    def total(n):
        return own[n] + decoded(got_y, n) + decoded(got_z, n) + decoded(got_yz, n)

    encode(send, Ellipsis, total(1 - high))
    keep[...] = total(high)


def sum_kernel(keep, got, out):
    out[...] = keep[...] + decoded(got, Ellipsis)


VMEM = pl.BlockSpec(memory_space=pltpu.MemorySpace.VMEM)
SMEM = pl.BlockSpec(memory_space=pltpu.MemorySpace.SMEM)
ANY = pl.BlockSpec(memory_space=pl.ANY)
HBM = pl.BlockSpec(memory_space=pltpu.MemorySpace.HBM)
FIXED = None


def call(kernel, name, ins, outs, scratch=(), aliases=None, flops=0, size=0, limit=4):
    return pl.pallas_call(
        kernel,
        name=name,
        out_shape=[pltpu.VMEM(s, d) if o is FIXED else jax.ShapeDtypeStruct(s, d) for s, d, o in outs],
        in_specs=ins,
        out_specs=[VMEM if o is FIXED else o for _, _, o in outs],
        scratch_shapes=list(scratch),
        input_output_aliases=aliases or {},
        compiler_params=pltpu.CompilerParams(vmem_limit_bytes=limit * 2**20),
        cost_estimate=pl.CostEstimate(flops=flops, transcendentals=0, bytes_accessed=size),
    )


def exchange(value, axis, bit):
    pairs = [(i, i ^ bit) for i in range(lax.axis_size(axis))]
    return lax.ppermute(value, axis, pairs)


def in_hbm(value):
    return pltpu.with_memory_space_constraint(value, pltpu.MemorySpace.HBM)


def tied(*values):
    return lax.optimization_barrier(values)


def reduce_blocks(keep, got, fillers):
    rows = keep.shape[1]
    code = (rows + 8, C)
    *sends, own = call(blocks_kernel, "blocks", [VMEM] * 2, [((2, *code), jnp.int16, VMEM)] * 3 + [((2, rows, C), F32, VMEM)])(keep, got)
    gots = [exchange(send, "space", bit) for bit, send in enumerate(sends, 1)]
    *gots, fill = tied(*gots, fillers[0](None))
    send, keep = call(last_kernel, "last", [VMEM] * 4, [(code, jnp.int16, VMEM), ((rows, C), F32, VMEM)])(own, *gots)
    got, fill = tied(exchange(send, "space", 4), fillers[1](fill))
    return call(sum_kernel, "sum", [VMEM] * 2, [((rows, C), F32, VMEM)])(keep, got)[0], fill


def on_device(features, out_grad, weight, neighbours, active):
    layers = lax.axis_size("space")
    strips, shift, bands = jnp.asarray(strip_matrix()), jnp.asarray(shift_matrix()), jnp.asarray(band_matrix())

    gm, own, mine, mask, strips = call(
        prep_kernel,
        "prep",
        [HBM] * 4,
        [
            ((BSIDE, PLANE, 2 * C), BF, VMEM),
            ((MINE + 208, 2 * C), BF, VMEM),
            ((208, 2 * C), BF, VMEM),
            ((14 * C, 2 * C), BF, VMEM),
            ((64, PLANE), BF, VMEM),
        ],
        [
            pltpu.SMEM((2, 6), jnp.int32),
            pltpu.VMEM((2, VOX), jnp.int32),
            pltpu.VMEM((2, VOX, C), BF),
            pltpu.SemaphoreType.DMA((7,)),
        ],
    )(in_hbm(neighbours), in_hbm(active), in_hbm(strips), in_hbm(out_grad))

    other = exchange(own, "sub", 1)
    pad, fs = call(
        features_kernel,
        "features",
        [VMEM] * 2 + [HBM],
        [((2, (EXT + 2) * PLANE, C), BF, VMEM), ((2, (EXT + 2) * 16, 2 * C), BF, VMEM)],
        [pltpu.VMEM((2, VOX, C), BF), pltpu.SemaphoreType.DMA],
        flops=10**7,
        size=10**6,
    )(mask, strips, in_hbm(features))

    ways = [(2 * i, 2 * i + 2) for i in range(layers - 1)] + [(2 * i + 3, 2 * i + 1) for i in range(layers - 1)]
    got = lax.ppermute(jnp.concatenate([mine, other[MINE:]], axis=0), ("space", "sub"), ways)

    kop_shape = (EXT, KROWS, 2 * C)
    work = 2 * 3 * C * 9 * C * EXT * PLANE
    x, acc = call(
        first_kernel,
        "first",
        [VMEM] * 5,
        [((2, EXT * PLANE, 9 * C), BF, FIXED), ((3 * C, 9 * C), F32, VMEM)],
        [pltpu.VMEM(kop_shape, BF)],
        flops=2 * work,
        size=8 * 2**20,
        limit=6,
    )(shift, gm, own, other, pad)
    got, acc = tied(got, acc)
    got2 = exchange(got, "sub", 1)
    (acc,) = call(
        second_kernel,
        "second",
        [VMEM, VMEM, VMEM],
        [((3 * C, 9 * C), F32, VMEM)],
        flops=work,
        size=4 * 2**20,
    )(pad, x, acc)

    size = 27 * C // (2 * layers)
    custom = layers == 8
    rows = (layers, size, C) if custom else (8, 216, C)
    exact = (rows, F32, VMEM)
    tilt_ins = (own, got, got2, fs, bands, acc)
    tilt_scratch = [pltpu.VMEM((2, EXT * 16, 2 * C), BF), pltpu.VMEM((2, 3 * C, 3 * C), F32)]
    keep, send, zs = call(
        tilt_kernel if custom else (lambda *refs: tilt_kernel(*refs, refs[7])),
        "tilt",
        [VMEM] * 6,
        [
            exact,
            ((layers, size + 8, C), jnp.int16, VMEM) if custom else exact,
            ((2, 2, EXT * 16, 3 * C), BF, VMEM),
        ],
        tilt_scratch + ([pltpu.VMEM(rows, F32)] if custom else []),
        flops=work // 4,
        size=4 * 2**20,
    )(*tilt_ins)

    def dgrad(*pieces):
        most = max(count for _, _, count in pieces) + 2

        def run(before):
            fresh = before is None
            return call(
                (lambda m, w, x_, z, *refs: dgrad_kernel(pieces, m, w, x_, z, None, *refs))
                if fresh
                else (lambda *refs: dgrad_kernel(pieces, *refs)),
                "dgrad",
                [VMEM] * 4 + ([] if fresh else [ANY]),
                [((2, VOX, C), BF, ANY)],
                [
                    pltpu.VMEM((most * PLANE, 3 * C), F32),
                    pltpu.VMEM((2, most * 16, 3 * C), F32),
                    pltpu.VMEM((PLANE + 16, C), F32),
                    pltpu.VMEM((2, VOX, C), BF),
                    pltpu.SemaphoreType.DMA((12,)),
                ],
                aliases={} if fresh else {4: 0},
                flops=work * sum(count for _, _, count in pieces) // 12,
                size=4 * 2**20,
                limit=12,
            )(mask, weight, x, zs, *(() if fresh else (before,)))[0]

        return run

    if custom:
        got = exchange(send, "sub", 1)
        got, zs = tied(got, zs)
        weight_grad, input_grad = reduce_blocks(keep, got, [dgrad((0, 0, 12), (1, 0, 4)), dgrad((1, 4, 8))])
    else:
        first = lax.axis_index("sub") == 0
        even = jnp.where(first, keep, send)
        odd = jnp.where(first, send, keep)
        kernel_term = jnp.stack([even, odd], axis=1).reshape(27 * C, C)
        weight_grad = lax.psum_scatter(kernel_term, ("space", "sub"), scatter_dimension=0, tiled=True)
        input_grad = dgrad((0, 0, 12), (1, 0, 12))(None)
    return input_grad, weight_grad


def solution(mesh):
    in_specs = (
        P(("scene", "space", "sub"), None, None),
        P(("scene", "space", "sub"), None, None),
        P(),
        P(("scene", "space", "sub"), None),
        P(("scene", "space", "sub"), None),
    )
    out_specs = (P(("scene", "space", "sub"), None, None), P(("scene", "space", "sub"), None))
    return jax.shard_map(
        on_device, mesh=mesh, in_specs=in_specs, out_specs=out_specs, check_vma=False
    )
```

```python
import jax
import jax.numpy as jnp
import numpy as np
from jax import lax
from jax.experimental import pallas as pl
from jax.experimental.pallas import tpu as pltpu
from jax.sharding import PartitionSpec as P

BSIDE = 12
PLANE = BSIDE * BSIDE
VOX = BSIDE * PLANE
EXT = BSIDE + 2
C = 128
KROWS = 256
MINE = PLANE + 208
BF = jnp.bfloat16
F32 = jnp.float32


def strip_matrix():
    m = np.zeros((64, PLANE), np.float32)
    for i in range(BSIDE):
        m[i, i * BSIDE] = 1
        m[16 + i, i * BSIDE + 11] = 1
        m[32 + i, i] = 1
        m[48 + i, 11 * BSIDE + i] = 1
    m[12, 0] = m[28, 11] = 1
    m[13, 11 * BSIDE] = m[29, 11 * BSIDE + 11] = 1
    return m.astype(jnp.bfloat16)


def shift_matrix():
    m = np.zeros((9, BSIDE, BSIDE, KROWS), np.float32)
    for k in range(9):
        for b in range(BSIDE):
            for c in range(BSIDE):
                sb, sc = b - (k // 3 - 1), c - (k % 3 - 1)
                if sc in (-1, 12):
                    row = {-1: 13, 12: 12}.get(sb, sb) + (176 if sc < 0 else 192)
                elif sb in (-1, 12):
                    row = sc + (144 if sb < 0 else 160)
                else:
                    row = sb * BSIDE + sc
                m[k, b, c, row] = 1
    return m.reshape(9 * PLANE, KROWS).astype(jnp.bfloat16)


def band_matrix():
    m = np.zeros((3, EXT, 16, EXT, 16), np.float32)
    for q in range(3):
        for b in range(BSIDE):
            source = b - (q - 1)
            for p in range(EXT):
                m[q, p, b, p, 13 if source < 0 else source] = 1
    return m.reshape(3 * EXT * 16, EXT * 16).astype(jnp.bfloat16)


def dot(a, b):
    return lax.dot_general(a, b, (((1,), (0,)), ((), ())), preferred_element_type=F32)


def dot_t(a, b):
    return lax.dot_general(a, b, (((1,), (1,)), ((), ())), preferred_element_type=F32)


def halves(x):
    return jnp.concatenate([x[:, C:], x[:, :C]], axis=1)


def per_half(first, second, rows=16):
    lane = lax.broadcasted_iota(jnp.int32, (rows, 2 * C), 1)
    return jnp.where(lane < C, first, second)


def masks(act, out):
    r = lax.broadcasted_iota(jnp.int32, (C, C), 0)
    eye = jnp.where(r == lax.broadcasted_iota(jnp.int32, (C, C), 1), 1.0, 0.0)
    wide = lax.broadcasted_iota(jnp.int32, (2 * C, 2 * C), 0) < C
    ones = jnp.where(wide == (lax.broadcasted_iota(jnp.int32, (2 * C, 2 * C), 1) < C), 1.0, 0.0).astype(BF)
    for n in range(0, VOX, C):
        cols = []
        for j in range(2):
            a = act[pl.ds(j, 1), pl.ds(n, min(C, VOX - n))].astype(F32)
            if n + C > VOX:
                a = jnp.concatenate([a, jnp.zeros((1, n + C - VOX), F32)], axis=1)
            cols.append((eye * a).astype(BF))
        out[pl.ds(n, C), :] = dot(jnp.concatenate(cols, axis=1), ones).astype(BF)


def prep_kernel(nb_hbm, act_hbm, strips_hbm, g_hbm, gm, message, mine, mask, strips, nb, act, g, sem):
    loads = [
        pltpu.make_async_copy(act_hbm, act, sem.at[0]),
        pltpu.make_async_copy(strips_hbm, strips, sem.at[1]),
        pltpu.make_async_copy(nb_hbm, nb, sem.at[2]),
    ]
    for n in range(4):
        rows = pl.ds(n * VOX // 4, VOX // 4)
        loads.append(pltpu.make_async_copy(g_hbm.at[:, rows], g.at[:, rows], sem.at[3 + n]))
    for load in loads:
        load.start()
    loads[0].wait()
    masks(act, mask)
    loads[2].wait()
    a0 = per_half((nb[0, 0] >= 0).astype(F32), (nb[1, 0] >= 0).astype(F32))
    b0 = per_half((nb[0, 2] >= 0).astype(F32), (nb[1, 2] >= 0).astype(F32))
    code = (2 * a0 + b0).astype(BF)
    a0, b0 = a0.astype(BF), b0.astype(BF)
    second = jnp.full((16, 2 * C), lax.axis_index("sub").astype(F32), F32).astype(BF)
    row14 = jnp.where(lax.broadcasted_iota(jnp.int32, (16, 2 * C), 0) == 14, 1.0, 0.0).astype(BF)
    loads[1].wait()
    for p in range(BSIDE):
        if p % 3 == 0:
            loads[3 + p // 3].wait()
        rows = pl.ds(p * PLANE, PLANE)
        plane = jnp.concatenate([g[0, rows, :], g[1, rows, :]], axis=1) * mask[rows, :]
        gm[p] = plane
        s = dot(strips[...], plane).astype(BF)
        here, there = s[0:16] * second + s[16:32] * (1 - second), s[16:32] * second + s[0:16] * (1 - second)
        if p == 0:
            here, there = here + code * row14, there + code * row14
        mine[pl.ds(p * 16, 16), :] = here
        message[pl.ds(MINE + p * 16, 16), :] = there
        message[pl.ds(PLANE + p * 16, 16), :] = s[32:48] * b0 + s[48:64] * (1 - b0)
    for r in range(0, PLANE, 16):
        message[pl.ds(r, 16), :] = gm[0, pl.ds(r, 16), :] * a0 + gm[11, pl.ds(r, 16), :] * (1 - a0)
    message[pl.ds(PLANE + 192, 16), :] = code


def features_kernel(mask, strips, f_hbm, pad, strip, strip_send, f, sem):
    load = pltpu.make_async_copy(f_hbm, f, sem)
    load.start()
    zero = jnp.zeros((2 * PLANE, C), BF)
    edge = jnp.zeros((32, 2 * C), BF)
    second = jnp.full((16, 2 * C), lax.axis_index("sub").astype(F32), F32).astype(BF)
    for j in range(2):
        pad[j, pl.ds(0, 2 * PLANE), :] = zero
        pad[j, pl.ds(EXT * PLANE, 2 * PLANE), :] = zero
    for ref in (strip, strip_send):
        ref[pl.ds(0, 32), :] = edge
        ref[pl.ds(EXT * 16, 32), :] = edge
    load.wait()
    for j in range(2):
        pad[j, pl.ds(2 * PLANE, VOX), :] = f[j] * mask[pl.ds(0, VOX), pl.ds(j * C, C)]
    for p in range(BSIDE):
        rows = pl.ds((p + 2) * PLANE, PLANE)
        s = dot(strips[pl.ds(0, 32), :], jnp.concatenate([pad[0, rows, :], pad[1, rows, :]], axis=1)).astype(BF)
        strip[pl.ds((p + 2) * 16, 16), :] = s[0:16] * (1 - second) + s[16:32] * second
        strip_send[pl.ds((p + 2) * 16, 16), :] = s[0:16] * second + s[16:32] * (1 - second)


def position(own):
    code = own[pl.ds(336, 16), :].astype(F32)
    a0 = jnp.where(code >= 2, 1.0, 0.0)
    b0 = code - 2 * a0
    return code, a0, b0


def candidates(refs, at):
    tiles = []
    for ref, base, swapped in refs:
        t = ref[pl.ds(base + at // 16 * 16, 16), :].astype(F32)
        t = jnp.broadcast_to(t[at % 16 : at % 16 + 1], (16, 2 * C))
        tiles.append(((ref, base, swapped), halves(t) if swapped else t))
    return tiles


def hits(cands, q):
    return [(*source, jnp.where(t == q, 1.0, 0.0).astype(BF)) for source, t in cands]


def gather(picks, row):
    total = None
    for ref, base, swapped, w in picks:
        x = ref[pl.ds(base + row, 16), :]
        x = (halves(x) if swapped else x) * w
        total = x if total is None else total + x
    return total


def layer_operands(gm, own, other, kop):
    code, a0, b0 = position(own)
    layer = candidates([(own, 0, True), (other, 0, False), (other, 0, True)], 336)
    pick_a = hits(layer, code + 2 - 4 * a0)
    pick_b = hits(layer, code + 1 - 2 * b0)
    pick_d = hits(layer, 3 - code)
    a0h, b0h = a0.astype(BF), b0.astype(BF)
    a1h, b1h = 1 - a0h, 1 - b0h
    rest = jnp.zeros((KROWS - 176, 2 * C), BF)
    for p in range(BSIDE):
        kop[p + 1, pl.ds(0, PLANE), :] = gm[p]
        side = gather(pick_b, PLANE + p * 16)
        kop[p + 1, pl.ds(144, 16), :] = side * b0h
        kop[p + 1, pl.ds(160, 16), :] = side * b1h
        kop[p + 1, pl.ds(176, KROWS - 176), :] = rest
    for r in range(0, PLANE, 16):
        kop[0, pl.ds(r, 16), :] = gather(pick_a, r)
    side = gather(pick_d, PLANE + 176) * a0h + gather(pick_d, PLANE) * a1h
    kop[0, pl.ds(144, 16), :] = side * b0h
    kop[0, pl.ds(160, 16), :] = side * b1h
    kop[0, pl.ds(176, KROWS - 176), :] = rest
    return a0h, a1h


def facing_plane(message, got, z):
    code, a0, b0 = position(message)
    row16 = lax.broadcasted_iota(jnp.int32, (16, 2 * C), 0)
    inner = jnp.where(row16 < 12, 1.0, 0.0).astype(BF)
    edge = jnp.where(row16 == 12, 1 - b0, jnp.where(row16 == 13, b0, 0.0)).astype(BF)
    a0h = a0.astype(BF)
    cands = candidates([(got, base, swapped) for base in (0, 192) for swapped in (False, True)], 14)
    near = [(*q, w * inner) for *q, w in hits(cands, code)]
    near += [(*q, w * edge) for *q, w in hits(cands, code + 1 - 2 * b0)]
    far = [(*q, w * inner) for *q, w in hits(cands, code + 2 - 4 * a0)]
    far += [(*q, w * edge) for *q, w in hits(cands, 3 - code)]
    for p in range(BSIDE):
        z[pl.ds((p + 1) * 16, 16), :] = gather(near, p * 16)
    z[pl.ds(0, 16), :] = gather(far, 11 * 16) * a0h
    z[pl.ds((EXT - 1) * 16, 16), :] = gather(far, 0) * (1 - a0h)


def shifted(shift, kop, x, ends):
    for p in range(EXT - 1):
        for k in range(9):
            if k == 4:
                y = kop[p, pl.ds(0, PLANE), :]
            else:
                y = dot(shift[pl.ds(k * PLANE, PLANE), :], kop[p]).astype(BF)
            for at in (p,) if p else (0, EXT - 1):
                v = y if p else y * ends[1 if at else 0]
                for j in range(2):
                    x[j, pl.ds(at * PLANE, PLANE), pl.ds(k * C, C)] = v[:, j * C : j * C + C]


def stacked(ref, j):
    return jnp.concatenate([ref[j, pl.ds(d * PLANE, EXT * PLANE), :] for d in range(3)], axis=1)


def dot_rows(a, b):
    return lax.dot_general(a, b, (((0,), (0,)), ((), ())), preferred_element_type=F32)


def first_kernel(shift, gm, own, other, pad, x, acc, kop):
    ends = [jnp.concatenate([w] * (PLANE // 16), axis=0) for w in layer_operands(gm, own, other, kop)]
    shifted(shift, kop, x, ends)
    acc[...] = dot_rows(stacked(pad, 0), x[0])
    acc[...] += dot_rows(stacked(pad, 1), x[1])


def encode(ref, at, v):
    top = jnp.maximum(jnp.max(jnp.abs(v), axis=0, keepdims=True), 1e-33)
    e = jnp.floor(jnp.log2(top)) - 14
    q = jnp.clip(jnp.round(v * jnp.exp2(-e)), -32767, 32767)
    ref[at] = jnp.concatenate([q, jnp.broadcast_to(e, (8, C))], axis=0).astype(jnp.int32).astype(jnp.int16)


def decoded(ref, at):
    v = ref[at].astype(jnp.int32).astype(F32)
    rows = v.shape[0] - 8
    return v[:rows] * jnp.exp2(v[rows : rows + 1])


def tilt_kernel(own, other, got, strip, strip_other, bands, acc, keep, code, zs, zs_send, z, more, send):
    sub = lax.axis_index("sub")
    rows = EXT * 16
    total = None
    for n, (message, features, out) in enumerate(((own, strip, zs), (other, strip_other, zs_send))):
        facing_plane(message, got, z.at[n])
        v = dot(bands[...], z[n]).astype(BF)
        for j in range(2):
            lanes = slice(j * C, j * C + C)
            out[j] = jnp.concatenate([v[q * rows : q * rows + rows, lanes] for q in range(3)], axis=1)
            f3 = jnp.concatenate([features[pl.ds(d * 16, rows), lanes] for d in range(3)], axis=1)
            term = dot_rows(f3, out[j])
            total = term if total is None else total + term
    more[...] = total
    size = keep.shape[1]
    for parity in range(2):

        @pl.when(sub == parity)
        def _(parity=parity):
            for t in range(27):
                da, k = divmod(t, 9)
                row = t * C
                while row < (t + 1) * C:
                    block = row // size
                    end = min((block + 1) * size, (t + 1) * C)
                    at = pl.ds(da * C + row - t * C, end - row)
                    v = acc[at, pl.ds(k * C, C)]
                    if k % 3 == 2 - 2 * parity:
                        v = v + more[at, pl.ds(k // 3 * C, C)]
                    ref = keep if block % 2 == parity else send
                    ref[block // 2, pl.ds(row - block * size, end - row), :] = v * (1.0 / VOX)
                    row = end

    if code is send:
        return
    for n in range(keep.shape[0]):
        encode(code, n, send[n])


def columns(w, ks):
    return jnp.concatenate([jnp.concatenate([w[d * 9 + k] for k in ks], axis=1) for d in range(3)], axis=0)


def joined(y, p, rows):
    total = y[pl.ds((p + 2) * rows, rows), pl.ds(0, C)]
    total = total + y[pl.ds((p + 1) * rows, rows), pl.ds(C, C)]
    return total + y[pl.ds(p * rows, rows), pl.ds(2 * C, C)]


def dgrad_kernel(pieces, mask, w, x, zs, zs_got, before, out, y, yz, plane, res, sem):
    del before
    core = lax.axis_index("sub")
    stores = []
    for j, first, count in pieces:
        rows = pl.ds(0, (count + 2) * PLANE)
        y[rows, :] = dot_t(x[j, pl.ds(first * PLANE, (count + 2) * PLANE), :], columns(w, range(9)))
        at = pl.ds(first * 16, (count + 2) * 16)
        for n in range(2):
            faces = jnp.where(core == n, zs[j, at, :], zs_got[j, at, :])
            yz[n, pl.ds(0, (count + 2) * 16), :] = dot_t(faces, columns(w, (2, 5, 8) if n == 0 else (0, 3, 6)))
        for p in range(count):
            plane[pl.ds(0, PLANE), :] = joined(y, p, PLANE)
            for n in range(2):
                at = pl.ds(11 * n, BSIDE, stride=BSIDE)
                plane[at, :] = plane[at, :] + joined(yz.at[n], p, 16)[:BSIDE]
            m = mask[pl.ds((first + p) * PLANE, PLANE), pl.ds(j * C, C)].astype(F32)
            at = pl.ds((first + p) * PLANE, PLANE)
            res[j, at, :] = (plane[pl.ds(0, PLANE), :] * m).astype(BF)
            if p % 2 == 1:
                at = pl.ds((first + p - 1) * PLANE, 2 * PLANE)
                stores.append(pltpu.make_async_copy(res.at[j, at], out.at[j, at], sem.at[len(stores)]))
                stores[-1].start()
    for store in stores:
        store.wait()


def place():
    s = lax.axis_index("space")
    return s % 2, s // 2 % 2, s // 4


def blocks_kernel(keep, got, send_y, send_z, send_yz, own):
    y, z, _ = place()
    for high in range(2):
        for ref, to_y, to_z in ((send_y, 1 - y, z), (send_z, y, 1 - z), (send_yz, 1 - y, 1 - z)):
            n = high * 4 + to_z * 2 + to_y
            encode(ref, high, keep[n] + decoded(got, n))
        n = high * 4 + z * 2 + y
        own[high] = keep[n] + decoded(got, n)


def last_kernel(own, got_y, got_z, got_yz, send, keep):
    high = place()[2]

    def total(n):
        return own[n] + decoded(got_y, n) + decoded(got_z, n) + decoded(got_yz, n)

    encode(send, Ellipsis, total(1 - high))
    keep[...] = total(high)


def sum_kernel(keep, got, out):
    out[...] = keep[...] + decoded(got, Ellipsis)


VMEM = pl.BlockSpec(memory_space=pltpu.MemorySpace.VMEM)
SMEM = pl.BlockSpec(memory_space=pltpu.MemorySpace.SMEM)
ANY = pl.BlockSpec(memory_space=pl.ANY)
HBM = pl.BlockSpec(memory_space=pltpu.MemorySpace.HBM)
FIXED = None


def call(kernel, name, ins, outs, scratch=(), aliases=None, flops=0, size=0, limit=4):
    return pl.pallas_call(
        kernel,
        name=name,
        out_shape=[pltpu.VMEM(s, d) if o is FIXED else jax.ShapeDtypeStruct(s, d) for s, d, o in outs],
        in_specs=ins,
        out_specs=[VMEM if o is FIXED else o for _, _, o in outs],
        scratch_shapes=list(scratch),
        input_output_aliases=aliases or {},
        compiler_params=pltpu.CompilerParams(vmem_limit_bytes=limit * 2**20),
        cost_estimate=pl.CostEstimate(flops=flops, transcendentals=0, bytes_accessed=size),
    )


def exchange(value, axis, bit):
    pairs = [(i, i ^ bit) for i in range(lax.axis_size(axis))]
    return lax.ppermute(value, axis, pairs)


def in_hbm(value):
    return pltpu.with_memory_space_constraint(value, pltpu.MemorySpace.HBM)


def tied(*values):
    return lax.optimization_barrier(values)


def reduce_blocks(keep, got, fillers):
    rows = keep.shape[1]
    code = (rows + 8, C)
    *sends, own = call(blocks_kernel, "blocks", [VMEM] * 2, [((2, *code), jnp.int16, VMEM)] * 3 + [((2, rows, C), F32, VMEM)])(keep, got)
    gots = [exchange(send, "space", bit) for bit, send in enumerate(sends, 1)]
    *gots, fill = tied(*gots, fillers[0](None))
    send, keep = call(last_kernel, "last", [VMEM] * 4, [(code, jnp.int16, VMEM), ((rows, C), F32, VMEM)])(own, *gots)
    got, fill = tied(exchange(send, "space", 4), fillers[1](fill))
    return call(sum_kernel, "sum", [VMEM] * 2, [((rows, C), F32, VMEM)])(keep, got)[0], fill


def on_device(features, out_grad, weight, neighbours, active):
    layers = lax.axis_size("space")
    strips, shift, bands = jnp.asarray(strip_matrix()), jnp.asarray(shift_matrix()), jnp.asarray(band_matrix())

    gm, own, mine, mask, strips = call(
        prep_kernel,
        "prep",
        [HBM] * 4,
        [
            ((BSIDE, PLANE, 2 * C), BF, VMEM),
            ((MINE + 192, 2 * C), BF, VMEM),
            ((192, 2 * C), BF, VMEM),
            ((14 * C, 2 * C), BF, VMEM),
            ((64, PLANE), BF, VMEM),
        ],
        [
            pltpu.SMEM((2, 6), jnp.int32),
            pltpu.VMEM((2, VOX), jnp.int32),
            pltpu.VMEM((2, VOX, C), BF),
            pltpu.SemaphoreType.DMA((7,)),
        ],
    )(in_hbm(neighbours), in_hbm(active), in_hbm(strips), in_hbm(out_grad))

    other = exchange(own, "sub", 1)
    pad, strip, strip_send = call(
        features_kernel,
        "features",
        [VMEM] * 2 + [HBM],
        [((2, (EXT + 2) * PLANE, C), BF, VMEM)] + [(((EXT + 2) * 16, 2 * C), BF, VMEM)] * 2,
        [pltpu.VMEM((2, VOX, C), BF), pltpu.SemaphoreType.DMA],
        flops=10**7,
        size=10**6,
    )(mask, strips, in_hbm(features))

    ways = [(2 * i, 2 * i + 2) for i in range(layers - 1)] + [(2 * i + 3, 2 * i + 1) for i in range(layers - 1)]
    got = lax.ppermute(jnp.concatenate([mine, other[MINE:]], axis=0), ("space", "sub"), ways)

    strip_other = exchange(strip_send, "sub", 1)

    kop_shape = (EXT - 1, KROWS, 2 * C)
    work = 2 * 3 * C * 9 * C * EXT * PLANE
    x, acc = call(
        first_kernel,
        "first",
        [VMEM] * 5,
        [((2, EXT * PLANE, 9 * C), BF, FIXED), ((3 * C, 9 * C), F32, VMEM)],
        [pltpu.VMEM(kop_shape, BF)],
        flops=2 * work,
        size=8 * 2**20,
        limit=6,
    )(shift, gm, own, other, pad)
    size = 27 * C // (2 * layers)
    custom = layers == 8
    rows = (layers, size, C) if custom else (8, 216, C)
    exact = (rows, F32, VMEM)
    tilt_ins = (own, other, got, strip, strip_other, bands, acc)
    tilt_scratch = [pltpu.VMEM((2, EXT * 16, 2 * C), BF), pltpu.VMEM((3 * C, 3 * C), F32)]
    keep, send, zs, zs_send = call(
        tilt_kernel if custom else (lambda *refs: tilt_kernel(*refs, refs[8])),
        "tilt",
        [VMEM] * 7,
        [
            exact,
            ((layers, size + 8, C), jnp.int16, VMEM) if custom else exact,
            ((2, EXT * 16, 3 * C), BF, VMEM),
            ((2, EXT * 16, 3 * C), BF, VMEM),
        ],
        tilt_scratch + ([pltpu.VMEM(rows, F32)] if custom else []),
        flops=work // 4,
        size=4 * 2**20,
    )(*tilt_ins)

    got = exchange(send, "sub", 1) if custom else None
    zs_got = exchange(zs_send, "sub", 1)

    def dgrad(*pieces):
        most = max(count for _, _, count in pieces) + 2

        def run(before):
            fresh = before is None
            return call(
                (lambda *refs: dgrad_kernel(pieces, *refs[:5], None, *refs[5:]))
                if fresh
                else (lambda *refs: dgrad_kernel(pieces, *refs)),
                "dgrad",
                [VMEM] * 5 + ([] if fresh else [ANY]),
                [((2, VOX, C), BF, ANY)],
                [
                    pltpu.VMEM((most * PLANE, 3 * C), F32),
                    pltpu.VMEM((2, most * 16, 3 * C), F32),
                    pltpu.VMEM((PLANE + 16, C), F32),
                    pltpu.VMEM((2, VOX, C), BF),
                    pltpu.SemaphoreType.DMA((12,)),
                ],
                aliases={} if fresh else {5: 0},
                flops=work * sum(count for _, _, count in pieces) // 12,
                size=4 * 2**20,
                limit=12,
            )(mask, weight, x, zs, zs_got, *(() if fresh else (before,)))[0]

        return run

    if custom:
        got, zs = tied(got, zs)
        weight_grad, input_grad = reduce_blocks(keep, got, [dgrad((0, 0, 12), (1, 0, 4)), dgrad((1, 4, 8))])
    else:
        first = lax.axis_index("sub") == 0
        even = jnp.where(first, keep, send)
        odd = jnp.where(first, send, keep)
        kernel_term = jnp.stack([even, odd], axis=1).reshape(27 * C, C)
        weight_grad = lax.psum_scatter(kernel_term, ("space", "sub"), scatter_dimension=0, tiled=True)
        input_grad = dgrad((0, 0, 12), (1, 0, 12))(None)
    return input_grad, weight_grad


def solution(mesh):
    in_specs = (
        P(("scene", "space", "sub"), None, None),
        P(("scene", "space", "sub"), None, None),
        P(),
        P(("scene", "space", "sub"), None),
        P(("scene", "space", "sub"), None),
    )
    out_specs = (P(("scene", "space", "sub"), None, None), P(("scene", "space", "sub"), None))
    return jax.shard_map(
        on_device, mesh=mesh, in_specs=in_specs, out_specs=out_specs, check_vma=False
    )
```

```python
import jax
import jax.numpy as jnp
import numpy as np
from jax import lax
from jax.experimental import pallas as pl
from jax.experimental.pallas import tpu as pltpu
from jax.sharding import PartitionSpec as P

BSIDE = 12
PLANE = BSIDE * BSIDE
VOX = BSIDE * PLANE
EXT = BSIDE + 2
C = 128
KROWS = 256
MINE = PLANE + 208
BF = jnp.bfloat16
F32 = jnp.float32


def strip_matrix():
    m = np.zeros((64, PLANE), np.float32)
    for i in range(BSIDE):
        m[i, i * BSIDE] = 1
        m[16 + i, i * BSIDE + 11] = 1
        m[32 + i, i] = 1
        m[52 + i, 11 * BSIDE + i] = 1
    m[12, 0] = m[28, 11] = 1
    m[13, 11 * BSIDE] = m[29, 11 * BSIDE + 11] = 1
    return m.astype(jnp.bfloat16)


def shift_matrix():
    m = np.zeros((9, BSIDE, BSIDE, KROWS), np.float32)
    for k in range(9):
        for b in range(BSIDE):
            for c in range(BSIDE):
                sb, sc = b - (k // 3 - 1), c - (k % 3 - 1)
                if 0 <= sc < BSIDE:
                    m[k, b, c, 16 + sb * BSIDE + sc] = 1
    return m.reshape(9 * PLANE, KROWS).astype(jnp.bfloat16)


def band_matrix():
    m = np.zeros((3, EXT, 16, EXT, 16), np.float32)
    for q in range(3):
        for b in range(BSIDE):
            source = b - (q - 1)
            for p in range(EXT):
                m[q, p, b, p, 13 if source < 0 else source] = 1
    return m.reshape(3 * EXT * 16, EXT * 16).astype(jnp.bfloat16)


def dot(a, b):
    return lax.dot_general(a, b, (((1,), (0,)), ((), ())), preferred_element_type=F32)


def dot_t(a, b):
    return lax.dot_general(a, b, (((1,), (1,)), ((), ())), preferred_element_type=F32)


def halves(x):
    return jnp.concatenate([x[:, C:], x[:, :C]], axis=1)


def per_half(first, second, rows=16):
    lane = lax.broadcasted_iota(jnp.int32, (rows, 2 * C), 1)
    return jnp.where(lane < C, first, second)


def masks(act, out):
    r = lax.broadcasted_iota(jnp.int32, (C, C), 0)
    eye = jnp.where(r == lax.broadcasted_iota(jnp.int32, (C, C), 1), 1.0, 0.0)
    wide = lax.broadcasted_iota(jnp.int32, (2 * C, 2 * C), 0) < C
    ones = jnp.where(wide == (lax.broadcasted_iota(jnp.int32, (2 * C, 2 * C), 1) < C), 1.0, 0.0).astype(BF)
    for n in range(0, VOX, C):
        cols = []
        for j in range(2):
            a = act[pl.ds(j, 1), pl.ds(n, min(C, VOX - n))].astype(F32)
            if n + C > VOX:
                a = jnp.concatenate([a, jnp.zeros((1, n + C - VOX), F32)], axis=1)
            cols.append((eye * a).astype(BF))
        out[pl.ds(n, C), :] = dot(jnp.concatenate(cols, axis=1), ones).astype(BF)


def prep_kernel(nb_hbm, act_hbm, strips_hbm, g_hbm, gm, message, mine, mask, strips, nb, act, g, sem):
    loads = [
        pltpu.make_async_copy(act_hbm, act, sem.at[0]),
        pltpu.make_async_copy(strips_hbm, strips, sem.at[1]),
        pltpu.make_async_copy(nb_hbm, nb, sem.at[2]),
    ]
    for n in range(4):
        rows = pl.ds(n * VOX // 4, VOX // 4)
        loads.append(pltpu.make_async_copy(g_hbm.at[:, rows], g.at[:, rows], sem.at[3 + n]))
    for load in loads:
        load.start()
    loads[0].wait()
    masks(act, mask)
    loads[2].wait()
    a0 = per_half((nb[0, 0] >= 0).astype(F32), (nb[1, 0] >= 0).astype(F32))
    b0 = per_half((nb[0, 2] >= 0).astype(F32), (nb[1, 2] >= 0).astype(F32))
    code = (2 * a0 + b0).astype(BF)
    a0, b0 = a0.astype(BF), b0.astype(BF)
    second = jnp.full((16, 2 * C), lax.axis_index("sub").astype(F32), F32).astype(BF)
    row14 = jnp.where(lax.broadcasted_iota(jnp.int32, (16, 2 * C), 0) == 14, 1.0, 0.0).astype(BF)
    loads[1].wait()
    for p in range(BSIDE):
        if p % 3 == 0:
            loads[3 + p // 3].wait()
        rows = pl.ds(p * PLANE, PLANE)
        plane = jnp.concatenate([g[0, rows, :], g[1, rows, :]], axis=1) * mask[rows, :]
        gm[p] = plane
        s = dot(strips[...], plane).astype(BF)
        here, there = s[0:16] * second + s[16:32] * (1 - second), s[16:32] * second + s[0:16] * (1 - second)
        if p == 0:
            here, there = here + code * row14, there + code * row14
        mine[pl.ds(p * 16, 16), :] = here
        message[pl.ds(MINE + p * 16, 16), :] = there
        message[pl.ds(PLANE + p * 16, 16), :] = s[32:48] * b0 + s[48:64] * (1 - b0)
    for r in range(0, PLANE, 16):
        message[pl.ds(r, 16), :] = gm[0, pl.ds(r, 16), :] * a0 + gm[11, pl.ds(r, 16), :] * (1 - a0)
    message[pl.ds(PLANE + 192, 16), :] = code


def features_kernel(mask, strips, f_hbm, pad, strip, strip_send, f, sem):
    load = pltpu.make_async_copy(f_hbm, f, sem)
    load.start()
    zero = jnp.zeros((2 * PLANE, C), BF)
    edge = jnp.zeros((32, 2 * C), BF)
    second = jnp.full((16, 2 * C), lax.axis_index("sub").astype(F32), F32).astype(BF)
    for j in range(2):
        pad[j, pl.ds(0, 2 * PLANE), :] = zero
        pad[j, pl.ds(EXT * PLANE, 2 * PLANE), :] = zero
    for ref in (strip, strip_send):
        ref[pl.ds(0, 32), :] = edge
        ref[pl.ds(EXT * 16, 32), :] = edge
    load.wait()
    for j in range(2):
        pad[j, pl.ds(2 * PLANE, VOX), :] = f[j] * mask[pl.ds(0, VOX), pl.ds(j * C, C)]
    for p in range(BSIDE):
        rows = pl.ds((p + 2) * PLANE, PLANE)
        s = dot(strips[pl.ds(0, 32), :], jnp.concatenate([pad[0, rows, :], pad[1, rows, :]], axis=1)).astype(BF)
        strip[pl.ds((p + 2) * 16, 16), :] = s[0:16] * (1 - second) + s[16:32] * second
        strip_send[pl.ds((p + 2) * 16, 16), :] = s[0:16] * second + s[16:32] * (1 - second)


def position(own):
    code = own[pl.ds(336, 16), :].astype(F32)
    a0 = jnp.where(code >= 2, 1.0, 0.0)
    b0 = code - 2 * a0
    return code, a0, b0


def candidates(refs, at):
    tiles = []
    for ref, base, swapped in refs:
        t = ref[pl.ds(base + at // 16 * 16, 16), :].astype(F32)
        t = jnp.broadcast_to(t[at % 16 : at % 16 + 1], (16, 2 * C))
        tiles.append(((ref, base, swapped), halves(t) if swapped else t))
    return tiles


def hits(cands, q):
    return [(*source, jnp.where(t == q, 1.0, 0.0).astype(BF)) for source, t in cands]


def gather(picks, row):
    total = None
    for ref, base, swapped, w in picks:
        x = ref[pl.ds(base + row, 16), :]
        x = (halves(x) if swapped else x) * w
        total = x if total is None else total + x
    return total


def layer_operands(gm, own, other, kop):
    code, a0, b0 = position(own)
    layer = candidates([(own, 0, True), (other, 0, False), (other, 0, True)], 336)
    pick_a = hits(layer, code + 2 - 4 * a0)
    pick_b = hits(layer, code + 1 - 2 * b0)
    pick_d = hits(layer, 3 - code)
    a0h, b0h = a0.astype(BF), b0.astype(BF)
    a1h, b1h = 1 - a0h, 1 - b0h
    rest = jnp.zeros((KROWS - 176, 2 * C), BF)
    for p in range(BSIDE):
        kop[p + 1, pl.ds(16, PLANE), :] = gm[p]
        side = gather(pick_b, PLANE + p * 16)
        kop[p + 1, pl.ds(0, 16), :] = side * b0h
        kop[p + 1, pl.ds(160, 16), :] = side * b1h
        kop[p + 1, pl.ds(176, KROWS - 176), :] = rest
    for r in range(0, PLANE, 16):
        kop[0, pl.ds(16 + r, 16), :] = gather(pick_a, r)
    side = gather(pick_d, PLANE + 176) * a0h + gather(pick_d, PLANE) * a1h
    kop[0, pl.ds(0, 16), :] = side * b0h
    kop[0, pl.ds(160, 16), :] = side * b1h
    kop[0, pl.ds(176, KROWS - 176), :] = rest
    return a0h, a1h


def facing_plane(message, got, z):
    code, a0, b0 = position(message)
    row16 = lax.broadcasted_iota(jnp.int32, (16, 2 * C), 0)
    inner = jnp.where(row16 < 12, 1.0, 0.0).astype(BF)
    edge = jnp.where(row16 == 12, 1 - b0, jnp.where(row16 == 13, b0, 0.0)).astype(BF)
    a0h = a0.astype(BF)
    cands = candidates([(got, base, swapped) for base in (0, 192) for swapped in (False, True)], 14)
    near = [(*q, w * inner) for *q, w in hits(cands, code)]
    near += [(*q, w * edge) for *q, w in hits(cands, code + 1 - 2 * b0)]
    far = [(*q, w * inner) for *q, w in hits(cands, code + 2 - 4 * a0)]
    far += [(*q, w * edge) for *q, w in hits(cands, 3 - code)]
    for p in range(BSIDE):
        z[pl.ds((p + 1) * 16, 16), :] = gather(near, p * 16)
    z[pl.ds(0, 16), :] = gather(far, 11 * 16) * a0h
    z[pl.ds((EXT - 1) * 16, 16), :] = gather(far, 0) * (1 - a0h)


def shifted(shift, kop, x, ends):
    for p in range(EXT - 1):
        for k in range(9):
            if k % 3 == 1:
                y = kop[p, pl.ds(16 - BSIDE * (k // 3 - 1), PLANE), :]
            else:
                y = dot(shift[pl.ds(k * PLANE, PLANE), :], kop[p]).astype(BF)
            for at in (p,) if p else (0, EXT - 1):
                v = y if p else y * ends[1 if at else 0]
                for j in range(2):
                    x[j, pl.ds(at * PLANE, PLANE), pl.ds(k * C, C)] = v[:, j * C : j * C + C]


def stacked(ref, j):
    return jnp.concatenate([ref[j, pl.ds(d * PLANE, EXT * PLANE), :] for d in range(3)], axis=1)


def dot_rows(a, b):
    return lax.dot_general(a, b, (((0,), (0,)), ((), ())), preferred_element_type=F32)


def first_kernel(shift, gm, own, other, pad, x, acc, kop):
    ends = [jnp.concatenate([w] * (PLANE // 16), axis=0) for w in layer_operands(gm, own, other, kop)]
    shifted(shift, kop, x, ends)
    acc[...] = dot_rows(stacked(pad, 0), x[0])
    acc[...] += dot_rows(stacked(pad, 1), x[1])


def encode(ref, at, v):
    top = jnp.maximum(jnp.max(jnp.abs(v), axis=0, keepdims=True), 1e-33)
    e = jnp.floor(jnp.log2(top)) - 14
    q = jnp.clip(jnp.round(v * jnp.exp2(-e)), -32767, 32767)
    ref[at] = jnp.concatenate([q, jnp.broadcast_to(e, (8, C))], axis=0).astype(jnp.int32).astype(jnp.int16)


def decoded(ref, at):
    v = ref[at].astype(jnp.int32).astype(F32)
    rows = v.shape[0] - 8
    return v[:rows] * jnp.exp2(v[rows : rows + 1])


def tilt_kernel(own, other, got, strip, strip_other, bands, acc, keep, code, zs, zs_send, z, more, send):
    sub = lax.axis_index("sub")
    rows = EXT * 16
    total = None
    for n, (message, features, out) in enumerate(((own, strip, zs), (other, strip_other, zs_send))):
        facing_plane(message, got, z.at[n])
        v = dot(bands[...], z[n]).astype(BF)
        for j in range(2):
            lanes = slice(j * C, j * C + C)
            out[j] = jnp.concatenate([v[q * rows : q * rows + rows, lanes] for q in range(3)], axis=1)
            f3 = jnp.concatenate([features[pl.ds(d * 16, rows), lanes] for d in range(3)], axis=1)
            term = dot_rows(f3, out[j])
            total = term if total is None else total + term
    more[...] = total
    size = keep.shape[1]
    for parity in range(2):

        @pl.when(sub == parity)
        def _(parity=parity):
            for t in range(27):
                da, k = divmod(t, 9)
                row = t * C
                while row < (t + 1) * C:
                    block = row // size
                    end = min((block + 1) * size, (t + 1) * C)
                    at = pl.ds(da * C + row - t * C, end - row)
                    v = acc[at, pl.ds(k * C, C)]
                    if k % 3 == 2 - 2 * parity:
                        v = v + more[at, pl.ds(k // 3 * C, C)]
                    ref = keep if block % 2 == parity else send
                    ref[block // 2, pl.ds(row - block * size, end - row), :] = v * (1.0 / VOX)
                    row = end

    if code is send:
        return
    for n in range(keep.shape[0]):
        encode(code, n, send[n])


def columns(w, ks):
    return jnp.concatenate([jnp.concatenate([w[d * 9 + k] for k in ks], axis=1) for d in range(3)], axis=0)


def joined(y, p, rows):
    total = y[pl.ds((p + 2) * rows, rows), pl.ds(0, C)]
    total = total + y[pl.ds((p + 1) * rows, rows), pl.ds(C, C)]
    return total + y[pl.ds(p * rows, rows), pl.ds(2 * C, C)]


def products_kernel(w, x, out):
    out[...] = dot_t(x[1, pl.ds(0, out.shape[0]), :], columns(w, range(9)))


def dgrad_kernel(pieces, mask, w, x, zs, zs_got, ready, before, out, y, yz, plane, res, sem):
    del before
    core = lax.axis_index("sub")
    stores = []
    for j, first, count, done in pieces:
        source = ready if done else y
        if not done:
            rows = pl.ds(0, (count + 2) * PLANE)
            y[rows, :] = dot_t(x[j, pl.ds(first * PLANE, (count + 2) * PLANE), :], columns(w, range(9)))
        at = pl.ds(first * 16, (count + 2) * 16)
        for n in range(2):
            faces = jnp.where(core == n, zs[j, at, :], zs_got[j, at, :])
            yz[n, pl.ds(0, (count + 2) * 16), :] = dot_t(faces, columns(w, (2, 5, 8) if n == 0 else (0, 3, 6)))
        for p in range(count):
            plane[pl.ds(0, PLANE), :] = joined(source, p, PLANE)
            for n in range(2):
                at = pl.ds(11 * n, BSIDE, stride=BSIDE)
                plane[at, :] = plane[at, :] + joined(yz.at[n], p, 16)[:BSIDE]
            m = mask[pl.ds((first + p) * PLANE, PLANE), pl.ds(j * C, C)].astype(F32)
            at = pl.ds((first + p) * PLANE, PLANE)
            res[j, at, :] = (plane[pl.ds(0, PLANE), :] * m).astype(BF)
            if p % 2 == 1:
                at = pl.ds((first + p - 1) * PLANE, 2 * PLANE)
                stores.append(pltpu.make_async_copy(res.at[j, at], out.at[j, at], sem.at[len(stores)]))
                stores[-1].start()
    for store in stores:
        store.wait()


def place():
    s = lax.axis_index("space")
    return s % 2, s // 2 % 2, s // 4


def blocks_kernel(keep, got, send_y, send_z, send_yz, own):
    y, z, _ = place()
    for high in range(2):
        for ref, to_y, to_z in ((send_y, 1 - y, z), (send_z, y, 1 - z), (send_yz, 1 - y, 1 - z)):
            n = high * 4 + to_z * 2 + to_y
            encode(ref, high, keep[n] + decoded(got, n))
        n = high * 4 + z * 2 + y
        own[high] = keep[n] + decoded(got, n)


def last_kernel(own, got_y, got_z, got_yz, send, keep):
    high = place()[2]

    def total(n):
        return own[n] + decoded(got_y, n) + decoded(got_z, n) + decoded(got_yz, n)

    encode(send, Ellipsis, total(1 - high))
    keep[...] = total(high)


def sum_kernel(keep, got, out):
    out[...] = keep[...] + decoded(got, Ellipsis)


VMEM = pl.BlockSpec(memory_space=pltpu.MemorySpace.VMEM)
SMEM = pl.BlockSpec(memory_space=pltpu.MemorySpace.SMEM)
ANY = pl.BlockSpec(memory_space=pl.ANY)
HBM = pl.BlockSpec(memory_space=pltpu.MemorySpace.HBM)
FIXED = None


def call(kernel, name, ins, outs, scratch=(), aliases=None, flops=0, size=0, limit=4):
    return pl.pallas_call(
        kernel,
        name=name,
        out_shape=[pltpu.VMEM(s, d) if o is FIXED else jax.ShapeDtypeStruct(s, d) for s, d, o in outs],
        in_specs=ins,
        out_specs=[VMEM if o is FIXED else o for _, _, o in outs],
        scratch_shapes=list(scratch),
        input_output_aliases=aliases or {},
        compiler_params=pltpu.CompilerParams(vmem_limit_bytes=limit * 2**20),
        cost_estimate=pl.CostEstimate(flops=flops, transcendentals=0, bytes_accessed=size),
    )


def exchange(value, axis, bit):
    pairs = [(i, i ^ bit) for i in range(lax.axis_size(axis))]
    return lax.ppermute(value, axis, pairs)


def in_hbm(value):
    return pltpu.with_memory_space_constraint(value, pltpu.MemorySpace.HBM)


def tied(*values):
    return lax.optimization_barrier(values)


def reduce_blocks(keep, got, fillers):
    rows = keep.shape[1]
    code = (rows + 8, C)
    *sends, own = call(blocks_kernel, "blocks", [VMEM] * 2, [((2, *code), jnp.int16, VMEM)] * 3 + [((2, rows, C), F32, VMEM)])(keep, got)
    gots = [exchange(send, "space", bit) for bit, send in enumerate(sends, 1)]
    *gots, fill = tied(*gots, fillers[0](None))
    send, keep = call(last_kernel, "last", [VMEM] * 4, [(code, jnp.int16, VMEM), ((rows, C), F32, VMEM)])(own, *gots)
    got, fill = tied(exchange(send, "space", 4), fillers[1](fill))
    return call(sum_kernel, "sum", [VMEM] * 2, [((rows, C), F32, VMEM)])(keep, got)[0], fill


def on_device(features, out_grad, weight, neighbours, active):
    layers = lax.axis_size("space")
    strips, shift, bands = jnp.asarray(strip_matrix()), jnp.asarray(shift_matrix()), jnp.asarray(band_matrix())

    gm, own, mine, mask, strips = call(
        prep_kernel,
        "prep",
        [HBM] * 4,
        [
            ((BSIDE, PLANE, 2 * C), BF, VMEM),
            ((MINE + 192, 2 * C), BF, VMEM),
            ((192, 2 * C), BF, VMEM),
            ((14 * C, 2 * C), BF, VMEM),
            ((64, PLANE), BF, VMEM),
        ],
        [
            pltpu.SMEM((2, 6), jnp.int32),
            pltpu.VMEM((2, VOX), jnp.int32),
            pltpu.VMEM((2, VOX, C), BF),
            pltpu.SemaphoreType.DMA((7,)),
        ],
    )(in_hbm(neighbours), in_hbm(active), in_hbm(strips), in_hbm(out_grad))

    other = exchange(own, "sub", 1)
    pad, strip, strip_send = call(
        features_kernel,
        "features",
        [VMEM] * 2 + [HBM],
        [((2, (EXT + 2) * PLANE, C), BF, VMEM)] + [(((EXT + 2) * 16, 2 * C), BF, VMEM)] * 2,
        [pltpu.VMEM((2, VOX, C), BF), pltpu.SemaphoreType.DMA],
        flops=10**7,
        size=10**6,
    )(mask, strips, in_hbm(features))

    ways = [(2 * i, 2 * i + 2) for i in range(layers - 1)] + [(2 * i + 3, 2 * i + 1) for i in range(layers - 1)]
    got = lax.ppermute(jnp.concatenate([mine, other[MINE:]], axis=0), ("space", "sub"), ways)

    strip_other = exchange(strip_send, "sub", 1)

    kop_shape = (EXT - 1, KROWS, 2 * C)
    work = 2 * 3 * C * 9 * C * EXT * PLANE
    x, acc = call(
        first_kernel,
        "first",
        [VMEM] * 5,
        [((2, EXT * PLANE, 9 * C), BF, FIXED), ((3 * C, 9 * C), F32, VMEM)],
        [pltpu.VMEM(kop_shape, BF)],
        flops=2 * work,
        size=8 * 2**20,
        limit=6,
    )(shift, gm, own, other, pad)
    size = 27 * C // (2 * layers)
    custom = layers == 8
    rows = (layers, size, C) if custom else (8, 216, C)
    exact = (rows, F32, VMEM)
    tilt_ins = (own, other, got, strip, strip_other, bands, acc)
    tilt_scratch = [pltpu.VMEM((2, EXT * 16, 2 * C), BF), pltpu.VMEM((3 * C, 3 * C), F32)]
    keep, send, zs, zs_send = call(
        tilt_kernel if custom else (lambda *refs: tilt_kernel(*refs, refs[8])),
        "tilt",
        [VMEM] * 7,
        [
            exact,
            ((layers, size + 8, C), jnp.int16, VMEM) if custom else exact,
            ((2, EXT * 16, 3 * C), BF, VMEM),
            ((2, EXT * 16, 3 * C), BF, VMEM),
        ],
        tilt_scratch + ([pltpu.VMEM(rows, F32)] if custom else []),
        flops=work // 4,
        size=4 * 2**20,
    )(*tilt_ins)

    send, x = tied(send, x)
    got = exchange(send, "sub", 1) if custom else None
    (ready,) = call(
        products_kernel,
        "products",
        [VMEM] * 2,
        [((6 * PLANE, 3 * C), F32, VMEM)],
        flops=work * 6 // EXT,
        size=4 * 2**20,
    )(weight, x)
    zs_got = exchange(zs_send, "sub", 1)

    def dgrad(*pieces):
        most = max(count for _, _, count, _ in pieces) + 2

        def run(before):
            fresh = before is None
            return call(
                (lambda *refs: dgrad_kernel(pieces, *refs[:6], None, *refs[6:]))
                if fresh
                else (lambda *refs: dgrad_kernel(pieces, *refs)),
                "dgrad",
                [VMEM] * 6 + ([] if fresh else [ANY]),
                [((2, VOX, C), BF, ANY)],
                [
                    pltpu.VMEM((most * PLANE, 3 * C), F32),
                    pltpu.VMEM((2, most * 16, 3 * C), F32),
                    pltpu.VMEM((PLANE + 16, C), F32),
                    pltpu.VMEM((2, VOX, C), BF),
                    pltpu.SemaphoreType.DMA((12,)),
                ],
                aliases={} if fresh else {6: 0},
                flops=work * sum(count for _, _, count, _ in pieces) // 12,
                size=4 * 2**20,
                limit=12,
            )(mask, weight, x, zs, zs_got, ready, *(() if fresh else (before,)))[0]

        return run

    if custom:
        got, zs, ready = tied(got, zs, ready)
        weight_grad, input_grad = reduce_blocks(keep, got, [dgrad((0, 0, 12, False), (1, 0, 4, True), (1, 4, 2, False)), dgrad((1, 6, 6, False))])
    else:
        first = lax.axis_index("sub") == 0
        even = jnp.where(first, keep, send)
        odd = jnp.where(first, send, keep)
        kernel_term = jnp.stack([even, odd], axis=1).reshape(27 * C, C)
        weight_grad = lax.psum_scatter(kernel_term, ("space", "sub"), scatter_dimension=0, tiled=True)
        input_grad = dgrad((0, 0, 12, False), (1, 0, 12, False))(None)
    return input_grad, weight_grad


def solution(mesh):
    in_specs = (
        P(("scene", "space", "sub"), None, None),
        P(("scene", "space", "sub"), None, None),
        P(),
        P(("scene", "space", "sub"), None),
        P(("scene", "space", "sub"), None),
    )
    out_specs = (P(("scene", "space", "sub"), None, None), P(("scene", "space", "sub"), None))
    return jax.shard_map(
        on_device, mesh=mesh, in_specs=in_specs, out_specs=out_specs, check_vma=False
    )
```

```python
import jax
import jax.numpy as jnp
import numpy as np
from jax import lax
from jax.experimental import pallas as pl
from jax.experimental.pallas import tpu as pltpu
from jax.sharding import PartitionSpec as P

BSIDE = 12
PLANE = BSIDE * BSIDE
VOX = BSIDE * PLANE
EXT = BSIDE + 2
C = 128
KROWS = 256
SPAN = 176
MINE = PLANE + 208
BF = jnp.bfloat16
F32 = jnp.float32


def strip_matrix():
    m = np.zeros((64, PLANE), np.float32)
    for i in range(BSIDE):
        m[i, i * BSIDE] = 1
        m[16 + i, i * BSIDE + 11] = 1
        m[32 + i, i] = 1
        m[52 + i, 11 * BSIDE + i] = 1
    m[12, 0] = m[28, 11] = 1
    m[13, 11 * BSIDE] = m[29, 11 * BSIDE + 11] = 1
    return m.astype(jnp.bfloat16)


def shift_matrix():
    m = np.zeros((2, SPAN, KROWS), np.float32)
    for n in range(2):
        for b in range(EXT):
            for c in range(BSIDE):
                source = c - (2 * n - 1)
                if 0 <= source < BSIDE:
                    m[n, 4 + b * BSIDE + c, 4 + b * BSIDE + source] = 1
    return m.reshape(2 * SPAN, KROWS).astype(jnp.bfloat16)


def band_matrix():
    m = np.zeros((3, EXT, 16, EXT, 16), np.float32)
    for q in range(3):
        for b in range(BSIDE):
            source = b - (q - 1)
            for p in range(EXT):
                m[q, p, b, p, 13 if source < 0 else source] = 1
    return m.reshape(3 * EXT * 16, EXT * 16).astype(jnp.bfloat16)


def dot(a, b):
    return lax.dot_general(a, b, (((1,), (0,)), ((), ())), preferred_element_type=F32)


def dot_t(a, b):
    return lax.dot_general(a, b, (((1,), (1,)), ((), ())), preferred_element_type=F32)


def halves(x):
    return jnp.concatenate([x[:, C:], x[:, :C]], axis=1)


def per_half(first, second, rows=16):
    lane = lax.broadcasted_iota(jnp.int32, (rows, 2 * C), 1)
    return jnp.where(lane < C, first, second)


def masks(act, out):
    r = lax.broadcasted_iota(jnp.int32, (C, C), 0)
    eye = jnp.where(r == lax.broadcasted_iota(jnp.int32, (C, C), 1), 1.0, 0.0)
    wide = lax.broadcasted_iota(jnp.int32, (2 * C, 2 * C), 0) < C
    ones = jnp.where(wide == (lax.broadcasted_iota(jnp.int32, (2 * C, 2 * C), 1) < C), 1.0, 0.0).astype(BF)
    for n in range(0, VOX, C):
        cols = []
        for j in range(2):
            a = act[pl.ds(j, 1), pl.ds(n, min(C, VOX - n))].astype(F32)
            if n + C > VOX:
                a = jnp.concatenate([a, jnp.zeros((1, n + C - VOX), F32)], axis=1)
            cols.append((eye * a).astype(BF))
        out[pl.ds(n, C), :] = dot(jnp.concatenate(cols, axis=1), ones).astype(BF)


def prep_kernel(nb_hbm, act_hbm, strips_hbm, g_hbm, gm, message, mine, mask, strips, nb, act, g, sem):
    loads = [
        pltpu.make_async_copy(act_hbm, act, sem.at[0]),
        pltpu.make_async_copy(strips_hbm, strips, sem.at[1]),
        pltpu.make_async_copy(nb_hbm, nb, sem.at[2]),
    ]
    for n in range(4):
        rows = pl.ds(n * VOX // 4, VOX // 4)
        loads.append(pltpu.make_async_copy(g_hbm.at[:, rows], g.at[:, rows], sem.at[3 + n]))
    for load in loads:
        load.start()
    loads[0].wait()
    masks(act, mask)
    loads[2].wait()
    a0 = per_half((nb[0, 0] >= 0).astype(F32), (nb[1, 0] >= 0).astype(F32))
    b0 = per_half((nb[0, 2] >= 0).astype(F32), (nb[1, 2] >= 0).astype(F32))
    code = (2 * a0 + b0).astype(BF)
    a0, b0 = a0.astype(BF), b0.astype(BF)
    second = jnp.full((16, 2 * C), lax.axis_index("sub").astype(F32), F32).astype(BF)
    row14 = jnp.where(lax.broadcasted_iota(jnp.int32, (16, 2 * C), 0) == 14, 1.0, 0.0).astype(BF)
    loads[1].wait()
    for p in range(BSIDE):
        if p % 3 == 0:
            loads[3 + p // 3].wait()
        rows = pl.ds(p * PLANE, PLANE)
        plane = jnp.concatenate([g[0, rows, :], g[1, rows, :]], axis=1) * mask[rows, :]
        gm[p] = plane
        s = dot(strips[...], plane).astype(BF)
        here, there = s[0:16] * second + s[16:32] * (1 - second), s[16:32] * second + s[0:16] * (1 - second)
        if p == 0:
            here, there = here + code * row14, there + code * row14
        mine[pl.ds(p * 16, 16), :] = here
        message[pl.ds(MINE + p * 16, 16), :] = there
        message[pl.ds(PLANE + p * 16, 16), :] = s[32:48] * b0 + s[48:64] * (1 - b0)
    for r in range(0, PLANE, 16):
        message[pl.ds(r, 16), :] = gm[0, pl.ds(r, 16), :] * a0 + gm[11, pl.ds(r, 16), :] * (1 - a0)
    message[pl.ds(PLANE + 192, 16), :] = code


def features_kernel(mask, strips, f_hbm, pad, strip, strip_send, f, sem):
    load = pltpu.make_async_copy(f_hbm, f, sem)
    load.start()
    zero = jnp.zeros((2 * PLANE, C), BF)
    edge = jnp.zeros((32, 2 * C), BF)
    second = jnp.full((16, 2 * C), lax.axis_index("sub").astype(F32), F32).astype(BF)
    for j in range(2):
        pad[j, pl.ds(0, 2 * PLANE), :] = zero
        pad[j, pl.ds(EXT * PLANE, 2 * PLANE), :] = zero
    for ref in (strip, strip_send):
        ref[pl.ds(0, 32), :] = edge
        ref[pl.ds(EXT * 16, 32), :] = edge
    load.wait()
    for j in range(2):
        pad[j, pl.ds(2 * PLANE, VOX), :] = f[j] * mask[pl.ds(0, VOX), pl.ds(j * C, C)]
    for p in range(BSIDE):
        rows = pl.ds((p + 2) * PLANE, PLANE)
        s = dot(strips[pl.ds(0, 32), :], jnp.concatenate([pad[0, rows, :], pad[1, rows, :]], axis=1)).astype(BF)
        strip[pl.ds((p + 2) * 16, 16), :] = s[0:16] * (1 - second) + s[16:32] * second
        strip_send[pl.ds((p + 2) * 16, 16), :] = s[0:16] * second + s[16:32] * (1 - second)


def position(own):
    code = own[pl.ds(336, 16), :].astype(F32)
    a0 = jnp.where(code >= 2, 1.0, 0.0)
    b0 = code - 2 * a0
    return code, a0, b0


def candidates(refs, at):
    tiles = []
    for ref, base, swapped in refs:
        t = ref[pl.ds(base + at // 16 * 16, 16), :].astype(F32)
        t = jnp.broadcast_to(t[at % 16 : at % 16 + 1], (16, 2 * C))
        tiles.append(((ref, base, swapped), halves(t) if swapped else t))
    return tiles


def hits(cands, q):
    return [(*source, jnp.where(t == q, 1.0, 0.0).astype(BF)) for source, t in cands]


def gather(picks, row):
    total = None
    for ref, base, swapped, w in picks:
        x = ref[pl.ds(base + row, 16), :]
        x = (halves(x) if swapped else x) * w
        total = x if total is None else total + x
    return total


def layer_operands(gm, own, other, kop):
    code, a0, b0 = position(own)
    layer = candidates([(own, 0, True), (other, 0, False), (other, 0, True)], 336)
    pick_a = hits(layer, code + 2 - 4 * a0)
    pick_b = hits(layer, code + 1 - 2 * b0)
    pick_d = hits(layer, 3 - code)
    a0h, b0h = a0.astype(BF), b0.astype(BF)
    a1h, b1h = 1 - a0h, 1 - b0h
    rest = jnp.zeros((KROWS - 176, 2 * C), BF)
    for p in range(BSIDE):
        kop[p + 1, pl.ds(16, PLANE), :] = gm[p]
        side = gather(pick_b, PLANE + p * 16)
        kop[p + 1, pl.ds(0, 16), :] = side * b0h
        kop[p + 1, pl.ds(160, 16), :] = side * b1h
        kop[p + 1, pl.ds(176, KROWS - 176), :] = rest
    for r in range(0, PLANE, 16):
        kop[0, pl.ds(16 + r, 16), :] = gather(pick_a, r)
    side = gather(pick_d, PLANE + 176) * a0h + gather(pick_d, PLANE) * a1h
    kop[0, pl.ds(0, 16), :] = side * b0h
    kop[0, pl.ds(160, 16), :] = side * b1h
    kop[0, pl.ds(176, KROWS - 176), :] = rest
    return a0h, a1h


def facing_plane(message, got, z):
    code, a0, b0 = position(message)
    row16 = lax.broadcasted_iota(jnp.int32, (16, 2 * C), 0)
    inner = jnp.where(row16 < 12, 1.0, 0.0).astype(BF)
    edge = jnp.where(row16 == 12, 1 - b0, jnp.where(row16 == 13, b0, 0.0)).astype(BF)
    a0h = a0.astype(BF)
    cands = candidates([(got, base, swapped) for base in (0, 192) for swapped in (False, True)], 14)
    near = [(*q, w * inner) for *q, w in hits(cands, code)]
    near += [(*q, w * edge) for *q, w in hits(cands, code + 1 - 2 * b0)]
    far = [(*q, w * inner) for *q, w in hits(cands, code + 2 - 4 * a0)]
    far += [(*q, w * edge) for *q, w in hits(cands, 3 - code)]
    for p in range(BSIDE):
        z[pl.ds((p + 1) * 16, 16), :] = gather(near, p * 16)
    z[pl.ds(0, 16), :] = gather(far, 11 * 16) * a0h
    z[pl.ds((EXT - 1) * 16, 16), :] = gather(far, 0) * (1 - a0h)


def shifted(shift, kop, sides, x, ends):
    for p in range(EXT - 1):
        for n in range(2):
            sides[p % 4, n] = dot(shift[pl.ds(n * SPAN, SPAN), :], kop[p]).astype(BF)
        for k in range(9):
            rows = pl.ds(16 - BSIDE * (k // 3 - 1), PLANE)
            y = kop[p, rows, :] if k % 3 == 1 else sides[p % 4, k % 3 // 2, rows, :]
            for at in (p,) if p else (0, EXT - 1):
                v = y if p else y * ends[1 if at else 0]
                for j in range(2):
                    x[j, pl.ds(at * PLANE, PLANE), pl.ds(k * C, C)] = v[:, j * C : j * C + C]


def stacked(ref, j):
    return jnp.concatenate([ref[j, pl.ds(d * PLANE, EXT * PLANE), :] for d in range(3)], axis=1)


def dot_rows(a, b):
    return lax.dot_general(a, b, (((0,), (0,)), ((), ())), preferred_element_type=F32)


def first_kernel(shift, gm, own, other, pad, x, acc, kop, sides):
    ends = [jnp.concatenate([w] * (PLANE // 16), axis=0) for w in layer_operands(gm, own, other, kop)]
    shifted(shift, kop, sides, x, ends)
    both = jnp.concatenate([stacked(pad, 0), stacked(pad, 1)], axis=0)
    acc[...] = dot_rows(both, x[...].reshape(both.shape[0], 9 * C))


def encode(ref, at, v):
    top = jnp.maximum(jnp.max(jnp.abs(v), axis=0, keepdims=True), 1e-33)
    e = jnp.floor(jnp.log2(top)) - 14
    q = jnp.clip(jnp.round(v * jnp.exp2(-e)), -32767, 32767)
    ref[at] = jnp.concatenate([q, jnp.broadcast_to(e, (8, C))], axis=0).astype(jnp.int32).astype(jnp.int16)


def decoded(ref, at):
    v = ref[at].astype(jnp.int32).astype(F32)
    rows = v.shape[0] - 8
    return v[:rows] * jnp.exp2(v[rows : rows + 1])


def tilt_kernel(own, other, got, strip, strip_other, bands, acc, keep, code, zs, zs_send, z, more, send):
    sub = lax.axis_index("sub")
    rows = EXT * 16
    for n, message in enumerate((own, other)):
        facing_plane(message, got, z.at[n])
    left, right = [], []
    for n, (features, out) in enumerate(((strip, zs), (strip_other, zs_send))):
        v = dot(bands[...], z[n]).astype(BF)
        for j in range(2):
            lanes = slice(j * C, j * C + C)
            right.append(jnp.concatenate([v[q * rows : q * rows + rows, lanes] for q in range(3)], axis=1))
            left.append(jnp.concatenate([features[pl.ds(d * 16, rows), lanes] for d in range(3)], axis=1))
            out[j] = right[-1]
    total = dot_rows(jnp.concatenate(left, axis=0), jnp.concatenate(right, axis=0))
    more[...] = total
    size = keep.shape[1]
    for parity in range(2):

        @pl.when(sub == parity)
        def _(parity=parity):
            for t in range(27):
                da, k = divmod(t, 9)
                row = t * C
                while row < (t + 1) * C:
                    block = row // size
                    end = min((block + 1) * size, (t + 1) * C)
                    at = pl.ds(da * C + row - t * C, end - row)
                    v = acc[at, pl.ds(k * C, C)]
                    if k % 3 == 2 - 2 * parity:
                        v = v + more[at, pl.ds(k // 3 * C, C)]
                    ref = keep if block % 2 == parity else send
                    ref[block // 2, pl.ds(row - block * size, end - row), :] = v * (1.0 / VOX)
                    row = end

    if code is send:
        return
    for n in range(keep.shape[0]):
        encode(code, n, send[n])


def columns(w, ks):
    return jnp.concatenate([jnp.concatenate([w[d * 9 + k] for k in ks], axis=1) for d in range(3)], axis=0)


def joined(y, p, rows):
    total = y[pl.ds((p + 2) * rows, rows), pl.ds(0, C)]
    total = total + y[pl.ds((p + 1) * rows, rows), pl.ds(C, C)]
    return total + y[pl.ds(p * rows, rows), pl.ds(2 * C, C)]


def products_kernel(w, x, out):
    out[...] = dot_t(x[1, pl.ds(0, out.shape[0]), :], columns(w, range(9)))


def dgrad_kernel(pieces, mask, w, x, zs, zs_got, ready, before, out, y, yz, plane, res, sem):
    del before
    core = lax.axis_index("sub")
    stores = []
    for j, first, count, done in pieces:
        source = ready if done else y
        if not done:
            rows = pl.ds(0, (count + 2) * PLANE)
            y[rows, :] = dot_t(x[j, pl.ds(first * PLANE, (count + 2) * PLANE), :], columns(w, range(9)))
        at = pl.ds(first * 16, (count + 2) * 16)
        for n in range(2):
            faces = jnp.where(core == n, zs[j, at, :], zs_got[j, at, :])
            yz[n, pl.ds(0, (count + 2) * 16), :] = dot_t(faces, columns(w, (2, 5, 8) if n == 0 else (0, 3, 6)))
        for p in range(count):
            plane[pl.ds(0, PLANE), :] = joined(source, p, PLANE)
            for n in range(2):
                at = pl.ds(11 * n, BSIDE, stride=BSIDE)
                plane[at, :] = plane[at, :] + joined(yz.at[n], p, 16)[:BSIDE]
            m = mask[pl.ds((first + p) * PLANE, PLANE), pl.ds(j * C, C)].astype(F32)
            at = pl.ds((first + p) * PLANE, PLANE)
            res[j, at, :] = (plane[pl.ds(0, PLANE), :] * m).astype(BF)
            if p % 2 == 1:
                at = pl.ds((first + p - 1) * PLANE, 2 * PLANE)
                stores.append(pltpu.make_async_copy(res.at[j, at], out.at[j, at], sem.at[len(stores)]))
                stores[-1].start()
    for store in stores:
        store.wait()


def place():
    s = lax.axis_index("space")
    return s % 2, s // 2 % 2, s // 4


def blocks_kernel(keep, got, send_y, send_z, send_yz, own):
    y, z, _ = place()
    for high in range(2):
        for ref, to_y, to_z in ((send_y, 1 - y, z), (send_z, y, 1 - z), (send_yz, 1 - y, 1 - z)):
            n = high * 4 + to_z * 2 + to_y
            encode(ref, high, keep[n] + decoded(got, n))
        n = high * 4 + z * 2 + y
        own[high] = keep[n] + decoded(got, n)


def last_kernel(own, got_y, got_z, got_yz, send, keep):
    high = place()[2]

    def total(n):
        return own[n] + decoded(got_y, n) + decoded(got_z, n) + decoded(got_yz, n)

    encode(send, Ellipsis, total(1 - high))
    keep[...] = total(high)


def sum_kernel(keep, got, out):
    out[...] = keep[...] + decoded(got, Ellipsis)


VMEM = pl.BlockSpec(memory_space=pltpu.MemorySpace.VMEM)
SMEM = pl.BlockSpec(memory_space=pltpu.MemorySpace.SMEM)
ANY = pl.BlockSpec(memory_space=pl.ANY)
HBM = pl.BlockSpec(memory_space=pltpu.MemorySpace.HBM)
FIXED = None


def call(kernel, name, ins, outs, scratch=(), aliases=None, flops=0, size=0, limit=6):
    return pl.pallas_call(
        kernel,
        name=name,
        out_shape=[pltpu.VMEM(s, d) if o is FIXED else jax.ShapeDtypeStruct(s, d) for s, d, o in outs],
        in_specs=ins,
        out_specs=[VMEM if o is FIXED else o for _, _, o in outs],
        scratch_shapes=list(scratch),
        input_output_aliases=aliases or {},
        compiler_params=pltpu.CompilerParams(vmem_limit_bytes=limit * 2**20),
        cost_estimate=pl.CostEstimate(flops=flops, transcendentals=0, bytes_accessed=size),
    )


def exchange(value, axis, bit):
    pairs = [(i, i ^ bit) for i in range(lax.axis_size(axis))]
    return lax.ppermute(value, axis, pairs)


def in_hbm(value):
    return pltpu.with_memory_space_constraint(value, pltpu.MemorySpace.HBM)


def tied(*values):
    return lax.optimization_barrier(values)


def reduce_blocks(keep, got, fillers):
    rows = keep.shape[1]
    code = (rows + 8, C)
    *sends, own = call(blocks_kernel, "blocks", [VMEM] * 2, [((2, *code), jnp.int16, VMEM)] * 3 + [((2, rows, C), F32, VMEM)])(keep, got)
    gots = [exchange(send, "space", bit) for bit, send in enumerate(sends, 1)]
    *gots, fill = tied(*gots, fillers[0](None))
    send, keep = call(last_kernel, "last", [VMEM] * 4, [(code, jnp.int16, VMEM), ((rows, C), F32, VMEM)])(own, *gots)
    got, fill = tied(exchange(send, "space", 4), fillers[1](fill))
    return call(sum_kernel, "sum", [VMEM] * 2, [((rows, C), F32, VMEM)])(keep, got)[0], fill


def on_device(features, out_grad, weight, neighbours, active):
    layers = lax.axis_size("space")
    strips, shift, bands = jnp.asarray(strip_matrix()), jnp.asarray(shift_matrix()), jnp.asarray(band_matrix())

    gm, own, mine, mask, strips = call(
        prep_kernel,
        "prep",
        [HBM] * 4,
        [
            ((BSIDE, PLANE, 2 * C), BF, VMEM),
            ((MINE + 192, 2 * C), BF, VMEM),
            ((192, 2 * C), BF, VMEM),
            ((14 * C, 2 * C), BF, VMEM),
            ((64, PLANE), BF, VMEM),
        ],
        [
            pltpu.SMEM((2, 6), jnp.int32),
            pltpu.VMEM((2, VOX), jnp.int32),
            pltpu.VMEM((2, VOX, C), BF),
            pltpu.SemaphoreType.DMA((7,)),
        ],
    )(in_hbm(neighbours), in_hbm(active), in_hbm(strips), in_hbm(out_grad))

    other = exchange(own, "sub", 1)
    pad, strip, strip_send = call(
        features_kernel,
        "features",
        [VMEM] * 2 + [HBM],
        [((2, (EXT + 2) * PLANE, C), BF, VMEM)] + [(((EXT + 2) * 16, 2 * C), BF, VMEM)] * 2,
        [pltpu.VMEM((2, VOX, C), BF), pltpu.SemaphoreType.DMA],
        flops=10**7,
        size=10**6,
    )(mask, strips, in_hbm(features))

    ways = [(2 * i, 2 * i + 2) for i in range(layers - 1)] + [(2 * i + 3, 2 * i + 1) for i in range(layers - 1)]
    got = lax.ppermute(jnp.concatenate([mine, other[MINE:]], axis=0), ("space", "sub"), ways)

    strip_other = exchange(strip_send, "sub", 1)

    kop_shape = (EXT - 1, KROWS, 2 * C)
    work = 2 * 3 * C * 9 * C * EXT * PLANE
    x, acc = call(
        first_kernel,
        "first",
        [VMEM] * 5,
        [((2, EXT * PLANE, 9 * C), BF, FIXED), ((3 * C, 9 * C), F32, VMEM)],
        [pltpu.VMEM(kop_shape, BF), pltpu.VMEM((4, 2, SPAN, 2 * C), BF)],
        flops=2 * work,
        size=8 * 2**20,
        limit=12,
    )(shift, gm, own, other, pad)
    size = 27 * C // (2 * layers)
    custom = layers == 8
    rows = (layers, size, C) if custom else (8, 216, C)
    exact = (rows, F32, VMEM)
    tilt_ins = (own, other, got, strip, strip_other, bands, acc)
    tilt_scratch = [pltpu.VMEM((2, EXT * 16, 2 * C), BF), pltpu.VMEM((3 * C, 3 * C), F32)]
    keep, send, zs, zs_send = call(
        tilt_kernel if custom else (lambda *refs: tilt_kernel(*refs, refs[8])),
        "tilt",
        [VMEM] * 7,
        [
            exact,
            ((layers, size + 8, C), jnp.int16, VMEM) if custom else exact,
            ((2, EXT * 16, 3 * C), BF, VMEM),
            ((2, EXT * 16, 3 * C), BF, VMEM),
        ],
        tilt_scratch + ([pltpu.VMEM(rows, F32)] if custom else []),
        flops=work // 4,
        size=4 * 2**20,
    )(*tilt_ins)

    send, x = tied(send, x)
    got = exchange(send, "sub", 1) if custom else None
    (ready,) = call(
        products_kernel,
        "products",
        [VMEM] * 2,
        [((6 * PLANE, 3 * C), F32, VMEM)],
        flops=work * 6 // EXT,
        size=4 * 2**20,
    )(weight, x)
    zs_got = exchange(zs_send, "sub", 1)

    def dgrad(*pieces):
        most = max(count for _, _, count, _ in pieces) + 2

        def run(before):
            fresh = before is None
            return call(
                (lambda *refs: dgrad_kernel(pieces, *refs[:6], None, *refs[6:]))
                if fresh
                else (lambda *refs: dgrad_kernel(pieces, *refs)),
                "dgrad",
                [VMEM] * 6 + ([] if fresh else [ANY]),
                [((2, VOX, C), BF, ANY)],
                [
                    pltpu.VMEM((most * PLANE, 3 * C), F32),
                    pltpu.VMEM((2, most * 16, 3 * C), F32),
                    pltpu.VMEM((PLANE + 16, C), F32),
                    pltpu.VMEM((2, VOX, C), BF),
                    pltpu.SemaphoreType.DMA((12,)),
                ],
                aliases={} if fresh else {6: 0},
                flops=work * sum(count for _, _, count, _ in pieces) // 12,
                size=4 * 2**20,
                limit=12,
            )(mask, weight, x, zs, zs_got, ready, *(() if fresh else (before,)))[0]

        return run

    if custom:
        got, zs, ready = tied(got, zs, ready)
        weight_grad, input_grad = reduce_blocks(keep, got, [dgrad((0, 0, 12, False), (1, 0, 4, True), (1, 4, 2, False)), dgrad((1, 6, 6, False))])
    else:
        first = lax.axis_index("sub") == 0
        even = jnp.where(first, keep, send)
        odd = jnp.where(first, send, keep)
        kernel_term = jnp.stack([even, odd], axis=1).reshape(27 * C, C)
        weight_grad = lax.psum_scatter(kernel_term, ("space", "sub"), scatter_dimension=0, tiled=True)
        input_grad = dgrad((0, 0, 12, False), (1, 0, 12, False))(None)
    return input_grad, weight_grad


def solution(mesh):
    in_specs = (
        P(("scene", "space", "sub"), None, None),
        P(("scene", "space", "sub"), None, None),
        P(),
        P(("scene", "space", "sub"), None),
        P(("scene", "space", "sub"), None),
    )
    out_specs = (P(("scene", "space", "sub"), None, None), P(("scene", "space", "sub"), None))
    return jax.shard_map(
        on_device, mesh=mesh, in_specs=in_specs, out_specs=out_specs, check_vma=False
    )
```

```python
import jax
import jax.numpy as jnp
import numpy as np
from jax import lax
from jax.experimental import pallas as pl
from jax.experimental.pallas import tpu as pltpu
from jax.sharding import PartitionSpec as P

BSIDE = 12
PLANE = BSIDE * BSIDE
VOX = BSIDE * PLANE
EXT = BSIDE + 2
C = 128
KROWS = 256
SPAN = 176
MINE = PLANE + 208
BF = jnp.bfloat16
F32 = jnp.float32


def strip_matrix():
    m = np.zeros((64, PLANE), np.float32)
    for i in range(BSIDE):
        m[i, i * BSIDE] = 1
        m[16 + i, i * BSIDE + 11] = 1
        m[32 + i, i] = 1
        m[52 + i, 11 * BSIDE + i] = 1
    m[12, 0] = m[28, 11] = 1
    m[13, 11 * BSIDE] = m[29, 11 * BSIDE + 11] = 1
    return m.astype(jnp.bfloat16)


def shift_matrix():
    m = np.zeros((2, SPAN, KROWS), np.float32)
    for n in range(2):
        for b in range(EXT):
            for c in range(BSIDE):
                source = c - (2 * n - 1)
                if 0 <= source < BSIDE:
                    m[n, 4 + b * BSIDE + c, 4 + b * BSIDE + source] = 1
    return m.reshape(2 * SPAN, KROWS).astype(jnp.bfloat16)


def band_matrix():
    m = np.zeros((3, EXT, 16, EXT, 16), np.float32)
    for q in range(3):
        for b in range(BSIDE):
            source = b - (q - 1)
            for p in range(EXT):
                m[q, p, b, p, 13 if source < 0 else source] = 1
    return m.reshape(3 * EXT * 16, EXT * 16).astype(jnp.bfloat16)


def dot(a, b):
    return lax.dot_general(a, b, (((1,), (0,)), ((), ())), preferred_element_type=F32)


def dot_t(a, b):
    return lax.dot_general(a, b, (((1,), (1,)), ((), ())), preferred_element_type=F32)


def halves(x):
    return jnp.concatenate([x[:, C:], x[:, :C]], axis=1)


def per_half(first, second, rows=16):
    lane = lax.broadcasted_iota(jnp.int32, (rows, 2 * C), 1)
    return jnp.where(lane < C, first, second)


def masks(act, out):
    r = lax.broadcasted_iota(jnp.int32, (C, C), 0)
    eye = jnp.where(r == lax.broadcasted_iota(jnp.int32, (C, C), 1), 1.0, 0.0)
    wide = lax.broadcasted_iota(jnp.int32, (2 * C, 2 * C), 0) < C
    ones = jnp.where(wide == (lax.broadcasted_iota(jnp.int32, (2 * C, 2 * C), 1) < C), 1.0, 0.0).astype(BF)
    for n in range(0, VOX, C):
        cols = []
        for j in range(2):
            a = act[pl.ds(j, 1), pl.ds(n, min(C, VOX - n))].astype(F32)
            if n + C > VOX:
                a = jnp.concatenate([a, jnp.zeros((1, n + C - VOX), F32)], axis=1)
            cols.append((eye * a).astype(BF))
        out[pl.ds(n, C), :] = dot(jnp.concatenate(cols, axis=1), ones).astype(BF)


def prep_kernel(nb_hbm, act_hbm, strips_hbm, g_hbm, gm, message, mine, mask, strips, nb, act, g, sem):
    loads = [
        pltpu.make_async_copy(act_hbm, act, sem.at[0]),
        pltpu.make_async_copy(strips_hbm, strips, sem.at[1]),
        pltpu.make_async_copy(nb_hbm, nb, sem.at[2]),
    ]
    for n in range(4):
        rows = pl.ds(n * VOX // 4, VOX // 4)
        loads.append(pltpu.make_async_copy(g_hbm.at[:, rows], g.at[:, rows], sem.at[3 + n]))
    for load in loads:
        load.start()
    loads[0].wait()
    masks(act, mask)
    loads[2].wait()
    a0 = per_half((nb[0, 0] >= 0).astype(F32), (nb[1, 0] >= 0).astype(F32))
    b0 = per_half((nb[0, 2] >= 0).astype(F32), (nb[1, 2] >= 0).astype(F32))
    code = (2 * a0 + b0).astype(BF)
    a0, b0 = a0.astype(BF), b0.astype(BF)
    second = jnp.full((16, 2 * C), lax.axis_index("sub").astype(F32), F32).astype(BF)
    row14 = jnp.where(lax.broadcasted_iota(jnp.int32, (16, 2 * C), 0) == 14, 1.0, 0.0).astype(BF)
    loads[1].wait()
    for p in range(BSIDE):
        if p % 3 == 0:
            loads[3 + p // 3].wait()
        rows = pl.ds(p * PLANE, PLANE)
        plane = jnp.concatenate([g[0, rows, :], g[1, rows, :]], axis=1) * mask[rows, :]
        gm[p] = plane
        s = dot(strips[...], plane).astype(BF)
        here, there = s[0:16] * second + s[16:32] * (1 - second), s[16:32] * second + s[0:16] * (1 - second)
        if p == 0:
            here, there = here + code * row14, there + code * row14
        mine[pl.ds(p * 16, 16), :] = here
        message[pl.ds(MINE + p * 16, 16), :] = there
        message[pl.ds(PLANE + p * 16, 16), :] = s[32:48] * b0 + s[48:64] * (1 - b0)
    for r in range(0, PLANE, 16):
        message[pl.ds(r, 16), :] = gm[0, pl.ds(r, 16), :] * a0 + gm[11, pl.ds(r, 16), :] * (1 - a0)
    message[pl.ds(PLANE + 192, 16), :] = code


def features_kernel(mask, strips, f_hbm, pad, strip, strip_send, f, sem):
    loads = [pltpu.make_async_copy(f_hbm.at[j], f.at[j], sem.at[j]) for j in range(2)]
    for load in loads:
        load.start()
    zero = jnp.zeros((2 * PLANE, C), BF)
    edge = jnp.zeros((32, 2 * C), BF)
    second = jnp.full((16, 2 * C), lax.axis_index("sub").astype(F32), F32).astype(BF)
    for j in range(2):
        pad[j, pl.ds(0, 2 * PLANE), :] = zero
        pad[j, pl.ds(EXT * PLANE, 2 * PLANE), :] = zero
    for ref in (strip, strip_send):
        ref[pl.ds(0, 32), :] = edge
        ref[pl.ds(EXT * 16, 32), :] = edge
    for j in range(2):
        loads[j].wait()
        pad[j, pl.ds(2 * PLANE, VOX), :] = f[j] * mask[pl.ds(0, VOX), pl.ds(j * C, C)]
    for p in range(BSIDE):
        rows = pl.ds((p + 2) * PLANE, PLANE)
        s = dot(strips[pl.ds(0, 32), :], jnp.concatenate([pad[0, rows, :], pad[1, rows, :]], axis=1)).astype(BF)
        strip[pl.ds((p + 2) * 16, 16), :] = s[0:16] * (1 - second) + s[16:32] * second
        strip_send[pl.ds((p + 2) * 16, 16), :] = s[0:16] * second + s[16:32] * (1 - second)


def position(own):
    code = own[pl.ds(336, 16), :].astype(F32)
    a0 = jnp.where(code >= 2, 1.0, 0.0)
    b0 = code - 2 * a0
    return code, a0, b0


def candidates(refs, at):
    tiles = []
    for ref, base, swapped in refs:
        t = ref[pl.ds(base + at // 16 * 16, 16), :].astype(F32)
        t = jnp.broadcast_to(t[at % 16 : at % 16 + 1], (16, 2 * C))
        tiles.append(((ref, base, swapped), halves(t) if swapped else t))
    return tiles


def hits(cands, q):
    return [(*source, jnp.where(t == q, 1.0, 0.0).astype(BF)) for source, t in cands]


def gather(picks, row):
    total = None
    for ref, base, swapped, w in picks:
        x = ref[pl.ds(base + row, 16), :]
        x = (halves(x) if swapped else x) * w
        total = x if total is None else total + x
    return total


def layer_operands(gm, own, other, kop):
    code, a0, b0 = position(own)
    layer = candidates([(own, 0, True), (other, 0, False), (other, 0, True)], 336)
    pick_a = hits(layer, code + 2 - 4 * a0)
    pick_b = hits(layer, code + 1 - 2 * b0)
    pick_d = hits(layer, 3 - code)
    a0h, b0h = a0.astype(BF), b0.astype(BF)
    a1h, b1h = 1 - a0h, 1 - b0h
    rest = jnp.zeros((KROWS - 176, 2 * C), BF)
    for p in range(BSIDE):
        kop[p + 1, pl.ds(16, PLANE), :] = gm[p]
        side = gather(pick_b, PLANE + p * 16)
        kop[p + 1, pl.ds(0, 16), :] = side * b0h
        kop[p + 1, pl.ds(160, 16), :] = side * b1h
        kop[p + 1, pl.ds(176, KROWS - 176), :] = rest
    for r in range(0, PLANE, 16):
        kop[0, pl.ds(16 + r, 16), :] = gather(pick_a, r)
    side = gather(pick_d, PLANE + 176) * a0h + gather(pick_d, PLANE) * a1h
    kop[0, pl.ds(0, 16), :] = side * b0h
    kop[0, pl.ds(160, 16), :] = side * b1h
    kop[0, pl.ds(176, KROWS - 176), :] = rest
    return a0h, a1h


def facing_plane(message, got, z):
    code, a0, b0 = position(message)
    row16 = lax.broadcasted_iota(jnp.int32, (16, 2 * C), 0)
    inner = jnp.where(row16 < 12, 1.0, 0.0).astype(BF)
    edge = jnp.where(row16 == 12, 1 - b0, jnp.where(row16 == 13, b0, 0.0)).astype(BF)
    a0h = a0.astype(BF)
    cands = candidates([(got, base, swapped) for base in (0, 192) for swapped in (False, True)], 14)
    near = [(*q, w * inner) for *q, w in hits(cands, code)]
    near += [(*q, w * edge) for *q, w in hits(cands, code + 1 - 2 * b0)]
    far = [(*q, w * inner) for *q, w in hits(cands, code + 2 - 4 * a0)]
    far += [(*q, w * edge) for *q, w in hits(cands, 3 - code)]
    for p in range(BSIDE):
        z[pl.ds((p + 1) * 16, 16), :] = gather(near, p * 16)
    z[pl.ds(0, 16), :] = gather(far, 11 * 16) * a0h
    z[pl.ds((EXT - 1) * 16, 16), :] = gather(far, 0) * (1 - a0h)


def shifted(shift, kop, sides, x, ends):
    for p in range(EXT - 1):
        for n in range(2):
            sides[p % 4, n] = dot(shift[pl.ds(n * SPAN, SPAN), :], kop[p]).astype(BF)
        for k in range(9):
            rows = pl.ds(16 - BSIDE * (k // 3 - 1), PLANE)
            y = kop[p, rows, :] if k % 3 == 1 else sides[p % 4, k % 3 // 2, rows, :]
            for at in (p,) if p else (0, EXT - 1):
                v = y if p else y * ends[1 if at else 0]
                for j in range(2):
                    x[j, pl.ds(at * PLANE, PLANE), pl.ds(k * C, C)] = v[:, j * C : j * C + C]


def stacked(ref, j):
    return jnp.concatenate([ref[j, pl.ds(d * PLANE, EXT * PLANE), :] for d in range(3)], axis=1)


def dot_rows(a, b):
    return lax.dot_general(a, b, (((0,), (0,)), ((), ())), preferred_element_type=F32)


def first_kernel(shift, gm, own, other, pad, x, acc, kop, sides):
    ends = [jnp.concatenate([w] * (PLANE // 16), axis=0) for w in layer_operands(gm, own, other, kop)]
    shifted(shift, kop, sides, x, ends)
    both = jnp.concatenate([stacked(pad, 0), stacked(pad, 1)], axis=0)
    acc[...] = dot_rows(both, x[...].reshape(both.shape[0], 9 * C))


def encode(ref, at, v):
    top = jnp.maximum(jnp.max(jnp.abs(v), axis=0, keepdims=True), 1e-33)
    e = jnp.floor(jnp.log2(top)) - 14
    q = jnp.clip(jnp.round(v * jnp.exp2(-e)), -32767, 32767)
    ref[at] = jnp.concatenate([q, jnp.broadcast_to(e, (8, C))], axis=0).astype(jnp.int32).astype(jnp.int16)


def decoded(ref, at):
    v = ref[at].astype(jnp.int32).astype(F32)
    rows = v.shape[0] - 8
    return v[:rows] * jnp.exp2(v[rows : rows + 1])


def tilt_kernel(own, other, got, strip, strip_other, bands, acc, keep, code, zs, zs_send, z, more, send):
    sub = lax.axis_index("sub")
    rows = EXT * 16
    for n, message in enumerate((own, other)):
        facing_plane(message, got, z.at[n])
    left, right = [], []
    for n, (features, out) in enumerate(((strip, zs), (strip_other, zs_send))):
        v = dot(bands[...], z[n]).astype(BF)
        for j in range(2):
            lanes = slice(j * C, j * C + C)
            right.append(jnp.concatenate([v[q * rows : q * rows + rows, lanes] for q in range(3)], axis=1))
            left.append(jnp.concatenate([features[pl.ds(d * 16, rows), lanes] for d in range(3)], axis=1))
            out[j] = right[-1]
    total = dot_rows(jnp.concatenate(left, axis=0), jnp.concatenate(right, axis=0))
    more[...] = total
    size = keep.shape[1]
    for parity in range(2):

        @pl.when(sub == parity)
        def _(parity=parity):
            for t in range(27):
                da, k = divmod(t, 9)
                row = t * C
                while row < (t + 1) * C:
                    block = row // size
                    end = min((block + 1) * size, (t + 1) * C)
                    at = pl.ds(da * C + row - t * C, end - row)
                    v = acc[at, pl.ds(k * C, C)]
                    if k % 3 == 2 - 2 * parity:
                        v = v + more[at, pl.ds(k // 3 * C, C)]
                    ref = keep if block % 2 == parity else send
                    ref[block // 2, pl.ds(row - block * size, end - row), :] = v
                    row = end

    if code is send:
        return
    for n in range(keep.shape[0]):
        encode(code, n, send[n])


def columns(w, ks):
    return jnp.concatenate([jnp.concatenate([w[d * 9 + k] for k in ks], axis=1) for d in range(3)], axis=0)


def joined(y, p, rows):
    total = y[pl.ds((p + 2) * rows, rows), pl.ds(0, C)]
    total = total + y[pl.ds((p + 1) * rows, rows), pl.ds(C, C)]
    return total + y[pl.ds(p * rows, rows), pl.ds(2 * C, C)]


def products_kernel(w, x, out):
    out[...] = dot_t(x[1, pl.ds(0, out.shape[0]), :], columns(w, range(9)))


def dgrad_kernel(pieces, mask, w, x, zs, zs_got, ready, before, out, y, yz, plane, res, sem):
    del before
    core = lax.axis_index("sub")
    stores = []
    for j, first, count, done in pieces:
        source = ready if done else y
        if not done:
            rows = pl.ds(0, (count + 2) * PLANE)
            y[rows, :] = dot_t(x[j, pl.ds(first * PLANE, (count + 2) * PLANE), :], columns(w, range(9)))
        at = pl.ds(first * 16, (count + 2) * 16)
        for n in range(2):
            faces = jnp.where(core == n, zs[j, at, :], zs_got[j, at, :])
            yz[n, pl.ds(0, (count + 2) * 16), :] = dot_t(faces, columns(w, (2, 5, 8) if n == 0 else (0, 3, 6)))
        for p in range(count):
            plane[pl.ds(0, PLANE), :] = joined(source, p, PLANE)
            for n in range(2):
                at = pl.ds(11 * n, BSIDE, stride=BSIDE)
                plane[at, :] = plane[at, :] + joined(yz.at[n], p, 16)[:BSIDE]
            m = mask[pl.ds((first + p) * PLANE, PLANE), pl.ds(j * C, C)].astype(F32)
            at = pl.ds((first + p) * PLANE, PLANE)
            res[j, at, :] = (plane[pl.ds(0, PLANE), :] * m).astype(BF)
            if p % 2 == 1:
                at = pl.ds((first + p - 1) * PLANE, 2 * PLANE)
                stores.append(pltpu.make_async_copy(res.at[j, at], out.at[j, at], sem.at[len(stores)]))
                stores[-1].start()
    for store in stores:
        store.wait()


def place():
    s = lax.axis_index("space")
    return s % 2, s // 2 % 2, s // 4


def blocks_kernel(keep, got, send_y, send_z, send_yz, own):
    y, z, _ = place()
    for high in range(2):
        for ref, to_y, to_z in ((send_y, 1 - y, z), (send_z, y, 1 - z), (send_yz, 1 - y, 1 - z)):
            n = high * 4 + to_z * 2 + to_y
            encode(ref, high, keep[n] + decoded(got, n))
        n = high * 4 + z * 2 + y
        own[high] = keep[n] + decoded(got, n)


def last_kernel(own, got_y, got_z, got_yz, send, keep):
    high = place()[2]

    def total(n):
        return own[n] + decoded(got_y, n) + decoded(got_z, n) + decoded(got_yz, n)

    encode(send, Ellipsis, total(1 - high))
    keep[...] = total(high)


def sum_kernel(keep, got, out):
    out[...] = (keep[...] + decoded(got, Ellipsis)) * (1.0 / VOX)


VMEM = pl.BlockSpec(memory_space=pltpu.MemorySpace.VMEM)
SMEM = pl.BlockSpec(memory_space=pltpu.MemorySpace.SMEM)
ANY = pl.BlockSpec(memory_space=pl.ANY)
HBM = pl.BlockSpec(memory_space=pltpu.MemorySpace.HBM)
FIXED = None


def call(kernel, name, ins, outs, scratch=(), aliases=None, flops=0, size=0, limit=6):
    return pl.pallas_call(
        kernel,
        name=name,
        out_shape=[pltpu.VMEM(s, d) if o is FIXED else jax.ShapeDtypeStruct(s, d) for s, d, o in outs],
        in_specs=ins,
        out_specs=[VMEM if o is FIXED else o for _, _, o in outs],
        scratch_shapes=list(scratch),
        input_output_aliases=aliases or {},
        compiler_params=pltpu.CompilerParams(vmem_limit_bytes=limit * 2**20),
        cost_estimate=pl.CostEstimate(flops=flops, transcendentals=0, bytes_accessed=size),
    )


def exchange(value, axis, bit):
    pairs = [(i, i ^ bit) for i in range(lax.axis_size(axis))]
    return lax.ppermute(value, axis, pairs)


def in_hbm(value):
    return pltpu.with_memory_space_constraint(value, pltpu.MemorySpace.HBM)


def tied(*values):
    return lax.optimization_barrier(values)


def reduce_blocks(keep, got, fillers):
    rows = keep.shape[1]
    code = (rows + 8, C)
    *sends, own = call(blocks_kernel, "blocks", [VMEM] * 2, [((2, *code), jnp.int16, VMEM)] * 3 + [((2, rows, C), F32, VMEM)])(keep, got)
    gots = [exchange(send, "space", bit) for bit, send in enumerate(sends, 1)]
    *gots, fill = tied(*gots, fillers[0](None))
    send, keep = call(last_kernel, "last", [VMEM] * 4, [(code, jnp.int16, VMEM), ((rows, C), F32, VMEM)])(own, *gots)
    got, fill = tied(exchange(send, "space", 4), fillers[1](fill))
    return call(sum_kernel, "sum", [VMEM] * 2, [((rows, C), F32, VMEM)])(keep, got)[0], fill


def on_device(features, out_grad, weight, neighbours, active):
    layers = lax.axis_size("space")
    strips, shift, bands = jnp.asarray(strip_matrix()), jnp.asarray(shift_matrix()), jnp.asarray(band_matrix())

    gm, own, mine, mask, strips = call(
        prep_kernel,
        "prep",
        [HBM] * 4,
        [
            ((BSIDE, PLANE, 2 * C), BF, VMEM),
            ((MINE + 192, 2 * C), BF, VMEM),
            ((192, 2 * C), BF, VMEM),
            ((14 * C, 2 * C), BF, VMEM),
            ((64, PLANE), BF, VMEM),
        ],
        [
            pltpu.SMEM((2, 6), jnp.int32),
            pltpu.VMEM((2, VOX), jnp.int32),
            pltpu.VMEM((2, VOX, C), BF),
            pltpu.SemaphoreType.DMA((7,)),
        ],
    )(in_hbm(neighbours), in_hbm(active), in_hbm(strips), in_hbm(out_grad))

    other = exchange(own, "sub", 1)
    pad, strip, strip_send = call(
        features_kernel,
        "features",
        [VMEM] * 2 + [HBM],
        [((2, (EXT + 2) * PLANE, C), BF, VMEM)] + [(((EXT + 2) * 16, 2 * C), BF, VMEM)] * 2,
        [pltpu.VMEM((2, VOX, C), BF), pltpu.SemaphoreType.DMA((2,))],
        flops=10**7,
        size=10**6,
    )(mask, strips, in_hbm(features))

    ways = [(2 * i, 2 * i + 2) for i in range(layers - 1)] + [(2 * i + 3, 2 * i + 1) for i in range(layers - 1)]
    got = lax.ppermute(jnp.concatenate([mine, other[MINE:]], axis=0), ("space", "sub"), ways)

    strip_other = exchange(strip_send, "sub", 1)

    kop_shape = (EXT - 1, KROWS, 2 * C)
    work = 2 * 3 * C * 9 * C * EXT * PLANE
    x, acc = call(
        first_kernel,
        "first",
        [VMEM] * 5,
        [((2, EXT * PLANE, 9 * C), BF, FIXED), ((3 * C, 9 * C), F32, VMEM)],
        [pltpu.VMEM(kop_shape, BF), pltpu.VMEM((4, 2, SPAN, 2 * C), BF)],
        flops=2 * work,
        size=8 * 2**20,
        limit=12,
    )(shift, gm, own, other, pad)
    size = 27 * C // (2 * layers)
    custom = layers == 8
    rows = (layers, size, C) if custom else (8, 216, C)
    exact = (rows, F32, VMEM)
    tilt_ins = (own, other, got, strip, strip_other, bands, acc)
    tilt_scratch = [pltpu.VMEM((2, EXT * 16, 2 * C), BF), pltpu.VMEM((3 * C, 3 * C), F32)]
    keep, send, zs, zs_send = call(
        tilt_kernel if custom else (lambda *refs: tilt_kernel(*refs, refs[8])),
        "tilt",
        [VMEM] * 7,
        [
            exact,
            ((layers, size + 8, C), jnp.int16, VMEM) if custom else exact,
            ((2, EXT * 16, 3 * C), BF, VMEM),
            ((2, EXT * 16, 3 * C), BF, VMEM),
        ],
        tilt_scratch + ([pltpu.VMEM(rows, F32)] if custom else []),
        flops=work // 4,
        size=4 * 2**20,
    )(*tilt_ins)

    send, x = tied(send, x)
    got = exchange(send, "sub", 1) if custom else None
    (ready,) = call(
        products_kernel,
        "products",
        [VMEM] * 2,
        [((6 * PLANE, 3 * C), F32, VMEM)],
        flops=work * 6 // EXT,
        size=4 * 2**20,
    )(weight, x)
    zs_got = exchange(zs_send, "sub", 1)

    def dgrad(*pieces):
        most = max(count for _, _, count, _ in pieces) + 2

        def run(before):
            fresh = before is None
            return call(
                (lambda *refs: dgrad_kernel(pieces, *refs[:6], None, *refs[6:]))
                if fresh
                else (lambda *refs: dgrad_kernel(pieces, *refs)),
                "dgrad",
                [VMEM] * 6 + ([] if fresh else [ANY]),
                [((2, VOX, C), BF, ANY)],
                [
                    pltpu.VMEM((most * PLANE, 3 * C), F32),
                    pltpu.VMEM((2, most * 16, 3 * C), F32),
                    pltpu.VMEM((PLANE + 16, C), F32),
                    pltpu.VMEM((2, VOX, C), BF),
                    pltpu.SemaphoreType.DMA((12,)),
                ],
                aliases={} if fresh else {6: 0},
                flops=work * sum(count for _, _, count, _ in pieces) // 12,
                size=4 * 2**20,
                limit=12,
            )(mask, weight, x, zs, zs_got, ready, *(() if fresh else (before,)))[0]

        return run

    if custom:
        got, zs, ready = tied(got, zs, ready)
        weight_grad, input_grad = reduce_blocks(keep, got, [dgrad((0, 0, 12, False), (1, 0, 4, True), (1, 4, 2, False)), dgrad((1, 6, 6, False))])
    else:
        first = lax.axis_index("sub") == 0
        even = jnp.where(first, keep, send)
        odd = jnp.where(first, send, keep)
        kernel_term = jnp.stack([even, odd], axis=1).reshape(27 * C, C)
        kernel_term = kernel_term * (1.0 / VOX)
        weight_grad = lax.psum_scatter(kernel_term, ("space", "sub"), scatter_dimension=0, tiled=True)
        input_grad = dgrad((0, 0, 12, False), (1, 0, 12, False))(None)
    return input_grad, weight_grad


def solution(mesh):
    in_specs = (
        P(("scene", "space", "sub"), None, None),
        P(("scene", "space", "sub"), None, None),
        P(),
        P(("scene", "space", "sub"), None),
        P(("scene", "space", "sub"), None),
    )
    out_specs = (P(("scene", "space", "sub"), None, None), P(("scene", "space", "sub"), None))
    return jax.shard_map(
        on_device, mesh=mesh, in_specs=in_specs, out_specs=out_specs, check_vma=False
    )
```

```python
import jax
import jax.numpy as jnp
import numpy as np
from jax import lax
from jax.experimental import pallas as pl
from jax.experimental.pallas import tpu as pltpu
from jax.sharding import PartitionSpec as P

BSIDE = 12
PLANE = BSIDE * BSIDE
VOX = BSIDE * PLANE
EXT = BSIDE + 2
C = 128
KROWS = 256
SPAN = 176
MINE = PLANE + 208
BF = jnp.bfloat16
F32 = jnp.float32


def strip_matrix():
    m = np.zeros((64, PLANE), np.float32)
    for i in range(BSIDE):
        m[i, i * BSIDE] = 1
        m[16 + i, i * BSIDE + 11] = 1
        m[32 + i, i] = 1
        m[52 + i, 11 * BSIDE + i] = 1
    m[12, 0] = m[28, 11] = 1
    m[13, 11 * BSIDE] = m[29, 11 * BSIDE + 11] = 1
    return m.astype(jnp.bfloat16)


def shift_matrix():
    m = np.zeros((2, SPAN, KROWS), np.float32)
    for n in range(2):
        for b in range(EXT):
            for c in range(BSIDE):
                source = c - (2 * n - 1)
                if 0 <= source < BSIDE:
                    m[n, 4 + b * BSIDE + c, 4 + b * BSIDE + source] = 1
    return m.reshape(2 * SPAN, KROWS).astype(jnp.bfloat16)


def band_matrix():
    m = np.zeros((3, EXT, 16, EXT, 16), np.float32)
    for q in range(3):
        for b in range(BSIDE):
            source = b - (q - 1)
            for p in range(EXT):
                m[q, p, b, p, 13 if source < 0 else source] = 1
    return m.reshape(3 * EXT * 16, EXT * 16).astype(jnp.bfloat16)


def dot(a, b):
    return lax.dot_general(a, b, (((1,), (0,)), ((), ())), preferred_element_type=F32)


def dot_t(a, b):
    return lax.dot_general(a, b, (((1,), (1,)), ((), ())), preferred_element_type=F32)


def halves(x):
    return jnp.concatenate([x[:, C:], x[:, :C]], axis=1)


def per_half(first, second, rows=16):
    lane = lax.broadcasted_iota(jnp.int32, (rows, 2 * C), 1)
    return jnp.where(lane < C, first, second)


def masks(act, out):
    r = lax.broadcasted_iota(jnp.int32, (C, C), 0)
    eye = jnp.where(r == lax.broadcasted_iota(jnp.int32, (C, C), 1), 1.0, 0.0)
    wide = lax.broadcasted_iota(jnp.int32, (2 * C, 2 * C), 0) < C
    ones = jnp.where(wide == (lax.broadcasted_iota(jnp.int32, (2 * C, 2 * C), 1) < C), 1.0, 0.0).astype(BF)
    for n in range(0, VOX, C):
        cols = []
        for j in range(2):
            a = act[pl.ds(j, 1), pl.ds(n, min(C, VOX - n))].astype(F32)
            if n + C > VOX:
                a = jnp.concatenate([a, jnp.zeros((1, n + C - VOX), F32)], axis=1)
            cols.append((eye * a).astype(BF))
        out[pl.ds(n, C), :] = dot(jnp.concatenate(cols, axis=1), ones).astype(BF)


def prep_kernel(nb_hbm, act_hbm, strips_hbm, g_hbm, gm, message, mine, mask, strips, nb, act, g, sem):
    loads = [
        pltpu.make_async_copy(act_hbm, act, sem.at[0]),
        pltpu.make_async_copy(strips_hbm, strips, sem.at[1]),
        pltpu.make_async_copy(nb_hbm, nb, sem.at[2]),
    ]
    for n in range(4):
        rows = pl.ds(n * VOX // 4, VOX // 4)
        loads.append(pltpu.make_async_copy(g_hbm.at[:, rows], g.at[:, rows], sem.at[3 + n]))
    for load in loads:
        load.start()
    loads[0].wait()
    masks(act, mask)
    loads[2].wait()
    a0 = per_half((nb[0, 0] >= 0).astype(F32), (nb[1, 0] >= 0).astype(F32))
    b0 = per_half((nb[0, 2] >= 0).astype(F32), (nb[1, 2] >= 0).astype(F32))
    code = (2 * a0 + b0).astype(BF)
    a0, b0 = a0.astype(BF), b0.astype(BF)
    second = jnp.full((16, 2 * C), lax.axis_index("sub").astype(F32), F32).astype(BF)
    row14 = jnp.where(lax.broadcasted_iota(jnp.int32, (16, 2 * C), 0) == 14, 1.0, 0.0).astype(BF)
    loads[1].wait()
    for p in range(BSIDE):
        if p % 3 == 0:
            loads[3 + p // 3].wait()
        rows = pl.ds(p * PLANE, PLANE)
        plane = jnp.concatenate([g[0, rows, :], g[1, rows, :]], axis=1) * mask[rows, :]
        gm[p] = plane
        s = dot(strips[...], plane).astype(BF)
        here, there = s[0:16] * second + s[16:32] * (1 - second), s[16:32] * second + s[0:16] * (1 - second)
        if p == 0:
            here, there = here + code * row14, there + code * row14
        mine[pl.ds(p * 16, 16), :] = here
        message[pl.ds(MINE + p * 16, 16), :] = there
        message[pl.ds(PLANE + p * 16, 16), :] = s[32:48] * b0 + s[48:64] * (1 - b0)
    for r in range(0, PLANE, 16):
        message[pl.ds(r, 16), :] = gm[0, pl.ds(r, 16), :] * a0 + gm[11, pl.ds(r, 16), :] * (1 - a0)
    message[pl.ds(PLANE + 192, 16), :] = code


def features_kernel(mask, strips, f_hbm, pad, strip, strip_send, f, sem):
    loads = [pltpu.make_async_copy(f_hbm.at[j], f.at[j], sem.at[j]) for j in range(2)]
    for load in loads:
        load.start()
    zero = jnp.zeros((2 * PLANE, C), BF)
    edge = jnp.zeros((32, 2 * C), BF)
    second = jnp.full((16, 2 * C), lax.axis_index("sub").astype(F32), F32).astype(BF)
    for j in range(2):
        pad[j, pl.ds(0, 2 * PLANE), :] = zero
        pad[j, pl.ds(EXT * PLANE, 2 * PLANE), :] = zero
    for ref in (strip, strip_send):
        ref[pl.ds(0, 32), :] = edge
        ref[pl.ds(EXT * 16, 32), :] = edge
    for j in range(2):
        loads[j].wait()
        pad[j, pl.ds(2 * PLANE, VOX), :] = f[j] * mask[pl.ds(0, VOX), pl.ds(j * C, C)]
    for p in range(BSIDE):
        rows = pl.ds((p + 2) * PLANE, PLANE)
        s = dot(strips[pl.ds(0, 32), :], jnp.concatenate([pad[0, rows, :], pad[1, rows, :]], axis=1)).astype(BF)
        strip[pl.ds((p + 2) * 16, 16), :] = s[0:16] * (1 - second) + s[16:32] * second
        strip_send[pl.ds((p + 2) * 16, 16), :] = s[0:16] * second + s[16:32] * (1 - second)


def position(own):
    code = own[pl.ds(336, 16), :].astype(F32)
    a0 = jnp.where(code >= 2, 1.0, 0.0)
    b0 = code - 2 * a0
    return code, a0, b0


def candidates(refs, at):
    tiles = []
    for ref, base, swapped in refs:
        t = ref[pl.ds(base + at // 16 * 16, 16), :].astype(F32)
        t = jnp.broadcast_to(t[at % 16 : at % 16 + 1], (16, 2 * C))
        tiles.append(((ref, base, swapped), halves(t) if swapped else t))
    return tiles


def hits(cands, q):
    return [(*source, jnp.where(t == q, 1.0, 0.0).astype(BF)) for source, t in cands]


def gather(picks, row):
    total = None
    for ref, base, swapped, w in picks:
        x = ref[pl.ds(base + row, 16), :]
        x = (halves(x) if swapped else x) * w
        total = x if total is None else total + x
    return total


def layer_operands(gm, own, other, kop):
    code, a0, b0 = position(own)
    layer = candidates([(own, 0, True), (other, 0, False), (other, 0, True)], 336)
    pick_a = hits(layer, code + 2 - 4 * a0)
    pick_b = hits(layer, code + 1 - 2 * b0)
    pick_d = hits(layer, 3 - code)
    a0h, b0h = a0.astype(BF), b0.astype(BF)
    a1h, b1h = 1 - a0h, 1 - b0h
    rest = jnp.zeros((KROWS - 176, 2 * C), BF)
    for p in range(BSIDE):
        kop[p + 1, pl.ds(16, PLANE), :] = gm[p]
        side = gather(pick_b, PLANE + p * 16)
        kop[p + 1, pl.ds(0, 16), :] = side * b0h
        kop[p + 1, pl.ds(160, 16), :] = side * b1h
        kop[p + 1, pl.ds(176, KROWS - 176), :] = rest
    for r in range(0, PLANE, 16):
        kop[0, pl.ds(16 + r, 16), :] = gather(pick_a, r)
    side = gather(pick_d, PLANE + 176) * a0h + gather(pick_d, PLANE) * a1h
    kop[0, pl.ds(0, 16), :] = side * b0h
    kop[0, pl.ds(160, 16), :] = side * b1h
    kop[0, pl.ds(176, KROWS - 176), :] = rest
    return a0h, a1h


def facing_plane(message, got, z):
    code, a0, b0 = position(message)
    row16 = lax.broadcasted_iota(jnp.int32, (16, 2 * C), 0)
    inner = jnp.where(row16 < 12, 1.0, 0.0).astype(BF)
    edge = jnp.where(row16 == 12, 1 - b0, jnp.where(row16 == 13, b0, 0.0)).astype(BF)
    a0h = a0.astype(BF)
    cands = candidates([(got, base, swapped) for base in (0, 192) for swapped in (False, True)], 14)
    near = [(*q, w * inner) for *q, w in hits(cands, code)]
    near += [(*q, w * edge) for *q, w in hits(cands, code + 1 - 2 * b0)]
    far = [(*q, w * inner) for *q, w in hits(cands, code + 2 - 4 * a0)]
    far += [(*q, w * edge) for *q, w in hits(cands, 3 - code)]
    for p in range(BSIDE):
        z[pl.ds((p + 1) * 16, 16), :] = gather(near, p * 16)
    z[pl.ds(0, 16), :] = gather(far, 11 * 16) * a0h
    z[pl.ds((EXT - 1) * 16, 16), :] = gather(far, 0) * (1 - a0h)


def shifted(shift, kop, sides, x, ends):
    for p in range(EXT - 1):
        for n in range(2):
            sides[p % 4, n] = dot(shift[pl.ds(n * SPAN, SPAN), :], kop[p]).astype(BF)
        for k in range(9):
            rows = pl.ds(16 - BSIDE * (k // 3 - 1), PLANE)
            y = kop[p, rows, :] if k % 3 == 1 else sides[p % 4, k % 3 // 2, rows, :]
            for at in (p,) if p else (0, EXT - 1):
                v = y if p else y * ends[1 if at else 0]
                for j in range(2):
                    x[j, pl.ds(at * PLANE, PLANE), pl.ds(k * C, C)] = v[:, j * C : j * C + C]


def stacked(ref, j):
    return jnp.concatenate([ref[j, pl.ds(d * PLANE, EXT * PLANE), :] for d in range(3)], axis=1)


def dot_rows(a, b):
    return lax.dot_general(a, b, (((0,), (0,)), ((), ())), preferred_element_type=F32)


def first_kernel(shift, gm, own, other, pad, x, acc, kop, sides):
    ends = [jnp.concatenate([w] * (PLANE // 16), axis=0) for w in layer_operands(gm, own, other, kop)]
    shifted(shift, kop, sides, x, ends)
    both = jnp.concatenate([stacked(pad, 0), stacked(pad, 1)], axis=0)
    acc[...] = dot_rows(both, x[...].reshape(both.shape[0], 9 * C))


def encode(ref, at, v):
    top = jnp.maximum(jnp.max(jnp.abs(v), axis=0, keepdims=True), 1e-33)
    e = jnp.floor(jnp.log2(top)) - 14
    q = jnp.clip(jnp.round(v * jnp.exp2(-e)), -32767, 32767)
    ref[at] = jnp.concatenate([q, jnp.broadcast_to(e, (8, C))], axis=0).astype(jnp.int32).astype(jnp.int16)


def decoded(ref, at):
    v = ref[at].astype(jnp.int32).astype(F32)
    rows = v.shape[0] - 8
    return v[:rows] * jnp.exp2(v[rows : rows + 1])


def tilt_kernel(own, other, got, strip, strip_other, bands, acc, keep, code, zs, zs_send, z, more, send):
    sub = lax.axis_index("sub")
    rows = EXT * 16
    for n, message in enumerate((own, other)):
        facing_plane(message, got, z.at[n])
    left, right = [], []
    for n, (features, out) in enumerate(((strip, zs), (strip_other, zs_send))):
        v = dot(bands[...], z[n]).astype(BF)
        for j in range(2):
            lanes = slice(j * C, j * C + C)
            right.append(jnp.concatenate([v[q * rows : q * rows + rows, lanes] for q in range(3)], axis=1))
            left.append(jnp.concatenate([features[pl.ds(d * 16, rows), lanes] for d in range(3)], axis=1))
            out[j] = right[-1]
    total = dot_rows(jnp.concatenate(left, axis=0), jnp.concatenate(right, axis=0))
    more[...] = total
    size = keep.shape[1]
    for parity in range(2):

        @pl.when(sub == parity)
        def _(parity=parity):
            for t in range(27):
                da, k = divmod(t, 9)
                row = t * C
                while row < (t + 1) * C:
                    block = row // size
                    end = min((block + 1) * size, (t + 1) * C)
                    at = pl.ds(da * C + row - t * C, end - row)
                    v = acc[at, pl.ds(k * C, C)]
                    if k % 3 == 2 - 2 * parity:
                        v = v + more[at, pl.ds(k // 3 * C, C)]
                    ref = keep if block % 2 == parity else send
                    ref[block // 2, pl.ds(row - block * size, end - row), :] = v
                    row = end

    if code is send:
        return
    for n in range(keep.shape[0]):
        encode(code, n, send[n])


def columns(w, ks):
    return jnp.concatenate([jnp.concatenate([w[d * 9 + k] for k in ks], axis=1) for d in range(3)], axis=0)


def joined(y, p, rows):
    total = y[pl.ds((p + 2) * rows, rows), pl.ds(0, C)]
    total = total + y[pl.ds((p + 1) * rows, rows), pl.ds(C, C)]
    return total + y[pl.ds(p * rows, rows), pl.ds(2 * C, C)]


def products_kernel(w, x, out):
    out[...] = dot_t(x[1, pl.ds(0, out.shape[0]), :], columns(w, range(9)))


def dgrad_kernel(pieces, mask, w, x, zs, zs_got, ready, before, out, y, yz, plane, res, sem):
    del before
    core = lax.axis_index("sub")
    stores = []
    for j, first, count, done in pieces:
        source = ready if done else y
        if not done:
            rows = pl.ds(0, (count + 2) * PLANE)
            y[rows, :] = dot_t(x[j, pl.ds(first * PLANE, (count + 2) * PLANE), :], columns(w, range(9)))
        at = pl.ds(first * 16, (count + 2) * 16)
        for n in range(2):
            faces = jnp.where(core == n, zs[j, at, :], zs_got[j, at, :])
            yz[n, pl.ds(0, (count + 2) * 16), :] = dot_t(faces, columns(w, (2, 5, 8) if n == 0 else (0, 3, 6)))
        for p in range(count):
            plane[pl.ds(0, PLANE), :] = joined(source, p, PLANE)
            for n in range(2):
                at = pl.ds(11 * n, BSIDE, stride=BSIDE)
                plane[at, :] = plane[at, :] + joined(yz.at[n], p, 16)[:BSIDE]
            m = mask[pl.ds((first + p) * PLANE, PLANE), pl.ds(j * C, C)].astype(F32)
            at = pl.ds((first + p) * PLANE, PLANE)
            res[j, at, :] = (plane[pl.ds(0, PLANE), :] * m).astype(BF)
            if p % 2 == 1:
                at = pl.ds((first + p - 1) * PLANE, 2 * PLANE)
                stores.append(pltpu.make_async_copy(res.at[j, at], out.at[j, at], sem.at[len(stores)]))
                stores[-1].start()
    for store in stores:
        store.wait()


def place():
    s = lax.axis_index("space")
    return s % 2, s // 2 % 2, s // 4


def blocks_kernel(keep, got, send_y, send_z, send_yz, own):
    y, z, _ = place()
    for high in range(2):
        for ref, to_y, to_z in ((send_y, 1 - y, z), (send_z, y, 1 - z), (send_yz, 1 - y, 1 - z)):
            n = high * 4 + to_z * 2 + to_y
            encode(ref, high, keep[n] + decoded(got, n))
        n = high * 4 + z * 2 + y
        own[high] = keep[n] + decoded(got, n)


def last_kernel(own, got_y, got_z, got_yz, send, keep):
    high = place()[2]

    def total(n):
        return own[n] + decoded(got_y, n) + decoded(got_z, n) + decoded(got_yz, n)

    encode(send, Ellipsis, total(1 - high))
    keep[...] = total(high)


def sum_kernel(keep, got, out):
    out[...] = (keep[...] + decoded(got, Ellipsis)) * (1.0 / VOX)


VMEM = pl.BlockSpec(memory_space=pltpu.MemorySpace.VMEM)
SMEM = pl.BlockSpec(memory_space=pltpu.MemorySpace.SMEM)
ANY = pl.BlockSpec(memory_space=pl.ANY)
HBM = pl.BlockSpec(memory_space=pltpu.MemorySpace.HBM)
FIXED = None


def call(kernel, name, ins, outs, scratch=(), aliases=None, flops=0, size=0, limit=6):
    return pl.pallas_call(
        kernel,
        name=name,
        out_shape=[pltpu.VMEM(s, d) if o is FIXED else jax.ShapeDtypeStruct(s, d) for s, d, o in outs],
        in_specs=ins,
        out_specs=[VMEM if o is FIXED else o for _, _, o in outs],
        scratch_shapes=list(scratch),
        input_output_aliases=aliases or {},
        compiler_params=pltpu.CompilerParams(vmem_limit_bytes=limit * 2**20),
        cost_estimate=pl.CostEstimate(flops=flops, transcendentals=0, bytes_accessed=size),
    )


def exchange(value, axis, bit):
    pairs = [(i, i ^ bit) for i in range(lax.axis_size(axis))]
    return lax.ppermute(value, axis, pairs)


def in_hbm(value):
    return pltpu.with_memory_space_constraint(value, pltpu.MemorySpace.HBM)


def tied(*values):
    return lax.optimization_barrier(values)


def reduce_blocks(keep, got, fillers):
    rows = keep.shape[1]
    code = (rows + 8, C)
    *sends, own = call(blocks_kernel, "blocks", [VMEM] * 2, [((2, *code), jnp.int16, VMEM)] * 3 + [((2, rows, C), F32, VMEM)])(keep, got)
    gots = [exchange(send, "space", bit) for bit, send in enumerate(sends, 1)]
    *gots, fill = tied(*gots, fillers[0](None))
    send, keep = call(last_kernel, "last", [VMEM] * 4, [(code, jnp.int16, VMEM), ((rows, C), F32, VMEM)])(own, *gots)
    got, fill = tied(exchange(send, "space", 4), fillers[1](fill))
    return call(sum_kernel, "sum", [VMEM] * 2, [((rows, C), F32, VMEM)])(keep, got)[0], fill


def on_device(features, out_grad, weight, neighbours, active):
    layers = lax.axis_size("space")
    strips, shift, bands = jnp.asarray(strip_matrix()), jnp.asarray(shift_matrix()), jnp.asarray(band_matrix())

    gm, own, mine, mask, strips = call(
        prep_kernel,
        "prep",
        [HBM] * 4,
        [
            ((BSIDE, PLANE, 2 * C), BF, VMEM),
            ((MINE + 192, 2 * C), BF, VMEM),
            ((192, 2 * C), BF, VMEM),
            ((14 * C, 2 * C), BF, VMEM),
            ((64, PLANE), BF, VMEM),
        ],
        [
            pltpu.SMEM((2, 6), jnp.int32),
            pltpu.VMEM((2, VOX), jnp.int32),
            pltpu.VMEM((2, VOX, C), BF),
            pltpu.SemaphoreType.DMA((7,)),
        ],
    )(in_hbm(neighbours), in_hbm(active), in_hbm(strips), in_hbm(out_grad))

    other = exchange(own, "sub", 1)
    pad, strip, strip_send = call(
        features_kernel,
        "features",
        [VMEM] * 2 + [HBM],
        [((2, (EXT + 2) * PLANE, C), BF, VMEM)] + [(((EXT + 2) * 16, 2 * C), BF, VMEM)] * 2,
        [pltpu.VMEM((2, VOX, C), BF), pltpu.SemaphoreType.DMA((2,))],
        flops=10**7,
        size=10**6,
    )(mask, strips, in_hbm(features))

    ways = [(2 * i, 2 * i + 2) for i in range(layers - 1)] + [(2 * i + 3, 2 * i + 1) for i in range(layers - 1)]
    got = lax.ppermute(jnp.concatenate([mine, other[MINE:]], axis=0), ("space", "sub"), ways)

    strip_other = exchange(strip_send, "sub", 1)

    kop_shape = (EXT - 1, KROWS, 2 * C)
    work = 2 * 3 * C * 9 * C * EXT * PLANE
    x, acc = call(
        first_kernel,
        "first",
        [VMEM] * 5,
        [((2, EXT * PLANE, 9 * C), BF, FIXED), ((3 * C, 9 * C), F32, VMEM)],
        [pltpu.VMEM(kop_shape, BF), pltpu.VMEM((4, 2, SPAN, 2 * C), BF)],
        flops=2 * work,
        size=8 * 2**20,
        limit=12,
    )(shift, gm, own, other, pad)
    size = 27 * C // (2 * layers)
    custom = layers == 8
    rows = (layers, size, C) if custom else (8, 216, C)
    exact = (rows, F32, VMEM)
    tilt_ins = (own, other, got, strip, strip_other, bands, acc)
    tilt_scratch = [pltpu.VMEM((2, EXT * 16, 2 * C), BF), pltpu.VMEM((3 * C, 3 * C), F32)]
    keep, send, zs, zs_send = call(
        tilt_kernel if custom else (lambda *refs: tilt_kernel(*refs, refs[8])),
        "tilt",
        [VMEM] * 7,
        [
            exact,
            ((layers, size + 8, C), jnp.int16, VMEM) if custom else exact,
            ((2, EXT * 16, 3 * C), BF, VMEM),
            ((2, EXT * 16, 3 * C), BF, VMEM),
        ],
        tilt_scratch + ([pltpu.VMEM(rows, F32)] if custom else []),
        flops=work // 4,
        size=4 * 2**20,
    )(*tilt_ins)

    send, x = tied(send, x)
    got = exchange(send, "sub", 1) if custom else None
    (ready,) = call(
        products_kernel,
        "products",
        [VMEM] * 2,
        [((6 * PLANE, 3 * C), F32, VMEM)],
        flops=work * 6 // EXT,
        size=4 * 2**20,
    )(weight, x)
    zs_got = exchange(zs_send, "sub", 1)

    def dgrad(*pieces):
        most = max(count for _, _, count, _ in pieces) + 2

        def run(before):
            fresh = before is None
            return call(
                (lambda *refs: dgrad_kernel(pieces, *refs[:6], None, *refs[6:]))
                if fresh
                else (lambda *refs: dgrad_kernel(pieces, *refs)),
                "dgrad",
                [VMEM] * 6 + ([] if fresh else [ANY]),
                [((2, VOX, C), BF, ANY)],
                [
                    pltpu.VMEM((most * PLANE, 3 * C), F32),
                    pltpu.VMEM((2, most * 16, 3 * C), F32),
                    pltpu.VMEM((PLANE + 16, C), F32),
                    pltpu.VMEM((2, VOX, C), BF),
                    pltpu.SemaphoreType.DMA((12,)),
                ],
                aliases={} if fresh else {6: 0},
                flops=work * sum(count for _, _, count, _ in pieces) // 12,
                size=4 * 2**20,
                limit=12,
            )(mask, weight, x, zs, zs_got, ready, *(() if fresh else (before,)))[0]

        return run

    if custom:
        got, zs, ready = tied(got, zs, ready)
        weight_grad, input_grad = reduce_blocks(keep, got, [dgrad((0, 0, 12, False), (1, 0, 4, True), (1, 4, 4, False)), dgrad((1, 8, 4, False))])
    else:
        first = lax.axis_index("sub") == 0
        even = jnp.where(first, keep, send)
        odd = jnp.where(first, send, keep)
        kernel_term = jnp.stack([even, odd], axis=1).reshape(27 * C, C)
        kernel_term = kernel_term * (1.0 / VOX)
        weight_grad = lax.psum_scatter(kernel_term, ("space", "sub"), scatter_dimension=0, tiled=True)
        input_grad = dgrad((0, 0, 12, False), (1, 0, 12, False))(None)
    return input_grad, weight_grad


def solution(mesh):
    in_specs = (
        P(("scene", "space", "sub"), None, None),
        P(("scene", "space", "sub"), None, None),
        P(),
        P(("scene", "space", "sub"), None),
        P(("scene", "space", "sub"), None),
    )
    out_specs = (P(("scene", "space", "sub"), None, None), P(("scene", "space", "sub"), None))
    return jax.shard_map(
        on_device, mesh=mesh, in_specs=in_specs, out_specs=out_specs, check_vma=False
    )
```
